32 devices in a mesh: groups: 2 (over y), tok: 4 (over z), lay: 2 (over x), head: 2 (over core).
Axes of the slice: x: 2, y: 2, z: 4, core: 2. Of those that a mesh axis runs over, the one named last changes fastest.
Arguments:
- keys: float32 [2, 4096, 1024], P('lay', ('groups', 'tok'), 'head'), parts along dimension 1, may hold values from -80 to 80, as said below
- values: float32 [2, 4096, 1024], P('lay', ('groups', 'tok'), 'head'), parts along dimension 1, may hold values from -24 to 24
- queries: float32 [2, 32, 8192], P('lay', 'groups', 'head'), parts along dimension 1, may hold values from -620 to 620, as said below
- start_block: float32 [4096, 256], P(('groups', 'tok')), parts along dimension 0, may hold values from -6 to 6
- lengths: int32 [32], P('groups'), parts along dimension 0, may hold values from 1 to 2048, as said below
Outputs:
- attended: float32 [2, 32, 2, 4096], P('lay', 'groups', 'head', 'tok'), parts along dimension 1
The draws below stay inside these ranges and needn't reach their ends.
There are 2 independent parts, one for each index of `groups`. The reference program is written for one: setup_inputs(seed, part) draws one part's arguments, and reference() takes and returns one part's arrays. A program takes and returns all parts, laid end to end along the dimension named above; each array names one. Nothing has to cross between parts.
Inputs may be any that keep to these rules, and one draw needn't show every extreme that they name: keys lie within this range. queries lie within this range. `lengths`: the longest row covers all 2048 tokens.
All inputs are finite; a program needn't handle non-finite values.
Results may differ from the reference program's by a relative error of at most 0.0003.
Values sent between devices are 32-bit elements; how exact they have to be, the bound alone decides.
No kernel may reach another device: no remote copies, remote signals or barrier semaphores. Data moves between devices by JAX's collectives and lax.ppermute only.
A program may use at most 64 MiB of HBM per device.

```python
import math
import jax
import jax.numpy as jnp
from jax import lax

KVH = 8
HD = 128
QH = 64
KVW = 1024
QW = 8192
RANK = 256
ROWS = 16
ITERS = 2
LAYERS = 2
TOKENS = 2048
N_HEAD = 2


def draw_keys(key, part):
    noise = jnp.clip(jax.random.normal(jax.random.fold_in(key, 11), (LAYERS, TOKENS, KVW), jnp.float32), -6.0, 6.0)
    column = jnp.exp(jax.random.uniform(jax.random.fold_in(key, 12), (1, 1, KVW), jnp.float32, math.log(0.5), math.log(2.0)))
    token = jnp.exp(jax.random.uniform(jax.random.fold_in(key, 13), (1, TOKENS, 1), jnp.float32, math.log(0.5), math.log(2.0)))
    return noise * column * token


def draw_queries(key, part):
    return jnp.clip(jax.random.normal(jax.random.fold_in(key, 31), (LAYERS, ROWS, QW), jnp.float32), -6.0, 6.0) * 6.0


def draw_lengths(key, part):
    drawn = jax.random.randint(jax.random.fold_in(key, 21), (ROWS,), 1, TOKENS + 1)
    picked = jax.random.randint(jax.random.fold_in(key, 22), (), 0, ROWS)
    return jnp.where(jnp.arange(ROWS) == picked, TOKENS, drawn).astype(jnp.int32)


def block_levels(rng, shape, split, least, largest):
    loudness = 1.0
    for axis_at, blocks in split:
        draws = jax.random.uniform(jax.random.fold_in(jax.random.fold_in(rng, 6), axis_at), (blocks,), jnp.float32, least / len(split), largest / len(split))
        loudness = loudness * jnp.repeat(jnp.exp(draws), shape[axis_at] // blocks).reshape((-1,) + (1,) * (len(shape) - 1 - axis_at))
    return loudness


def scatter_about(key, extent, spread, limit, pieces=(), kind=jnp.bfloat16):
    values = jax.random.normal(key, extent, jnp.float32) * spread
    if len(pieces) > 0:
        values = block_levels(key, extent, pieces, -0.22, 0.18) * values
    return jnp.clip(values, min=-limit, max=limit).astype(kind)


def setup_inputs(seed: int = 0, part: int = 0) -> dict:
    key_of = jax.random.split(jax.random.key(seed), 6)
    part_keys = jax.random.split(jax.random.fold_in(key_of[5], part), 6)
    return {
        "keys": draw_keys(jax.random.fold_in(jax.random.fold_in(key_of[5], part), 71), part),
        "values": scatter_about(part_keys[1], (LAYERS, TOKENS, KVW), 4.0, 24.0, ((0, 2), (1, 4), (2, 2)), jnp.float32),
        "queries": draw_queries(jax.random.fold_in(jax.random.fold_in(key_of[5], part), 71), part),
        "start_block": scatter_about(part_keys[3], (TOKENS, RANK), 1.0, 6.0, ((0, 4),), jnp.float32),
        "lengths": draw_lengths(jax.random.fold_in(jax.random.fold_in(key_of[5], part), 71), part),
    }


NEG = -1e+30

def orthonormal(block):
    highest = lax.Precision.HIGHEST
    gram = jnp.dot(block.T.astype(jnp.float32), block.astype(jnp.float32), precision=highest, preferred_element_type=jnp.float32)
    lower = jnp.linalg.cholesky(gram)
    return lax.linalg.triangular_solve(lower, block, left_side=False, lower=True, transpose_a=True)

def reference(keys, values, queries, start_block, lengths):
    highest = lax.Precision.HIGHEST
    basis = orthonormal(start_block)
    for step in range(ITERS):
        coef = jnp.einsum('lsc,sr->lcr', keys, basis, precision=highest)
        block = jnp.einsum('lsc,lcr->sr', keys, coef, precision=highest)
        basis = orthonormal(block)
    coef = jnp.einsum('lsc,sr->lcr', keys, basis, precision=highest)
    group = QH // KVH
    quer = queries.reshape(LAYERS, ROWS, KVH, group, HD)
    factor = coef.reshape(LAYERS, KVH, HD, RANK)
    reduced = jnp.einsum('lbgid,lgdr->lgibr', quer, factor, precision=highest) / math.sqrt(HD)
    scores = jnp.einsum('sr,lgibr->lgibs', basis, reduced, precision=highest)
    position = jnp.arange(TOKENS, dtype=jnp.int32)
    valid = position[None, :] < lengths[:, None]
    masked = jnp.where(valid, scores, NEG)
    peak = lax.optimization_barrier(jnp.max(masked, axis=-1, keepdims=True))
    weight = jnp.where(valid, jnp.exp(scores - peak), 0.0)
    total = lax.optimization_barrier(jnp.sum(weight, axis=-1))
    vals = values.reshape(LAYERS, TOKENS, KVH, HD)
    summed = jnp.einsum('lgibs,lsgd->lgibd', weight, vals, precision=highest)
    result = summed / total[..., None]
    result = result.reshape(LAYERS, QH, ROWS, HD).transpose(0, 2, 1, 3)
    return result.reshape(LAYERS, ROWS, N_HEAD, QH // N_HEAD * HD)
```

```python
import functools
import math

import jax
import jax.numpy as jnp
from jax import lax
from jax.experimental import pallas as pl
from jax.experimental.pallas import tpu as pltpu
from jax.sharding import PartitionSpec as P

KVH = 8
HD = 128
QH = 64
ITERS = 2

NEG = -1e30
HIGHEST = lax.Precision.HIGHEST


def product(left, right, dims):
    return lax.dot_general(
        left, right, (dims, ((), ())), precision=HIGHEST, preferred_element_type=jnp.float32
    )


def diagonal_inverse(tile, size, step):
    width = 2 * size
    rows = lax.broadcasted_iota(jnp.int32, (size, width), 0)
    cols = lax.broadcasted_iota(jnp.int32, (size, width), 1)
    state = jnp.concatenate([tile, jnp.zeros_like(tile)], axis=1)
    state = state + jnp.where(cols == rows + size, 1.0, 0.0)
    scale = jnp.zeros((size, width), jnp.float32)
    for start in range(0, size, step):
        col = [
            jnp.broadcast_to(state[:, start + i : start + i + 1], (size, width))
            for i in range(step)
        ]
        row = [state[start + i : start + i + 1, :] for i in range(step)]
        inverse = []
        for i in range(step):
            pivot = col[i][start + i : start + i + 1, :]
            inverse.append(1.0 / pivot)
            scale = jnp.where(rows == start + i, lax.rsqrt(pivot), scale)
            for k in range(i + 1, step):
                ratio = col[i][start + k : start + k + 1, :] * inverse[i]
                row[k] = row[k] - ratio * row[i]
                col[k] = col[k] - ratio * col[i]
        for i in range(step):
            below = jnp.where(rows > start + i, col[i], 0.0)
            state = state - below * (row[i] * inverse[i])
    return (state * scale)[:, size:]


def factor_kernel(size, step, gram_ref, out_ref, work_ref):
    rank = gram_ref.shape[0]
    work_ref[...] = gram_ref[...]
    out_ref[...] = jnp.zeros((rank, rank), jnp.float32)
    for at in range(0, rank, size):
        here, rest = pl.ds(at, size), pl.ds(at + size, rank - at - size)
        tile = diagonal_inverse(work_ref[here, here], size, step)
        if at > 0:
            before = pl.ds(0, at)
            out_ref[here, before] = product(tile, out_ref[here, before], ((1,), (0,)))
        out_ref[here, here] = tile
        if at + size < rank:
            panel = product(tile, work_ref[here, rest], ((1,), (0,)))
            work_ref[rest, rest] = work_ref[rest, rest] - product(panel, panel, ((0,), (0,)))
            done = pl.ds(0, at + size)
            out_ref[rest, done] = out_ref[rest, done] - product(
                panel, out_ref[here, done], ((0,), (0,))
            )


def inverse_factor(gram):
    rank = gram.shape[0]
    return pl.pallas_call(
        functools.partial(factor_kernel, 128, 8),
        out_shape=jax.ShapeDtypeStruct((rank, rank), jnp.float32),
        in_specs=[pl.BlockSpec(memory_space=pltpu.VMEM)],
        out_specs=pl.BlockSpec(memory_space=pltpu.VMEM),
        scratch_shapes=[pltpu.VMEM((rank, rank), jnp.float32)],
        cost_estimate=pl.CostEstimate(flops=400_000_000, bytes_accessed=600_000, transcendentals=0),
    )(gram)


def distances(axis):
    size = lax.axis_size(axis)
    return [1 << i for i in range(size.bit_length() - 1)]


def side(axis, distance):
    return lax.axis_index(axis) // distance % 2


def swap(x, axis, distance):
    pairs = [(i, i ^ distance) for i in range(lax.axis_size(axis))]
    return lax.ppermute(x, axis, pairs)


def halve(x, axis, distance):
    half = x.shape[0] // 2
    mine = side(axis, distance)
    keep = lax.dynamic_slice_in_dim(x, mine * half, half, 0)
    send = lax.dynamic_slice_in_dim(x, (1 - mine) * half, half, 0)
    return keep + swap(send, axis, distance)


def double(x, axis, distance):
    other = swap(x, axis, distance)
    first = side(axis, distance) == 0
    return jnp.concatenate([jnp.where(first, x, other), jnp.where(first, other, x)])


def summed_rows(x, hops):
    for hop in hops:
        x = halve(x, *hop)
    for hop in reversed(hops):
        x = double(x, *hop)
    return x


def body(keys, values, queries, start_block, lengths):
    _, tok_dev, kv_dev = keys.shape
    keys, values = keys[0], values[0]
    rank = start_block.shape[1]
    rows = queries.shape[1]
    local_heads = queries.shape[2] // HD
    group = QH // KVH
    kv_local = kv_dev // HD
    tok_hops = [("tok", d) for d in distances("tok")]
    wide_hops = [("head", d) for d in distances("head")] + [("lay", d) for d in distances("lay")]

    def whole_gram(block):
        share = rank
        at = 0
        for axis, distance in reversed(wide_hops):
            share //= 2
            at = at + side(axis, distance) * share
        part = lax.dynamic_slice_in_dim(block, at, share, 1)
        gram = product(part, block, ((0,), (0,)))
        for hop in tok_hops:
            gram = gram + swap(gram, *hop)
        for hop in wide_hops:
            gram = double(gram, *hop)
        return gram

    def project(block):
        return summed_rows(product(keys, block, ((0,), (0,))), tok_hops)

    def mix(coef):
        return summed_rows(product(keys, coef, ((1,), (0,))), wide_hops)

    block = start_block
    for step in range(ITERS):
        lower = inverse_factor(whole_gram(block))
        block = product(mix(project(block)), lower, ((1,), (1,)))
    lower = inverse_factor(whole_gram(block))
    coef = product(project(block), lower, ((1,), (1,)))
    basis = product(block, lower, ((1,), (1,)))

    quer = queries.reshape(rows, kv_local, group, HD)
    factor = coef.reshape(kv_local, HD, rank)
    reduced = jnp.einsum("bgid,gdr->gibr", quer, factor, precision=HIGHEST) / math.sqrt(HD)
    reduced = reduced.reshape(kv_local, group * rows, rank)
    scores = jnp.einsum("tr,gxr->tgx", basis, reduced, precision=HIGHEST)
    position = lax.axis_index("tok") * tok_dev + jnp.arange(tok_dev, dtype=jnp.int32)
    valid = position[:, None] < lengths[None, :]
    valid = jnp.tile(valid, (1, group))[:, None, :]
    peak = jnp.max(jnp.where(valid, scores, NEG), axis=0)
    weight = jnp.where(valid, jnp.exp(scores - peak[None]), 0.0)
    total = jnp.sum(weight, axis=0)
    vals = values.reshape(tok_dev, kv_local, HD)
    summed = jnp.einsum("tgx,tgd->gxd", weight, vals, precision=HIGHEST)
    peak = peak.reshape(local_heads, rows)
    total = total.reshape(local_heads, rows)
    summed = summed.reshape(local_heads, rows, HD)

    share = local_heads // lax.axis_size("tok")
    peak, total, summed = jax.tree.map(
        lambda a: a.reshape((-1, share) + a.shape[1:]), (peak, total, summed)
    )

    def pack(part):
        top, tot, acc = part
        blank = jnp.zeros(top.shape[:-1] + (HD - 2 * rows,), jnp.float32)
        extra = jnp.concatenate([top, tot, blank], axis=-1).reshape(-1, HD)
        return jnp.concatenate([acc.reshape(-1, HD), extra])

    def unpack(buffer, like):
        count = like[0].shape[0] * share
        extra = buffer[count * rows :]
        return (
            extra[:, :rows].reshape(like[0].shape),
            extra[:, rows : 2 * rows].reshape(like[0].shape),
            buffer[: count * rows].reshape(like[2].shape),
        )

    state = (peak, total, summed)
    for hop in tok_hops:
        mine = side(*hop)
        pairs = jax.tree.map(lambda a: a.reshape((-1, 2) + a.shape[1:]), state)
        keep = jax.tree.map(lambda a: lax.dynamic_index_in_dim(a, mine, 1, False), pairs)
        send = jax.tree.map(lambda a: lax.dynamic_index_in_dim(a, 1 - mine, 1, False), pairs)
        got = unpack(swap(pack(send), *hop), keep)
        top = jnp.maximum(keep[0], got[0])
        one, two = jnp.exp(keep[0] - top), jnp.exp(got[0] - top)
        state = (
            top,
            keep[1] * one + got[1] * two,
            keep[2] * one[..., None] + got[2] * two[..., None],
        )
    result = state[2][0] / state[1][0][..., None]
    return result.transpose(1, 0, 2).reshape(1, rows, 1, share * HD)


def solution(mesh):
    return jax.shard_map(
        body,
        mesh=mesh,
        in_specs=(
            P("lay", ("groups", "tok"), "head"),
            P("lay", ("groups", "tok"), "head"),
            P("lay", "groups", "head"),
            P(("groups", "tok"), None),
            P("groups"),
        ),
        out_specs=P("lay", "groups", "head", "tok"),
        check_vma=False,
    )
```

```python
import functools
import math

import jax
import jax.numpy as jnp
from jax import lax
from jax.experimental import pallas as pl
from jax.experimental.pallas import tpu as pltpu
from jax.sharding import PartitionSpec as P

KVH = 8
HD = 128
QH = 64
ITERS = 2

NEG = -1e30
HIGHEST = lax.Precision.HIGHEST


def product(left, right, dims):
    return lax.dot_general(
        left, right, (dims, ((), ())), precision=HIGHEST, preferred_element_type=jnp.float32
    )


def diagonal_inverse(tile, size, step):
    width = 2 * size
    rows = lax.broadcasted_iota(jnp.int32, (size, width), 0)
    cols = lax.broadcasted_iota(jnp.int32, (size, width), 1)
    state = jnp.concatenate([tile, jnp.zeros_like(tile)], axis=1)
    state = state + jnp.where(cols == rows + size, 1.0, 0.0)
    scale = jnp.zeros((size, width), jnp.float32)
    for start in range(0, size, step):
        col = [
            jnp.broadcast_to(state[:, start + i : start + i + 1], (size, width))
            for i in range(step)
        ]
        row = [state[start + i : start + i + 1, :] for i in range(step)]
        inverse = []
        for i in range(step):
            pivot = col[i][start + i : start + i + 1, :]
            inverse.append(1.0 / pivot)
            scale = jnp.where(rows == start + i, lax.rsqrt(pivot), scale)
            for k in range(i + 1, step):
                ratio = col[i][start + k : start + k + 1, :] * inverse[i]
                row[k] = row[k] - ratio * row[i]
                col[k] = col[k] - ratio * col[i]
        for i in range(step):
            below = jnp.where(rows > start + i, col[i], 0.0)
            state = state - below * (row[i] * inverse[i])
    return (state * scale)[:, size:]


def vmem(*shape):
    return jax.ShapeDtypeStruct(shape, jnp.float32)


def call(kernel, out_shape, *args, scratch=(), flops=0):
    spec = pl.BlockSpec(memory_space=pltpu.VMEM)
    single = not isinstance(out_shape, (tuple, list))
    moved = sum(4 * math.prod(a.shape) for a in (*args, *((out_shape,) if single else out_shape)))
    return pl.pallas_call(
        kernel,
        out_shape=out_shape,
        in_specs=[spec] * len(args),
        out_specs=spec if single else [spec] * len(out_shape),
        scratch_shapes=[pltpu.VMEM(s, jnp.float32) for s in scratch],
        compiler_params=pltpu.CompilerParams(vmem_limit_bytes=40 << 20),
        cost_estimate=pl.CostEstimate(flops=flops, bytes_accessed=moved, transcendentals=0),
    )(*args)


def factor_first_kernel(own_ref, *refs):
    *part_refs, tile_ref, panel_ref, left_ref, gram_ref = refs
    part_refs = (own_ref, *part_refs)
    if len(part_refs) == 1:
        gram_ref[...] = own_ref[...]
    else:
        lay, head = lax.axis_index("lay"), lax.axis_index("head")
        rows = own_ref.shape[0]
        for i, ref in enumerate(part_refs):
            at = (2 * (head ^ (i // 2)) + (lay ^ (i % 2))) * rows
            gram_ref[pl.ds(pl.multiple_of(at, rows), rows), :] = ref[...]
    half = tile_ref.shape[0]
    low, high = pl.ds(0, half), pl.ds(half, half)
    tile = diagonal_inverse(gram_ref[low, low], half, 8)
    panel = product(tile, gram_ref[low, high], ((1,), (0,)))
    tile_ref[...] = tile
    panel_ref[...] = panel
    left_ref[...] = gram_ref[high, high] - product(panel, panel, ((0,), (0,)))


def factor_second_kernel(tile_ref, panel_ref, left_ref, out_ref):
    half = tile_ref.shape[0]
    low, high = pl.ds(0, half), pl.ds(half, half)
    tile = diagonal_inverse(left_ref[...], half, 8)
    cross = product(panel_ref[...], tile_ref[...], ((0,), (0,)))
    out_ref[low, low] = tile_ref[...]
    out_ref[low, high] = jnp.zeros((half, half), jnp.float32)
    out_ref[high, low] = -product(tile, cross, ((1,), (0,)))
    out_ref[high, high] = tile


def inverse_factor(*parts):
    rank = parts[0].shape[1]
    half = rank // 2
    pieces = call(
        factor_first_kernel,
        [vmem(half, half)] * 3,
        *parts,
        scratch=[(rank, rank)],
        flops=2_000_000_000,
    )
    return call(factor_second_kernel, vmem(rank, rank), *pieces, flops=2_000_000_000)


def distances(axis):
    size = lax.axis_size(axis)
    return [1 << i for i in range(size.bit_length() - 1)]


def side(axis, distance):
    return lax.axis_index(axis) // distance % 2


def swap(x, axis, distance):
    pairs = [(i, i ^ distance) for i in range(lax.axis_size(axis))]
    return lax.ppermute(x, axis, pairs)


def halve(x, axis, distance):
    half = x.shape[0] // 2
    mine = side(axis, distance)
    keep = lax.dynamic_slice_in_dim(x, mine * half, half, 0)
    send = lax.dynamic_slice_in_dim(x, (1 - mine) * half, half, 0)
    return keep + swap(send, axis, distance)


def double(x, axis, distance):
    other = swap(x, axis, distance)
    first = side(axis, distance) == 0
    return jnp.concatenate([jnp.where(first, x, other), jnp.where(first, other, x)])


def summed_rows(x, hops):
    for hop in hops:
        x = halve(x, *hop)
    for hop in reversed(hops):
        x = double(x, *hop)
    return x


def spread_body(keys, values, queries, start_block, lengths):
    _, tok_dev, kv_dev = keys.shape
    keys, values = keys[0], values[0]
    rank = start_block.shape[1]
    rows = queries.shape[1]
    local_heads = queries.shape[2] // HD
    group = QH // KVH
    kv_local = kv_dev // HD
    tok_hops = [("tok", d) for d in distances("tok")]
    wide_hops = [("head", d) for d in distances("head")] + [("lay", d) for d in distances("lay")]

    def whole_gram(block):
        share = rank
        at = 0
        for axis, distance in reversed(wide_hops):
            share //= 2
            at = at + side(axis, distance) * share
        part = lax.dynamic_slice_in_dim(block, at, share, 1)
        gram = product(part, block, ((0,), (0,)))
        for hop in tok_hops:
            gram = gram + swap(gram, *hop)
        for hop in wide_hops:
            gram = double(gram, *hop)
        return gram

    def project(block):
        return summed_rows(product(keys, block, ((0,), (0,))), tok_hops)

    def mix(coef):
        return summed_rows(product(keys, coef, ((1,), (0,))), wide_hops)

    block = start_block
    for step in range(ITERS):
        lower = inverse_factor(whole_gram(block))
        block = product(mix(project(block)), lower, ((1,), (1,)))
    lower = inverse_factor(whole_gram(block))
    coef = product(project(block), lower, ((1,), (1,)))
    basis = product(block, lower, ((1,), (1,)))

    quer = queries.reshape(rows, kv_local, group, HD)
    factor = coef.reshape(kv_local, HD, rank)
    reduced = jnp.einsum("bgid,gdr->gibr", quer, factor, precision=HIGHEST) / math.sqrt(HD)
    reduced = reduced.reshape(kv_local, group * rows, rank)
    scores = jnp.einsum("tr,gxr->tgx", basis, reduced, precision=HIGHEST)
    position = lax.axis_index("tok") * tok_dev + jnp.arange(tok_dev, dtype=jnp.int32)
    valid = position[:, None] < lengths[None, :]
    valid = jnp.tile(valid, (1, group))[:, None, :]
    peak = jnp.max(jnp.where(valid, scores, NEG), axis=0)
    weight = jnp.where(valid, jnp.exp(scores - peak[None]), 0.0)
    total = jnp.sum(weight, axis=0)
    vals = values.reshape(tok_dev, kv_local, HD)
    summed = jnp.einsum("tgx,tgd->gxd", weight, vals, precision=HIGHEST)
    peak = peak.reshape(local_heads, rows)
    total = total.reshape(local_heads, rows)
    summed = summed.reshape(local_heads, rows, HD)

    share = local_heads // lax.axis_size("tok")
    peak, total, summed = jax.tree.map(
        lambda a: a.reshape((-1, share) + a.shape[1:]), (peak, total, summed)
    )

    def pack(part):
        top, tot, acc = part
        blank = jnp.zeros(top.shape[:-1] + (HD - 2 * rows,), jnp.float32)
        extra = jnp.concatenate([top, tot, blank], axis=-1).reshape(-1, HD)
        return jnp.concatenate([acc.reshape(-1, HD), extra])

    def unpack(buffer, like):
        count = like[0].shape[0] * share
        extra = buffer[count * rows :]
        return (
            extra[:, :rows].reshape(like[0].shape),
            extra[:, rows : 2 * rows].reshape(like[0].shape),
            buffer[: count * rows].reshape(like[2].shape),
        )

    state = (peak, total, summed)
    for hop in tok_hops:
        mine = side(*hop)
        pairs = jax.tree.map(lambda a: a.reshape((-1, 2) + a.shape[1:]), state)
        keep = jax.tree.map(lambda a: lax.dynamic_index_in_dim(a, mine, 1, False), pairs)
        send = jax.tree.map(lambda a: lax.dynamic_index_in_dim(a, 1 - mine, 1, False), pairs)
        got = unpack(swap(pack(send), *hop), keep)
        top = jnp.maximum(keep[0], got[0])
        one, two = jnp.exp(keep[0] - top), jnp.exp(got[0] - top)
        state = (
            top,
            keep[1] * one + got[1] * two,
            keep[2] * one[..., None] + got[2] * two[..., None],
        )
    result = state[2][0] / state[1][0][..., None]
    return result.transpose(1, 0, 2).reshape(1, rows, 1, share * HD)


def pair_sides():
    return side("tok", 1), side("tok", 2), lax.axis_index("lay"), lax.axis_index("head")


def lanes(index, size=HD):
    return pl.ds(pl.multiple_of(index * size, size), size)


def gram_share(block_ref, scratch_ref, out_ref):
    _, _, lay, head = pair_sides()
    half = block_ref.shape[1] // 2
    rows = out_ref.shape[0]
    scratch_ref[...] = product(block_ref[:, lanes(head, half)], block_ref[...], ((0,), (0,)))
    out_ref[...] = scratch_ref[lanes(lay, rows), :]


def start_kernel(keys_ref, block_ref, keep_ref, send_ref, kept_ref, gram_ref, scratch_ref):
    mine, _, _, _ = pair_sides()
    gram_share(block_ref, scratch_ref, gram_ref)
    for i in range(2):
        at = pl.ds(i * HD, HD)
        other = keys_ref[:, lanes(2 * i + 1 - mine)]
        send_ref[at, :] = product(other, block_ref[...], ((0,), (0,)))
        kept_ref[:, at] = keys_ref[:, lanes(2 * i + mine)]
        keep_ref[at, :] = product(kept_ref[:, at], block_ref[...], ((0,), (0,)))


def mix_kernel(own_ref, other_ref, first_ref, second_ref, keep_ref, send_ref):
    mine, _, _, head = pair_sides()
    coef = first_ref[...] + second_ref[...]
    half = own_ref.shape[0] // 2
    for keys_ref, piece in ((own_ref, mine), (other_ref, 1 - mine)):
        to = lanes(piece, half)
        keep_ref[to, :] = product(keys_ref[lanes(head, half), :], coef, ((1,), (0,)))
        send_ref[to, :] = product(keys_ref[lanes(1 - head, half), :], coef, ((1,), (0,)))


def streams_kernel(first_ref, second_ref, a_keep, a_send, b_keep, b_send):
    mine, _, lay, _ = pair_sides()
    half = first_ref.shape[0] // 2
    quarter, eighth = half // 2, half // 4

    def rows(piece, at, count):
        here = pl.ds(pl.multiple_of(piece * half + at, count), count)
        return first_ref[here, :] + second_ref[here, :]

    for piece in range(2):
        to = pl.ds(piece * eighth, eighth)
        a_keep[to, :] = rows(piece, lay * eighth, eighth)
        a_send[to, :] = rows(piece, (1 - lay) * eighth, eighth)
    b_keep[...] = rows(mine, quarter, quarter)
    b_send[...] = rows(1 - mine, quarter, quarter)


def summed_streams(keep, send):
    got = swap(send, "head", 1)
    quarter = vmem(keep.shape[0] // 4, keep.shape[1])
    a_keep, a_send, b_keep, b_send = call(streams_kernel, [quarter] * 4, keep, got)
    a = a_keep + swap(a_send, "lay", 1)
    b = b_keep + swap(b_send, "tok", 1)
    a, b = a + swap(a, "tok", 1), b + swap(b, "lay", 1)
    stack = jnp.concatenate([a, swap(a, "lay", 1), b, swap(b, "tok", 1)])
    return stack, swap(stack, "head", 1)


def block_kernel(
    own_ref, other_ref, near_ref, far_ref, lower_ref, block_ref, proj_ref, gram_ref, whole_ref, scratch_ref
):
    mine, _, lay, head = pair_sides()
    count = near_ref.shape[0] // 4
    half, eighth = count // 2, count // 2
    piece_rows = near_ref.shape[0]
    for ref, owner in ((near_ref, head), (far_ref, 1 - head)):
        for i in range(2):
            for piece in range(2):
                place = (piece ^ mine) * piece_rows + owner * (piece_rows // 2)
                to = place + (lay ^ i) * half
                whole_ref[pl.ds(pl.multiple_of(to, half), half), :] = ref[
                    pl.ds(i * count + piece * half, half), :
                ]
            place = i * piece_rows + owner * (piece_rows // 2) + count
            whole_ref[pl.ds(pl.multiple_of(place, count), count), :] = ref[
                pl.ds((2 + i) * count, count), :
            ]
    block_ref[...] = product(whole_ref[...], lower_ref[...], ((1,), (1,)))
    gram_share(block_ref, scratch_ref, gram_ref)
    proj_ref[...] = product(own_ref[...], block_ref[pl.ds(0, piece_rows), :], ((0,), (0,))) + product(
        other_ref[...], block_ref[pl.ds(piece_rows, piece_rows), :], ((0,), (0,))
    )


def attend_kernel(
    query_ref, block_ref, first_ref, second_ref, lower_ref, own_ref, other_ref, length_ref, keep_ref, send_ref
):
    mine, upper, _, _ = pair_sides()
    rows = query_ref.shape[0]
    group = QH // KVH
    tokens = own_ref.shape[0]
    lower = lower_ref[...]
    basis = product(block_ref[...], lower, ((1,), (1,)))
    here = lax.axis_index("tok") * tokens
    there = (lax.axis_index("tok") ^ 1) * tokens
    at = lax.broadcasted_iota(jnp.int32, (2 * tokens, group * rows), 0)
    position = jnp.where(at < tokens, here + at, there + at - tokens)
    valid = position < length_ref[...]
    for ref, which in ((keep_ref, upper), (send_ref, 1 - upper)):
        local = lanes(which)
        coef = product(first_ref[local, :] + second_ref[local, :], lower, ((1,), (1,)))
        quer = jnp.concatenate(
            [query_ref[:, lanes((2 * which + mine) * group + i)] for i in range(group)]
        )
        reduced = product(quer, coef, ((1,), (0,))) / math.sqrt(HD)
        scores = product(basis, reduced, ((1,), (1,)))
        peak = jnp.max(jnp.where(valid, scores, NEG), axis=0, keepdims=True)
        weight = jnp.where(valid, jnp.exp(scores - peak), 0.0)
        ref[pl.ds(0, HD), :] = product(own_ref[:, local], weight[:tokens], ((0,), (0,))) + product(
            other_ref[:, local], weight[tokens:], ((0,), (0,))
        )
        ref[pl.ds(HD, 8), :] = jnp.broadcast_to(peak, (8, group * rows))
        ref[pl.ds(HD + 8, 8), :] = jnp.broadcast_to(
            jnp.sum(weight, axis=0, keepdims=True), (8, group * rows)
        )


def merge_kernel(first_ref, second_ref, out_ref):
    rows = out_ref.shape[0]
    top = jnp.maximum(first_ref[pl.ds(HD, 1), :], second_ref[pl.ds(HD, 1), :])
    one = jnp.exp(first_ref[pl.ds(HD, 1), :] - top)
    two = jnp.exp(second_ref[pl.ds(HD, 1), :] - top)
    total = first_ref[pl.ds(HD + 8, 1), :] * one + second_ref[pl.ds(HD + 8, 1), :] * two
    acc = first_ref[pl.ds(0, HD), :] * one + second_ref[pl.ds(0, HD), :] * two
    result = (acc / total).T
    for i in range(QH // KVH):
        out_ref[:, pl.ds(i * HD, HD)] = result[i * rows : (i + 1) * rows, :]


def whole_factor(share):
    share = share + swap(share, "tok", 2)
    beside = swap(share, "lay", 1)
    return inverse_factor(share, beside, swap(share, "head", 1), swap(beside, "head", 1))


def after(x, *others):
    return lax.optimization_barrier((x, *others))[0]


def paired_body(keys, values, queries, start_block, lengths):
    _, tokens, width = keys.shape
    keys, values, queries = keys[0], values[0], queries[0]
    rank = start_block.shape[1]
    rows = queries.shape[0]
    half, share = width // 2, rank // 4
    mine = side("tok", 1)

    def columns(x, parity):
        parts = x.reshape(tokens, 2, 2, HD)
        return lax.dynamic_index_in_dim(parts, parity, 2, False).reshape(tokens, half)

    keys_other = swap(columns(keys, 1 - mine), "tok", 1)
    keep, send, keys_own, gram = call(
        start_kernel,
        [vmem(half, rank), vmem(half, rank), vmem(tokens, half), vmem(share, rank)],
        keys,
        start_block,
        scratch=[(rank // 2, rank)],
        flops=900_000_000,
    )
    proj = keep + swap(send, "tok", 1)
    gram = gram + swap(gram, "tok", 1)
    for step in range(ITERS):
        first, second = proj, swap(proj, "tok", 2)
        lower = whole_factor(gram)
        z_keep, z_send = call(
            mix_kernel,
            [vmem(tokens, rank)] * 2,
            keys_own,
            keys_other,
            first,
            second,
            flops=900_000_000,
        )
        near, far = summed_streams(z_keep, z_send)
        block, proj, gram = call(
            block_kernel,
            [vmem(2 * tokens, rank), vmem(half, rank), vmem(share, rank)],
            keys_own,
            keys_other,
            near,
            far,
            lower,
            scratch=[(2 * tokens, rank), (rank // 2, rank)],
            flops=1_500_000_000,
        )
        if step == 0:
            values_other = swap(after(columns(values, 1 - mine), block), "tok", 1)
    lower = whole_factor(gram)
    second = swap(proj, "tok", 2)
    keep, send = call(
        attend_kernel,
        [vmem(HD + 16, HD)] * 2,
        queries,
        block,
        proj,
        second,
        lower,
        columns(values, mine),
        values_other,
        jnp.tile(lengths, QH // KVH)[None, :],
        flops=3_000_000_000,
    )
    result = call(merge_kernel, vmem(rows, half * 4), keep, swap(send, "tok", 2))
    return result[None, :, None, :]


def solution(mesh):
    paired = (mesh.shape["tok"], mesh.shape["lay"], mesh.shape["head"]) == (4, 2, 2)
    body = paired_body if paired else spread_body
    return jax.shard_map(
        body,
        mesh=mesh,
        in_specs=(
            P("lay", ("groups", "tok"), "head"),
            P("lay", ("groups", "tok"), "head"),
            P("lay", "groups", "head"),
            P(("groups", "tok"), None),
            P("groups"),
        ),
        out_specs=P("lay", "groups", "head", "tok"),
        check_vma=False,
    )
```

```python
import functools
import math

import jax
import jax.numpy as jnp
from jax import lax
from jax.experimental import pallas as pl
from jax.experimental.pallas import tpu as pltpu
from jax.sharding import PartitionSpec as P

KVH = 8
HD = 128
QH = 64
ITERS = 2

NEG = -1e30
HIGHEST = lax.Precision.HIGHEST


def product(left, right, dims):
    return lax.dot_general(
        left, right, (dims, ((), ())), precision=HIGHEST, preferred_element_type=jnp.float32
    )


def diagonal_inverse(tile, step=8):
    size = tile.shape[0]
    rows = lax.broadcasted_iota(jnp.int32, (size, 2 * size), 0)
    cols = lax.broadcasted_iota(jnp.int32, (size, 2 * size), 1)
    state = jnp.concatenate([tile, jnp.zeros_like(tile)], axis=1)
    state = state + jnp.where(cols == rows + size, 1.0, 0.0)
    done = []
    for start in range(0, size, step):
        col = [
            jnp.broadcast_to(state[:, start + i : start + i + 1], state.shape) for i in range(step)
        ]
        row = [state[i : i + 1, :] for i in range(step)]
        state = state[step:]
        for i in range(step):
            pivot = col[i][i : i + 1, :]
            inverse = 1.0 / pivot
            for k in range(i + 1, step):
                ratio = col[i][k : k + 1, :] * inverse
                row[k] = row[k] - ratio * row[i]
                col[k] = col[k] - ratio * col[i]
            if start + step < size:
                state = state - col[i][step:] * (row[i] * inverse)
            done.append(row[i] * lax.rsqrt(pivot))
    return jnp.concatenate(done)[:, size:]


def vmem(*shape):
    return jax.ShapeDtypeStruct(shape, jnp.float32)


def call(kernel, out_shape, *args, scratch=(), flops=0):
    spec = pl.BlockSpec(memory_space=pltpu.VMEM)
    single = not isinstance(out_shape, (tuple, list))
    moved = sum(4 * math.prod(a.shape) for a in (*args, *((out_shape,) if single else out_shape)))
    return pl.pallas_call(
        kernel,
        out_shape=out_shape,
        in_specs=[spec] * len(args),
        out_specs=spec if single else [spec] * len(out_shape),
        scratch_shapes=[pltpu.VMEM(s, jnp.float32) for s in scratch],
        compiler_params=pltpu.CompilerParams(vmem_limit_bytes=40 << 20),
        cost_estimate=pl.CostEstimate(flops=flops, bytes_accessed=moved, transcendentals=0),
    )(*args)


def factor_kernel(own_ref, *refs):
    *part_refs, out_ref, gram_ref, tile_ref, panel_ref = refs
    part_refs = (own_ref, *part_refs)
    if len(part_refs) == 1:
        gram_ref[...] = own_ref[...]
    else:
        lay, head = lax.axis_index("lay"), lax.axis_index("head")
        rows = own_ref.shape[0]
        for i, ref in enumerate(part_refs):
            at = (2 * (head ^ (i // 2)) + (lay ^ (i % 2))) * rows
            gram_ref[pl.ds(pl.multiple_of(at, rows), rows), :] = ref[...]
    half = tile_ref.shape[0]
    low, high = pl.ds(0, half), pl.ds(half, half)

    @pl.loop(0, 2)
    def _(i):
        here = pl.ds(pl.multiple_of(i * half, half), half)
        tile_ref[...] = diagonal_inverse(gram_ref[here, here])
        out_ref[here, here] = tile_ref[...]

        @pl.when(i == 0)
        def _():
            panel = product(tile_ref[...], gram_ref[low, high], ((1,), (0,)))
            gram_ref[high, high] = gram_ref[high, high] - product(panel, panel, ((0,), (0,)))
            panel_ref[...] = product(panel, tile_ref[...], ((0,), (0,)))
            out_ref[low, high] = jnp.zeros((half, half), jnp.float32)

        @pl.when(i == 1)
        def _():
            out_ref[high, low] = -product(tile_ref[...], panel_ref[...], ((1,), (0,)))


def inverse_factor(*parts):
    rank = parts[0].shape[1]
    half = rank // 2
    return call(
        factor_kernel,
        vmem(rank, rank),
        *parts,
        scratch=[(rank, rank), (half, half), (half, half)],
        flops=10_000_000_000,
    )


def distances(axis):
    size = lax.axis_size(axis)
    return [1 << i for i in range(size.bit_length() - 1)]


def side(axis, distance):
    return lax.axis_index(axis) // distance % 2


def swap(x, axis, distance):
    pairs = [(i, i ^ distance) for i in range(lax.axis_size(axis))]
    return lax.ppermute(x, axis, pairs)


def halve(x, axis, distance):
    half = x.shape[0] // 2
    mine = side(axis, distance)
    keep = lax.dynamic_slice_in_dim(x, mine * half, half, 0)
    send = lax.dynamic_slice_in_dim(x, (1 - mine) * half, half, 0)
    return keep + swap(send, axis, distance)


def double(x, axis, distance):
    other = swap(x, axis, distance)
    first = side(axis, distance) == 0
    return jnp.concatenate([jnp.where(first, x, other), jnp.where(first, other, x)])


def summed_rows(x, hops):
    for hop in hops:
        x = halve(x, *hop)
    for hop in reversed(hops):
        x = double(x, *hop)
    return x


def spread_body(keys, values, queries, start_block, lengths):
    _, tok_dev, kv_dev = keys.shape
    keys, values = keys[0], values[0]
    rank = start_block.shape[1]
    rows = queries.shape[1]
    local_heads = queries.shape[2] // HD
    group = QH // KVH
    kv_local = kv_dev // HD
    tok_hops = [("tok", d) for d in distances("tok")]
    wide_hops = [("head", d) for d in distances("head")] + [("lay", d) for d in distances("lay")]

    def whole_gram(block):
        share = rank
        at = 0
        for axis, distance in reversed(wide_hops):
            share //= 2
            at = at + side(axis, distance) * share
        part = lax.dynamic_slice_in_dim(block, at, share, 1)
        gram = product(part, block, ((0,), (0,)))
        for hop in tok_hops:
            gram = gram + swap(gram, *hop)
        for hop in wide_hops:
            gram = double(gram, *hop)
        return gram

    def project(block):
        return summed_rows(product(keys, block, ((0,), (0,))), tok_hops)

    def mix(coef):
        return summed_rows(product(keys, coef, ((1,), (0,))), wide_hops)

    block = start_block
    for step in range(ITERS):
        lower = inverse_factor(whole_gram(block))
        block = product(mix(project(block)), lower, ((1,), (1,)))
    lower = inverse_factor(whole_gram(block))
    coef = product(project(block), lower, ((1,), (1,)))
    basis = product(block, lower, ((1,), (1,)))

    quer = queries.reshape(rows, kv_local, group, HD)
    factor = coef.reshape(kv_local, HD, rank)
    reduced = jnp.einsum("bgid,gdr->gibr", quer, factor, precision=HIGHEST) / math.sqrt(HD)
    reduced = reduced.reshape(kv_local, group * rows, rank)
    scores = jnp.einsum("tr,gxr->tgx", basis, reduced, precision=HIGHEST)
    position = lax.axis_index("tok") * tok_dev + jnp.arange(tok_dev, dtype=jnp.int32)
    valid = position[:, None] < lengths[None, :]
    valid = jnp.tile(valid, (1, group))[:, None, :]
    peak = jnp.max(jnp.where(valid, scores, NEG), axis=0)
    weight = jnp.where(valid, jnp.exp(scores - peak[None]), 0.0)
    total = jnp.sum(weight, axis=0)
    vals = values.reshape(tok_dev, kv_local, HD)
    summed = jnp.einsum("tgx,tgd->gxd", weight, vals, precision=HIGHEST)
    peak = peak.reshape(local_heads, rows)
    total = total.reshape(local_heads, rows)
    summed = summed.reshape(local_heads, rows, HD)

    share = local_heads // lax.axis_size("tok")
    peak, total, summed = jax.tree.map(
        lambda a: a.reshape((-1, share) + a.shape[1:]), (peak, total, summed)
    )

    def pack(part):
        top, tot, acc = part
        blank = jnp.zeros(top.shape[:-1] + (HD - 2 * rows,), jnp.float32)
        extra = jnp.concatenate([top, tot, blank], axis=-1).reshape(-1, HD)
        return jnp.concatenate([acc.reshape(-1, HD), extra])

    def unpack(buffer, like):
        count = like[0].shape[0] * share
        extra = buffer[count * rows :]
        return (
            extra[:, :rows].reshape(like[0].shape),
            extra[:, rows : 2 * rows].reshape(like[0].shape),
            buffer[: count * rows].reshape(like[2].shape),
        )

    state = (peak, total, summed)
    for hop in tok_hops:
        mine = side(*hop)
        pairs = jax.tree.map(lambda a: a.reshape((-1, 2) + a.shape[1:]), state)
        keep = jax.tree.map(lambda a: lax.dynamic_index_in_dim(a, mine, 1, False), pairs)
        send = jax.tree.map(lambda a: lax.dynamic_index_in_dim(a, 1 - mine, 1, False), pairs)
        got = unpack(swap(pack(send), *hop), keep)
        top = jnp.maximum(keep[0], got[0])
        one, two = jnp.exp(keep[0] - top), jnp.exp(got[0] - top)
        state = (
            top,
            keep[1] * one + got[1] * two,
            keep[2] * one[..., None] + got[2] * two[..., None],
        )
    result = state[2][0] / state[1][0][..., None]
    return result.transpose(1, 0, 2).reshape(1, rows, 1, share * HD)


def pair_sides():
    return side("tok", 1), side("tok", 2), lax.axis_index("lay"), lax.axis_index("head")


def lanes(index, size=HD):
    return pl.ds(pl.multiple_of(index * size, size), size)


def share_of(scratch_ref, out_ref):
    rows = out_ref.shape[0]
    out_ref[...] = scratch_ref[lanes(lax.axis_index("lay"), rows), :]


def start_kernel(
    keys_ref, block_ref, keep_ref, send_ref, kept_ref, sent_ref, gram_ref, scratch_ref
):
    mine, _, _, head = pair_sides()
    half = block_ref.shape[1] // 2

    @pl.loop(0, 2)
    def _(i):
        at = lanes(i)
        kept_ref[:, at] = keys_ref[:, lanes(2 * i + mine)]
        sent_ref[:, at] = keys_ref[:, lanes(2 * i + 1 - mine)]

    send_ref[...] = product(sent_ref[...], block_ref[...], ((0,), (0,)))
    keep_ref[...] = product(kept_ref[...], block_ref[...], ((0,), (0,)))
    scratch_ref[...] = product(block_ref[:, lanes(head, half)], block_ref[...], ((0,), (0,)))
    share_of(scratch_ref, gram_ref)


def mix_kernel(own_ref, other_ref, first_ref, second_ref, keep_ref, send_ref, coef_ref):
    mine, _, _, head = pair_sides()
    coef_ref[...] = first_ref[...] + second_ref[...]
    half = own_ref.shape[0] // 2
    for keys_ref, piece in ((own_ref, mine), (other_ref, 1 - mine)):
        to = lanes(piece, half)

        @pl.loop(0, 2)
        def _(i):
            term = product(keys_ref[lanes(i, half), :], coef_ref[...], ((1,), (0,)))

            @pl.when(i == head)
            def _():
                keep_ref[to, :] = term

            @pl.when(i != head)
            def _():
                send_ref[to, :] = term


def streams_kernel(first_ref, second_ref, a_keep, a_send, b_keep, b_send):
    mine, _, lay, _ = pair_sides()
    half = first_ref.shape[0] // 2
    quarter, eighth = half // 2, half // 4

    def rows(piece, at, count):
        here = pl.ds(pl.multiple_of(piece * half + at, count), count)
        return first_ref[here, :] + second_ref[here, :]

    for piece in range(2):
        to = pl.ds(piece * eighth, eighth)
        a_keep[to, :] = rows(piece, lay * eighth, eighth)
        a_send[to, :] = rows(piece, (1 - lay) * eighth, eighth)
    b_keep[...] = rows(mine, quarter, quarter)
    b_send[...] = rows(1 - mine, quarter, quarter)


def summed_streams(keep, send, lower):
    got = swap(send, "head", 1)
    quarter = vmem(keep.shape[0] // 4, keep.shape[1])
    a_keep, a_send, b_keep, b_send = call(streams_kernel, [quarter] * 4, keep, got)
    a = a_keep + swap(a_send, "lay", 1)
    b = b_keep + swap(b_send, "tok", 1)
    a, b = a + swap(a, "tok", 1), b + swap(b, "lay", 1)
    a = after(a, lower)
    stack = jnp.concatenate([a, swap(a, "lay", 1), b, swap(b, "tok", 1)])
    return stack, swap(stack, "head", 1)


def block_kernel(
    own_ref, other_ref, near_ref, far_ref, lower_ref, block_ref, proj_ref, gram_ref, whole_ref, scratch_ref
):
    mine, _, lay, head = pair_sides()
    count = near_ref.shape[0] // 4
    half, eighth = count // 2, count // 2
    piece_rows = near_ref.shape[0]
    for ref, owner in ((near_ref, head), (far_ref, 1 - head)):
        for i in range(2):
            for piece in range(2):
                place = (piece ^ mine) * piece_rows + owner * (piece_rows // 2)
                to = place + (lay ^ i) * half
                whole_ref[pl.ds(pl.multiple_of(to, half), half), :] = ref[
                    pl.ds(i * count + piece * half, half), :
                ]
            place = i * piece_rows + owner * (piece_rows // 2) + count
            whole_ref[pl.ds(pl.multiple_of(place, count), count), :] = ref[
                pl.ds((2 + i) * count, count), :
            ]
    columns = scratch_ref.shape[0]
    proj_ref[...] = jnp.zeros(proj_ref.shape, jnp.float32)
    scratch_ref[...] = jnp.zeros(scratch_ref.shape, jnp.float32)
    for i, keys_ref in enumerate((own_ref, other_ref)):

        @pl.loop(0, 2)
        def _(k):
            rows = piece_rows // 2
            here = pl.ds(pl.multiple_of(i * piece_rows + k * rows, rows), rows)
            block_ref[here, :] = product(whole_ref[here, :], lower_ref[...], ((1,), (1,)))
            block = block_ref[here, :]
            proj_ref[...] += product(keys_ref[lanes(k, rows), :], block, ((0,), (0,)))
            scratch_ref[...] += product(block_ref[here, lanes(head, columns)], block, ((0,), (0,)))

    share_of(scratch_ref, gram_ref)


def attend_kernel(
    query_ref,
    block_ref,
    first_ref,
    second_ref,
    lower_ref,
    own_ref,
    low_ref,
    high_ref,
    length_ref,
    keep_ref,
    send_ref,
    basis_ref,
    score_ref,
):
    mine, upper, _, _ = pair_sides()
    group = QH // KVH
    tokens = own_ref.shape[0]
    width = score_ref.shape[1]

    @pl.loop(0, 4)
    def _(i):
        here = lanes(i, tokens // 2)
        basis_ref[here, :] = product(block_ref[here, :], lower_ref[...], ((1,), (1,)))

    first = lax.axis_index("tok") * tokens
    second = (lax.axis_index("tok") ^ 1) * tokens
    at = lax.broadcasted_iota(jnp.int32, (2 * tokens, width), 0)
    valid = jnp.where(at < tokens, first + at, second + at - tokens) < length_ref[...]

    @pl.loop(0, 2)
    def _(which):
        local = lanes(which)
        coef = product(first_ref[local, :] + second_ref[local, :], lower_ref[...], ((1,), (1,)))
        quer = jnp.concatenate(
            [query_ref[:, lanes((2 * which + mine) * group + i)] for i in range(group)]
        )
        reduced = product(quer, coef, ((1,), (0,))) / math.sqrt(HD)
        score_ref[...] = product(basis_ref[...], reduced, ((1,), (1,)))
        peak = jnp.max(jnp.where(valid, score_ref[...], NEG), axis=0, keepdims=True)
        weight = jnp.where(valid, jnp.exp(score_ref[...] - peak), 0.0)
        total = jnp.sum(weight, axis=0, keepdims=True)
        other = jnp.where(which == 0, low_ref[...], high_ref[...])
        acc = product(own_ref[:, local], weight[:tokens], ((0,), (0,))) + product(
            other, weight[tokens:], ((0,), (0,))
        )

        def give(ref):
            ref[pl.ds(0, HD), :] = acc
            ref[pl.ds(HD, 8), :] = jnp.broadcast_to(peak, (8, width))
            ref[pl.ds(HD + 8, 8), :] = jnp.broadcast_to(total, (8, width))

        pl.when(which == upper)(lambda: give(keep_ref))
        pl.when(which != upper)(lambda: give(send_ref))


def merge_kernel(first_ref, second_ref, out_ref):
    rows = out_ref.shape[0]
    top = jnp.maximum(first_ref[pl.ds(HD, 1), :], second_ref[pl.ds(HD, 1), :])
    one = jnp.exp(first_ref[pl.ds(HD, 1), :] - top)
    two = jnp.exp(second_ref[pl.ds(HD, 1), :] - top)
    total = first_ref[pl.ds(HD + 8, 1), :] * one + second_ref[pl.ds(HD + 8, 1), :] * two
    acc = first_ref[pl.ds(0, HD), :] * one + second_ref[pl.ds(0, HD), :] * two
    result = (acc / total).T
    for i in range(QH // KVH):
        out_ref[:, pl.ds(i * HD, HD)] = result[i * rows : (i + 1) * rows, :]


def gathered(share):
    beside = swap(share, "lay", 1)
    return share, beside, swap(share, "head", 1), swap(beside, "head", 1)


def after(x, *others):
    return lax.optimization_barrier((x, *others))[0]


def split_kernel(values_ref, kept_ref, first_ref, second_ref):
    mine, _, _, _ = pair_sides()
    for i, ref in enumerate((first_ref, second_ref)):
        kept_ref[:, pl.ds(i * HD, HD)] = values_ref[:, lanes(2 * i + mine)]
        ref[...] = values_ref[:, lanes(2 * i + 1 - mine)]


def paired_body(keys, values, queries, start_block, lengths):
    _, tokens, width = keys.shape
    keys, values, queries = keys[0], values[0], queries[0]
    rank = start_block.shape[1]
    rows = queries.shape[0]
    half, share = width // 2, rank // 4

    keep, send, keys_own, keys_send, gram = call(
        start_kernel,
        [vmem(half, rank)] * 2 + [vmem(tokens, half)] * 2 + [vmem(share, rank)],
        keys,
        start_block,
        scratch=[(rank // 2, rank)],
        flops=900_000_000,
    )
    gram = gram + swap(gram, "tok", 1)
    proj = keep + swap(send, "tok", 1)
    keys_other = swap(after(keys_send, proj), "tok", 1)
    values_own, *values_send = call(
        split_kernel,
        [vmem(tokens, half)] + [vmem(tokens, HD)] * 2,
        after(values, proj),
    )
    values_other = []
    lower = None
    for step in range(ITERS + 1):
        gram = gram + swap(gram, "tok", 2)
        last = step == ITERS
        if last:
            proj = after(proj, gram)
        first, second = proj, swap(proj, "tok", 2)
        if step > 0 and len(values_other) < 2:
            values_other.append(swap(after(values_send[len(values_other)], proj), "tok", 1))
        parts = gathered(gram)
        lower = inverse_factor(*parts)
        if last:
            break
        if step == 0:
            first = after(first, lower, values_own)
        else:
            first = after(first, *parts, *values_other)
        z_keep, z_send = call(
            mix_kernel,
            [vmem(tokens, rank)] * 2,
            keys_own,
            keys_other,
            first,
            second,
            scratch=[(half, rank)],
            flops=900_000_000,
        )
        near, far = summed_streams(z_keep, z_send, lower)
        block, proj, gram = call(
            block_kernel,
            [vmem(2 * tokens, rank), vmem(half, rank), vmem(share, rank)],
            keys_own,
            keys_other,
            near,
            far,
            lower,
            scratch=[(2 * tokens, rank), (rank // 2, rank)],
            flops=1_500_000_000,
        )
    keep, send = call(
        attend_kernel,
        [vmem(HD + 16, HD)] * 2,
        queries,
        block,
        first,
        second,
        lower,
        values_own,
        *values_other,
        jnp.tile(lengths, QH // KVH)[None, :],
        scratch=[(2 * tokens, rank), (2 * tokens, QH // KVH * rows)],
        flops=3_000_000_000,
    )
    result = call(merge_kernel, vmem(rows, half * 4), keep, swap(send, "tok", 2))
    return result[None, :, None, :]


def solution(mesh):
    paired = (mesh.shape["tok"], mesh.shape["lay"], mesh.shape["head"]) == (4, 2, 2)
    body = paired_body if paired else spread_body
    return jax.shard_map(
        body,
        mesh=mesh,
        in_specs=(
            P("lay", ("groups", "tok"), "head"),
            P("lay", ("groups", "tok"), "head"),
            P("lay", "groups", "head"),
            P(("groups", "tok"), None),
            P("groups"),
        ),
        out_specs=P("lay", "groups", "head", "tok"),
        check_vma=False,
    )
```

```python
import functools
import math

import jax
import jax.numpy as jnp
from jax import lax
from jax.experimental import pallas as pl
from jax.experimental.pallas import tpu as pltpu
from jax.sharding import PartitionSpec as P

KVH = 8
HD = 128
QH = 64
ITERS = 2

NEG = -1e30
HIGHEST = lax.Precision.HIGHEST


def product(left, right, dims):
    return lax.dot_general(
        left, right, (dims, ((), ())), precision=HIGHEST, preferred_element_type=jnp.float32
    )


def diagonal_inverse(tile, step=8):
    size = tile.shape[0]
    rows = lax.broadcasted_iota(jnp.int32, (size, 2 * size), 0)
    cols = lax.broadcasted_iota(jnp.int32, (size, 2 * size), 1)
    state = jnp.concatenate([tile, jnp.zeros_like(tile)], axis=1)
    state = state + jnp.where(cols == rows + size, 1.0, 0.0)
    done = []
    for start in range(0, size, step):
        col = [
            jnp.broadcast_to(state[:, start + i : start + i + 1], state.shape) for i in range(step)
        ]
        row = [state[i : i + 1, :] for i in range(step)]
        state = state[step:]
        for i in range(step):
            pivot = col[i][i : i + 1, :]
            inverse = 1.0 / pivot
            for k in range(i + 1, step):
                ratio = col[i][k : k + 1, :] * inverse
                row[k] = row[k] - ratio * row[i]
                col[k] = col[k] - ratio * col[i]
            if start + step < size:
                state = state - col[i][step:] * (row[i] * inverse)
            done.append(row[i] * lax.rsqrt(pivot))
    return jnp.concatenate(done)[:, size:]


def vmem(*shape):
    return jax.ShapeDtypeStruct(shape, jnp.float32)


def call(kernel, out_shape, *args, scratch=(), flops=0):
    spec = pl.BlockSpec(memory_space=pltpu.VMEM)
    single = not isinstance(out_shape, (tuple, list))
    moved = sum(4 * math.prod(a.shape) for a in (*args, *((out_shape,) if single else out_shape)))
    return pl.pallas_call(
        kernel,
        out_shape=out_shape,
        in_specs=[spec] * len(args),
        out_specs=spec if single else [spec] * len(out_shape),
        scratch_shapes=[pltpu.VMEM(s, jnp.float32) for s in scratch],
        compiler_params=pltpu.CompilerParams(vmem_limit_bytes=40 << 20),
        cost_estimate=pl.CostEstimate(flops=flops, bytes_accessed=moved, transcendentals=0),
    )(*args)


def whole_gram(own_ref, part_refs, gram_ref):
    if not part_refs:
        gram_ref[...] = own_ref[...]
        return
    lay, head = lax.axis_index("lay"), lax.axis_index("head")
    rows = own_ref.shape[0]
    for i, ref in enumerate((own_ref, *part_refs)):
        at = (2 * (head ^ (i // 2)) + (lay ^ (i % 2))) * rows
        gram_ref[pl.ds(pl.multiple_of(at, rows), rows), :] = ref[...]


def factor_kernel(own_ref, *refs):
    *part_refs, out_ref, gram_ref, tile_ref, cross_ref = refs
    whole_gram(own_ref, part_refs, gram_ref)
    half = tile_ref.shape[0]
    low, high = pl.ds(0, half), pl.ds(half, half)

    @pl.loop(0, 2)
    def _(i):
        here = pl.ds(pl.multiple_of(i * half, half), half)
        tile_ref[...] = diagonal_inverse(gram_ref[here, here])
        out_ref[here, here] = tile_ref[...]

        @pl.when(i == 0)
        def _():
            panel = product(tile_ref[...], gram_ref[low, high], ((1,), (0,)))
            gram_ref[high, high] = gram_ref[high, high] - product(panel, panel, ((0,), (0,)))
            cross_ref[...] = product(panel, tile_ref[...], ((0,), (0,)))
            out_ref[low, high] = jnp.zeros((half, half), jnp.float32)

        @pl.when(i == 1)
        def _():
            out_ref[high, low] = -product(tile_ref[...], cross_ref[...], ((1,), (0,)))


def factor_low_kernel(own_ref, *refs):
    *part_refs, tile_ref, cross_ref, left_ref, gram_ref = refs
    whole_gram(own_ref, part_refs, gram_ref)
    half = tile_ref.shape[0]
    low, high = pl.ds(0, half), pl.ds(half, half)
    tile_ref[...] = diagonal_inverse(gram_ref[low, low])
    panel = product(tile_ref[...], gram_ref[low, high], ((1,), (0,)))
    left_ref[...] = gram_ref[high, high] - product(panel, panel, ((0,), (0,)))
    cross_ref[...] = product(panel, tile_ref[...], ((0,), (0,)))


def factor_high_kernel(tile_ref, cross_ref, left_ref, out_ref):
    half = tile_ref.shape[0]
    low, high = pl.ds(0, half), pl.ds(half, half)
    out_ref[low, low] = tile_ref[...]
    out_ref[low, high] = jnp.zeros((half, half), jnp.float32)
    out_ref[high, high] = diagonal_inverse(left_ref[...])
    out_ref[high, low] = -product(out_ref[high, high], cross_ref[...], ((1,), (0,)))


FACTOR_FLOPS = 1_000_000_000


def inverse_factor(*parts):
    rank = parts[0].shape[1]
    half = rank // 2
    return call(
        factor_kernel,
        vmem(rank, rank),
        *parts,
        scratch=[(rank, rank), (half, half), (half, half)],
        flops=FACTOR_FLOPS,
    )


def inverse_factor_low(*parts):
    rank = parts[0].shape[1]
    half = rank // 2
    return call(
        factor_low_kernel, [vmem(half, half)] * 3, *parts, scratch=[(rank, rank)], flops=FACTOR_FLOPS
    )


def inverse_factor_high(*halves):
    rank = 2 * halves[0].shape[0]
    return call(factor_high_kernel, vmem(rank, rank), *halves, flops=FACTOR_FLOPS)


def distances(axis):
    size = lax.axis_size(axis)
    return [1 << i for i in range(size.bit_length() - 1)]


def side(axis, distance):
    return lax.axis_index(axis) // distance % 2


def swap(x, axis, distance):
    pairs = [(i, i ^ distance) for i in range(lax.axis_size(axis))]
    return lax.ppermute(x, axis, pairs)


def halve(x, axis, distance):
    half = x.shape[0] // 2
    mine = side(axis, distance)
    keep = lax.dynamic_slice_in_dim(x, mine * half, half, 0)
    send = lax.dynamic_slice_in_dim(x, (1 - mine) * half, half, 0)
    return keep + swap(send, axis, distance)


def double(x, axis, distance):
    other = swap(x, axis, distance)
    first = side(axis, distance) == 0
    return jnp.concatenate([jnp.where(first, x, other), jnp.where(first, other, x)])


def summed_rows(x, hops):
    for hop in hops:
        x = halve(x, *hop)
    for hop in reversed(hops):
        x = double(x, *hop)
    return x


def spread_body(keys, values, queries, start_block, lengths):
    _, tok_dev, kv_dev = keys.shape
    keys, values = keys[0], values[0]
    rank = start_block.shape[1]
    rows = queries.shape[1]
    local_heads = queries.shape[2] // HD
    group = QH // KVH
    kv_local = kv_dev // HD
    tok_hops = [("tok", d) for d in distances("tok")]
    wide_hops = [("head", d) for d in distances("head")] + [("lay", d) for d in distances("lay")]

    def whole_gram(block):
        share = rank
        at = 0
        for axis, distance in reversed(wide_hops):
            share //= 2
            at = at + side(axis, distance) * share
        part = lax.dynamic_slice_in_dim(block, at, share, 1)
        gram = product(part, block, ((0,), (0,)))
        for hop in tok_hops:
            gram = gram + swap(gram, *hop)
        for hop in wide_hops:
            gram = double(gram, *hop)
        return gram

    def project(block):
        return summed_rows(product(keys, block, ((0,), (0,))), tok_hops)

    def mix(coef):
        return summed_rows(product(keys, coef, ((1,), (0,))), wide_hops)

    block = start_block
    for step in range(ITERS):
        lower = inverse_factor(whole_gram(block))
        block = product(mix(project(block)), lower, ((1,), (1,)))
    lower = inverse_factor(whole_gram(block))
    coef = product(project(block), lower, ((1,), (1,)))
    basis = product(block, lower, ((1,), (1,)))

    quer = queries.reshape(rows, kv_local, group, HD)
    factor = coef.reshape(kv_local, HD, rank)
    reduced = jnp.einsum("bgid,gdr->gibr", quer, factor, precision=HIGHEST) / math.sqrt(HD)
    reduced = reduced.reshape(kv_local, group * rows, rank)
    scores = jnp.einsum("tr,gxr->tgx", basis, reduced, precision=HIGHEST)
    position = lax.axis_index("tok") * tok_dev + jnp.arange(tok_dev, dtype=jnp.int32)
    valid = position[:, None] < lengths[None, :]
    valid = jnp.tile(valid, (1, group))[:, None, :]
    peak = jnp.max(jnp.where(valid, scores, NEG), axis=0)
    weight = jnp.where(valid, jnp.exp(scores - peak[None]), 0.0)
    total = jnp.sum(weight, axis=0)
    vals = values.reshape(tok_dev, kv_local, HD)
    summed = jnp.einsum("tgx,tgd->gxd", weight, vals, precision=HIGHEST)
    peak = peak.reshape(local_heads, rows)
    total = total.reshape(local_heads, rows)
    summed = summed.reshape(local_heads, rows, HD)

    share = local_heads // lax.axis_size("tok")
    peak, total, summed = jax.tree.map(
        lambda a: a.reshape((-1, share) + a.shape[1:]), (peak, total, summed)
    )

    def pack(part):
        top, tot, acc = part
        blank = jnp.zeros(top.shape[:-1] + (HD - 2 * rows,), jnp.float32)
        extra = jnp.concatenate([top, tot, blank], axis=-1).reshape(-1, HD)
        return jnp.concatenate([acc.reshape(-1, HD), extra])

    def unpack(buffer, like):
        count = like[0].shape[0] * share
        extra = buffer[count * rows :]
        return (
            extra[:, :rows].reshape(like[0].shape),
            extra[:, rows : 2 * rows].reshape(like[0].shape),
            buffer[: count * rows].reshape(like[2].shape),
        )

    state = (peak, total, summed)
    for hop in tok_hops:
        mine = side(*hop)
        pairs = jax.tree.map(lambda a: a.reshape((-1, 2) + a.shape[1:]), state)
        keep = jax.tree.map(lambda a: lax.dynamic_index_in_dim(a, mine, 1, False), pairs)
        send = jax.tree.map(lambda a: lax.dynamic_index_in_dim(a, 1 - mine, 1, False), pairs)
        got = unpack(swap(pack(send), *hop), keep)
        top = jnp.maximum(keep[0], got[0])
        one, two = jnp.exp(keep[0] - top), jnp.exp(got[0] - top)
        state = (
            top,
            keep[1] * one + got[1] * two,
            keep[2] * one[..., None] + got[2] * two[..., None],
        )
    result = state[2][0] / state[1][0][..., None]
    return result.transpose(1, 0, 2).reshape(1, rows, 1, share * HD)


def pair_sides():
    return side("tok", 1), side("tok", 2), lax.axis_index("lay"), lax.axis_index("head")


def lanes(index, size=HD):
    return pl.ds(pl.multiple_of(index * size, size), size)


def gram_share(block_ref, scratch_ref, out_ref):
    _, _, lay, head = pair_sides()
    rows, half = out_ref.shape[0], scratch_ref.shape[0]
    scratch_ref[...] = product(block_ref[:, lanes(head, half)], block_ref[...], ((0,), (0,)))
    out_ref[...] = scratch_ref[lanes(lay, rows), :]


def gram_kernel(block_ref, out_ref, scratch_ref):
    gram_share(block_ref, scratch_ref, out_ref)


def start_kernel(keys_ref, block_ref, keep_ref, send_ref, kept_ref, sent_ref):
    mine, _, _, _ = pair_sides()
    for i in range(2):
        at = pl.ds(i * HD, HD)
        kept_ref[:, at] = keys_ref[:, lanes(2 * i + mine)]
        sent_ref[:, at] = keys_ref[:, lanes(2 * i + 1 - mine)]
    send_ref[...] = product(sent_ref[...], block_ref[...], ((0,), (0,)))
    keep_ref[...] = product(kept_ref[...], block_ref[...], ((0,), (0,)))


def mix_kernel(own_ref, other_ref, first_ref, second_ref, keep_ref, send_ref):
    mine, _, _, head = pair_sides()
    coef = first_ref[...] + second_ref[...]
    half = own_ref.shape[0] // 2
    for keys_ref, piece in ((own_ref, mine), (other_ref, 1 - mine)):
        to = lanes(piece, half)
        keep_ref[to, :] = product(keys_ref[lanes(head, half), :], coef, ((1,), (0,)))
        send_ref[to, :] = product(keys_ref[lanes(1 - head, half), :], coef, ((1,), (0,)))


def streams_kernel(first_ref, second_ref, a_keep, a_send, b_keep, b_send):
    mine, _, lay, _ = pair_sides()
    half = first_ref.shape[0] // 2
    quarter, eighth = half // 2, half // 4

    def rows(piece, at, count):
        here = pl.ds(pl.multiple_of(piece * half + at, count), count)
        return first_ref[here, :] + second_ref[here, :]

    for piece in range(2):
        to = pl.ds(piece * eighth, eighth)
        a_keep[to, :] = rows(piece, lay * eighth, eighth)
        a_send[to, :] = rows(piece, (1 - lay) * eighth, eighth)
    b_keep[...] = rows(mine, quarter, quarter)
    b_send[...] = rows(1 - mine, quarter, quarter)


def summed_streams(keep, send, lower):
    got = swap(send, "head", 1)
    quarter = vmem(keep.shape[0] // 4, keep.shape[1])
    a_keep, a_send, b_keep, b_send = call(streams_kernel, [quarter] * 4, keep, got)
    a = a_keep + swap(a_send, "lay", 1)
    b = b_keep + swap(b_send, "tok", 1)
    a, b = a + swap(a, "tok", 1), b + swap(b, "lay", 1)
    a = after(a, lower)
    stack = jnp.concatenate([a, swap(a, "lay", 1), b, swap(b, "tok", 1)])
    return stack, swap(stack, "head", 1)


def block_kernel(near_ref, far_ref, lower_ref, block_ref, gram_ref, whole_ref, scratch_ref):
    mine, _, lay, head = pair_sides()
    count = near_ref.shape[0] // 4
    half = count // 2
    piece_rows = near_ref.shape[0]
    for ref, owner in ((near_ref, head), (far_ref, 1 - head)):
        for i in range(2):
            for piece in range(2):
                place = (piece ^ mine) * piece_rows + owner * (piece_rows // 2)
                to = place + (lay ^ i) * half
                whole_ref[pl.ds(pl.multiple_of(to, half), half), :] = ref[
                    pl.ds(i * count + piece * half, half), :
                ]
            place = i * piece_rows + owner * (piece_rows // 2) + count
            whole_ref[pl.ds(pl.multiple_of(place, count), count), :] = ref[
                pl.ds((2 + i) * count, count), :
            ]
    block_ref[...] = product(whole_ref[...], lower_ref[...], ((1,), (1,)))
    gram_share(block_ref, scratch_ref, gram_ref)


def project_kernel(own_ref, other_ref, block_ref, proj_ref):
    rows = own_ref.shape[0]
    proj_ref[...] = product(own_ref[...], block_ref[pl.ds(0, rows), :], ((0,), (0,))) + product(
        other_ref[...], block_ref[pl.ds(rows, rows), :], ((0,), (0,))
    )


def attend_kernel(
    query_ref,
    block_ref,
    first_ref,
    second_ref,
    lower_ref,
    own_ref,
    low_ref,
    high_ref,
    length_ref,
    keep_ref,
    send_ref,
    basis_ref,
):
    mine, upper, _, _ = pair_sides()
    group = QH // KVH
    tokens = own_ref.shape[0]
    width = length_ref.shape[1]
    basis_ref[...] = product(block_ref[...], lower_ref[...], ((1,), (1,)))
    coef = product(first_ref[...] + second_ref[...], lower_ref[...], ((1,), (1,)))
    reduced = []
    for which in range(2):
        quer = jnp.concatenate(
            [query_ref[:, lanes((2 * which + mine) * group + i)] for i in range(group)]
        )
        factor = coef[which * HD : (which + 1) * HD]
        reduced.append(product(quer, factor, ((1,), (0,))) / math.sqrt(HD))
    scores = product(basis_ref[...], jnp.concatenate(reduced), ((1,), (1,)))
    first = lax.axis_index("tok") * tokens
    second = (lax.axis_index("tok") ^ 1) * tokens
    at = lax.broadcasted_iota(jnp.int32, scores.shape, 0)
    valid = jnp.where(at < tokens, first + at, second + at - tokens) < length_ref[...]
    peak = jnp.max(jnp.where(valid, scores, NEG), axis=0, keepdims=True)
    weight = jnp.where(valid, jnp.exp(scores - peak), 0.0)
    total = jnp.sum(weight, axis=0, keepdims=True)
    half = width // 2
    for which, there_ref in enumerate((low_ref, high_ref)):
        here = slice(which * half, (which + 1) * half)
        acc = product(own_ref[:, pl.ds(which * HD, HD)], weight[:tokens, here], ((0,), (0,)))
        acc = acc + product(there_ref[...], weight[tokens:, here], ((0,), (0,)))

        def give(ref):
            ref[pl.ds(0, HD), :] = acc
            ref[pl.ds(HD, 8), :] = jnp.broadcast_to(peak[:, here], (8, half))
            ref[pl.ds(HD + 8, 8), :] = jnp.broadcast_to(total[:, here], (8, half))

        pl.when(upper == which)(lambda: give(keep_ref))
        pl.when(upper != which)(lambda: give(send_ref))


def merge_kernel(first_ref, second_ref, out_ref):
    rows = out_ref.shape[0]
    top = jnp.maximum(first_ref[pl.ds(HD, 1), :], second_ref[pl.ds(HD, 1), :])
    one = jnp.exp(first_ref[pl.ds(HD, 1), :] - top)
    two = jnp.exp(second_ref[pl.ds(HD, 1), :] - top)
    total = first_ref[pl.ds(HD + 8, 1), :] * one + second_ref[pl.ds(HD + 8, 1), :] * two
    acc = first_ref[pl.ds(0, HD), :] * one + second_ref[pl.ds(0, HD), :] * two
    result = (acc / total).T
    for i in range(QH // KVH):
        out_ref[:, pl.ds(i * HD, HD)] = result[i * rows : (i + 1) * rows, :]


def gathered(share):
    beside = swap(share, "lay", 1)
    return share, beside, swap(share, "head", 1), swap(beside, "head", 1)


def after(x, *others):
    return lax.optimization_barrier((x, *others))[0]


def split_kernel(values_ref, kept_ref, first_ref, second_ref):
    mine, _, _, _ = pair_sides()
    for i, ref in enumerate((first_ref, second_ref)):
        kept_ref[:, pl.ds(i * HD, HD)] = values_ref[:, lanes(2 * i + mine)]
        ref[...] = values_ref[:, lanes(2 * i + 1 - mine)]


def paired_body(keys, values, queries, start_block, lengths):
    _, tokens, width = keys.shape
    keys, values, queries = keys[0], values[0], queries[0]
    rank = start_block.shape[1]
    rows = queries.shape[0]
    half, share = width // 2, rank // 4

    gram = call(
        gram_kernel,
        vmem(share, rank),
        start_block,
        scratch=[(rank // 2, rank)],
        flops=400_000_000,
    )
    keep, send, keys_own, keys_send = call(
        start_kernel,
        [vmem(half, rank)] * 2 + [vmem(tokens, half)] * 2,
        keys,
        after(start_block, gram),
        flops=900_000_000,
    )
    gram = gram + swap(gram, "tok", 1)
    proj = keep + swap(after(send, gram), "tok", 1)
    keys_other = swap(after(keys_send, proj), "tok", 1)
    values_own, *values_send = call(
        split_kernel,
        [vmem(tokens, half)] + [vmem(tokens, HD)] * 2,
        after(values, proj),
    )
    values_other = []
    lower = None
    for step in range(ITERS + 1):
        gram = gram + swap(gram, "tok", 2)
        last = step == ITERS
        first, second = proj, swap(proj, "tok", 2)
        if step > 0 and len(values_other) < 2:
            values_other.append(swap(after(values_send[len(values_other)], proj, gram), "tok", 1))
        parts = gathered(gram)
        if step == 0 or last:
            lower = inverse_factor(*parts)
            first = after(first, lower, values_own)
        else:
            halves = inverse_factor_low(*parts)
            first = after(first, halves[0], *values_other)
            lower = inverse_factor_high(*halves)
        if last:
            break
        z_keep, z_send = call(
            mix_kernel,
            [vmem(tokens, rank)] * 2,
            keys_own,
            keys_other,
            first,
            second,
            flops=900_000_000,
        )
        near, far = summed_streams(z_keep, z_send, lower)
        block, gram = call(
            block_kernel,
            [vmem(2 * tokens, rank), vmem(share, rank)],
            near,
            far,
            lower,
            scratch=[(2 * tokens, rank), (rank // 2, rank)],
            flops=1_200_000_000,
        )
        proj = call(
            project_kernel,
            vmem(half, rank),
            keys_own,
            keys_other,
            block,
            flops=900_000_000,
        )
    keep, send = call(
        attend_kernel,
        [vmem(HD + 16, HD)] * 2,
        queries,
        block,
        first,
        second,
        lower,
        values_own,
        *values_other,
        jnp.tile(lengths, 2 * (QH // KVH))[None, :],
        scratch=[(2 * tokens, rank)],
        flops=3_000_000_000,
    )
    result = call(merge_kernel, vmem(rows, half * 4), keep, swap(send, "tok", 2))
    return result[None, :, None, :]


def solution(mesh):
    paired = (mesh.shape["tok"], mesh.shape["lay"], mesh.shape["head"]) == (4, 2, 2)
    body = paired_body if paired else spread_body
    return jax.shard_map(
        body,
        mesh=mesh,
        in_specs=(
            P("lay", ("groups", "tok"), "head"),
            P("lay", ("groups", "tok"), "head"),
            P("lay", "groups", "head"),
            P(("groups", "tok"), None),
            P("groups"),
        ),
        out_specs=P("lay", "groups", "head", "tok"),
        check_vma=False,
    )
```

```python
import functools
import math

import jax
import jax.numpy as jnp
from jax import lax
from jax.experimental import pallas as pl
from jax.experimental.pallas import tpu as pltpu
from jax.sharding import PartitionSpec as P

KVH = 8
HD = 128
QH = 64
ITERS = 2

NEG = -1e30
HIGHEST = lax.Precision.HIGHEST


def product(left, right, dims):
    return lax.dot_general(
        left, right, (dims, ((), ())), precision=HIGHEST, preferred_element_type=jnp.float32
    )


def diagonal_inverse(tile, step=8):
    size = tile.shape[0]
    rows = lax.broadcasted_iota(jnp.int32, (size, 2 * size), 0)
    cols = lax.broadcasted_iota(jnp.int32, (size, 2 * size), 1)
    state = jnp.concatenate([tile, jnp.zeros_like(tile)], axis=1)
    state = state + jnp.where(cols == rows + size, 1.0, 0.0)
    done = []
    for start in range(0, size, step):
        col = [
            jnp.broadcast_to(state[:, start + i : start + i + 1], state.shape) for i in range(step)
        ]
        row = [state[i : i + 1, :] for i in range(step)]
        state = state[step:]
        for i in range(step):
            pivot = col[i][i : i + 1, :]
            inverse = 1.0 / pivot
            for k in range(i + 1, step):
                ratio = col[i][k : k + 1, :] * inverse
                row[k] = row[k] - ratio * row[i]
                col[k] = col[k] - ratio * col[i]
            if start + step < size:
                state = state - col[i][step:] * (row[i] * inverse)
            done.append(row[i] * lax.rsqrt(pivot))
    return jnp.concatenate(done)[:, size:]


def vmem(*shape):
    return jax.ShapeDtypeStruct(shape, jnp.float32)


def call(kernel, out_shape, *args, scratch=(), flops=0):
    spec = pl.BlockSpec(memory_space=pltpu.VMEM)
    single = not isinstance(out_shape, (tuple, list))
    moved = sum(4 * math.prod(a.shape) for a in (*args, *((out_shape,) if single else out_shape)))
    return pl.pallas_call(
        kernel,
        out_shape=out_shape,
        in_specs=[spec] * len(args),
        out_specs=spec if single else [spec] * len(out_shape),
        scratch_shapes=[pltpu.VMEM(s, jnp.float32) for s in scratch],
        compiler_params=pltpu.CompilerParams(vmem_limit_bytes=40 << 20),
        cost_estimate=pl.CostEstimate(flops=flops, bytes_accessed=moved, transcendentals=0),
    )(*args)


def whole_gram(own_ref, part_refs, gram_ref):
    if not part_refs:
        gram_ref[...] = own_ref[...]
        return
    lay, head = lax.axis_index("lay"), lax.axis_index("head")
    rows = own_ref.shape[0]
    for i, ref in enumerate((own_ref, *part_refs)):
        at = (2 * (head ^ (i // 2)) + (lay ^ (i % 2))) * rows
        gram_ref[pl.ds(pl.multiple_of(at, rows), rows), :] = ref[...]


def factor_kernel(own_ref, *refs):
    *part_refs, out_ref, gram_ref, tile_ref, cross_ref = refs
    whole_gram(own_ref, part_refs, gram_ref)
    half = tile_ref.shape[0]
    low, high = pl.ds(0, half), pl.ds(half, half)

    @pl.loop(0, 2)
    def _(i):
        here = pl.ds(pl.multiple_of(i * half, half), half)
        tile_ref[...] = diagonal_inverse(gram_ref[here, here])
        out_ref[here, here] = tile_ref[...]

        @pl.when(i == 0)
        def _():
            panel = product(tile_ref[...], gram_ref[low, high], ((1,), (0,)))
            gram_ref[high, high] = gram_ref[high, high] - product(panel, panel, ((0,), (0,)))
            cross_ref[...] = product(panel, tile_ref[...], ((0,), (0,)))
            out_ref[low, high] = jnp.zeros((half, half), jnp.float32)

        @pl.when(i == 1)
        def _():
            out_ref[high, low] = -product(tile_ref[...], cross_ref[...], ((1,), (0,)))


def factor_low_kernel(own_ref, *refs):
    *part_refs, tile_ref, cross_ref, left_ref, gram_ref = refs
    whole_gram(own_ref, part_refs, gram_ref)
    half = tile_ref.shape[0]
    low, high = pl.ds(0, half), pl.ds(half, half)
    tile_ref[...] = diagonal_inverse(gram_ref[low, low])
    panel = product(tile_ref[...], gram_ref[low, high], ((1,), (0,)))
    left_ref[...] = gram_ref[high, high] - product(panel, panel, ((0,), (0,)))
    cross_ref[...] = product(panel, tile_ref[...], ((0,), (0,)))


def factor_high_kernel(tile_ref, cross_ref, left_ref, out_ref):
    half = tile_ref.shape[0]
    low, high = pl.ds(0, half), pl.ds(half, half)
    out_ref[low, low] = tile_ref[...]
    out_ref[low, high] = jnp.zeros((half, half), jnp.float32)
    out_ref[high, high] = diagonal_inverse(left_ref[...])
    out_ref[high, low] = -product(out_ref[high, high], cross_ref[...], ((1,), (0,)))


FACTOR_FLOPS = 1_000_000_000


def inverse_factor(*parts):
    rank = parts[0].shape[1]
    half = rank // 2
    return call(
        factor_kernel,
        vmem(rank, rank),
        *parts,
        scratch=[(rank, rank), (half, half), (half, half)],
        flops=FACTOR_FLOPS,
    )


def inverse_factor_low(*parts):
    rank = parts[0].shape[1]
    half = rank // 2
    return call(
        factor_low_kernel, [vmem(half, half)] * 3, *parts, scratch=[(rank, rank)], flops=FACTOR_FLOPS
    )


def inverse_factor_high(*halves):
    rank = 2 * halves[0].shape[0]
    return call(factor_high_kernel, vmem(rank, rank), *halves, flops=FACTOR_FLOPS)


def distances(axis):
    size = lax.axis_size(axis)
    return [1 << i for i in range(size.bit_length() - 1)]


def side(axis, distance):
    return lax.axis_index(axis) // distance % 2


def swap(x, axis, distance):
    pairs = [(i, i ^ distance) for i in range(lax.axis_size(axis))]
    return lax.ppermute(x, axis, pairs)


def halve(x, axis, distance):
    half = x.shape[0] // 2
    mine = side(axis, distance)
    keep = lax.dynamic_slice_in_dim(x, mine * half, half, 0)
    send = lax.dynamic_slice_in_dim(x, (1 - mine) * half, half, 0)
    return keep + swap(send, axis, distance)


def double(x, axis, distance):
    other = swap(x, axis, distance)
    first = side(axis, distance) == 0
    return jnp.concatenate([jnp.where(first, x, other), jnp.where(first, other, x)])


def summed_rows(x, hops):
    for hop in hops:
        x = halve(x, *hop)
    for hop in reversed(hops):
        x = double(x, *hop)
    return x


def spread_body(keys, values, queries, start_block, lengths):
    _, tok_dev, kv_dev = keys.shape
    keys, values = keys[0], values[0]
    rank = start_block.shape[1]
    rows = queries.shape[1]
    local_heads = queries.shape[2] // HD
    group = QH // KVH
    kv_local = kv_dev // HD
    tok_hops = [("tok", d) for d in distances("tok")]
    wide_hops = [("head", d) for d in distances("head")] + [("lay", d) for d in distances("lay")]

    def whole_gram(block):
        share = rank
        at = 0
        for axis, distance in reversed(wide_hops):
            share //= 2
            at = at + side(axis, distance) * share
        part = lax.dynamic_slice_in_dim(block, at, share, 1)
        gram = product(part, block, ((0,), (0,)))
        for hop in tok_hops:
            gram = gram + swap(gram, *hop)
        for hop in wide_hops:
            gram = double(gram, *hop)
        return gram

    def project(block):
        return summed_rows(product(keys, block, ((0,), (0,))), tok_hops)

    def mix(coef):
        return summed_rows(product(keys, coef, ((1,), (0,))), wide_hops)

    block = start_block
    for step in range(ITERS):
        lower = inverse_factor(whole_gram(block))
        block = product(mix(project(block)), lower, ((1,), (1,)))
    lower = inverse_factor(whole_gram(block))
    coef = product(project(block), lower, ((1,), (1,)))
    basis = product(block, lower, ((1,), (1,)))

    quer = queries.reshape(rows, kv_local, group, HD)
    factor = coef.reshape(kv_local, HD, rank)
    reduced = jnp.einsum("bgid,gdr->gibr", quer, factor, precision=HIGHEST) / math.sqrt(HD)
    reduced = reduced.reshape(kv_local, group * rows, rank)
    scores = jnp.einsum("tr,gxr->tgx", basis, reduced, precision=HIGHEST)
    position = lax.axis_index("tok") * tok_dev + jnp.arange(tok_dev, dtype=jnp.int32)
    valid = position[:, None] < lengths[None, :]
    valid = jnp.tile(valid, (1, group))[:, None, :]
    peak = jnp.max(jnp.where(valid, scores, NEG), axis=0)
    weight = jnp.where(valid, jnp.exp(scores - peak[None]), 0.0)
    total = jnp.sum(weight, axis=0)
    vals = values.reshape(tok_dev, kv_local, HD)
    summed = jnp.einsum("tgx,tgd->gxd", weight, vals, precision=HIGHEST)
    peak = peak.reshape(local_heads, rows)
    total = total.reshape(local_heads, rows)
    summed = summed.reshape(local_heads, rows, HD)

    share = local_heads // lax.axis_size("tok")
    peak, total, summed = jax.tree.map(
        lambda a: a.reshape((-1, share) + a.shape[1:]), (peak, total, summed)
    )

    def pack(part):
        top, tot, acc = part
        blank = jnp.zeros(top.shape[:-1] + (HD - 2 * rows,), jnp.float32)
        extra = jnp.concatenate([top, tot, blank], axis=-1).reshape(-1, HD)
        return jnp.concatenate([acc.reshape(-1, HD), extra])

    def unpack(buffer, like):
        count = like[0].shape[0] * share
        extra = buffer[count * rows :]
        return (
            extra[:, :rows].reshape(like[0].shape),
            extra[:, rows : 2 * rows].reshape(like[0].shape),
            buffer[: count * rows].reshape(like[2].shape),
        )

    state = (peak, total, summed)
    for hop in tok_hops:
        mine = side(*hop)
        pairs = jax.tree.map(lambda a: a.reshape((-1, 2) + a.shape[1:]), state)
        keep = jax.tree.map(lambda a: lax.dynamic_index_in_dim(a, mine, 1, False), pairs)
        send = jax.tree.map(lambda a: lax.dynamic_index_in_dim(a, 1 - mine, 1, False), pairs)
        got = unpack(swap(pack(send), *hop), keep)
        top = jnp.maximum(keep[0], got[0])
        one, two = jnp.exp(keep[0] - top), jnp.exp(got[0] - top)
        state = (
            top,
            keep[1] * one + got[1] * two,
            keep[2] * one[..., None] + got[2] * two[..., None],
        )
    result = state[2][0] / state[1][0][..., None]
    return result.transpose(1, 0, 2).reshape(1, rows, 1, share * HD)


def pair_sides():
    return side("tok", 1), side("tok", 2), lax.axis_index("lay"), lax.axis_index("head")


def lanes(index, size=HD):
    return pl.ds(pl.multiple_of(index * size, size), size)


def gram_share(block_ref, scratch_ref, out_ref):
    _, _, lay, head = pair_sides()
    rows, half = out_ref.shape[0], scratch_ref.shape[0]
    scratch_ref[...] = product(block_ref[:, lanes(head, half)], block_ref[...], ((0,), (0,)))
    out_ref[...] = scratch_ref[lanes(lay, rows), :]


def gram_kernel(block_ref, out_ref, scratch_ref):
    gram_share(block_ref, scratch_ref, out_ref)


def start_kernel(keys_ref, block_ref, keep_ref, send_ref, kept_ref, sent_ref):
    mine, _, _, _ = pair_sides()
    for i in range(2):
        at = pl.ds(i * HD, HD)
        kept_ref[:, at] = keys_ref[:, lanes(2 * i + mine)]
        sent_ref[:, at] = keys_ref[:, lanes(2 * i + 1 - mine)]
    send_ref[...] = product(sent_ref[...], block_ref[...], ((0,), (0,)))
    keep_ref[...] = product(kept_ref[...], block_ref[...], ((0,), (0,)))


def mix_kernel(sent, own_ref, other_ref, first_ref, second_ref, out_ref):
    mine, _, _, head = pair_sides()
    coef = first_ref[...] + second_ref[...]
    half = own_ref.shape[0] // 2
    rows = lanes(head ^ int(sent), half)
    for keys_ref, piece in ((own_ref, mine), (other_ref, 1 - mine)):
        out_ref[lanes(piece, half), :] = product(keys_ref[rows, :], coef, ((1,), (0,)))


def streams_kernel(first_ref, second_ref, a_keep, a_send, b_keep, b_send):
    mine, _, lay, _ = pair_sides()
    half = first_ref.shape[0] // 2
    quarter, eighth = half // 2, half // 4

    def rows(piece, at, count):
        here = pl.ds(pl.multiple_of(piece * half + at, count), count)
        return first_ref[here, :] + second_ref[here, :]

    for piece in range(2):
        to = pl.ds(piece * eighth, eighth)
        a_keep[to, :] = rows(piece, lay * eighth, eighth)
        a_send[to, :] = rows(piece, (1 - lay) * eighth, eighth)
    b_keep[...] = rows(mine, quarter, quarter)
    b_send[...] = rows(1 - mine, quarter, quarter)


def summed_streams(keep, send, lower):
    got = swap(send, "head", 1)
    quarter = vmem(keep.shape[0] // 4, keep.shape[1])
    a_keep, a_send, b_keep, b_send = call(streams_kernel, [quarter] * 4, keep, got)
    a = a_keep + swap(a_send, "lay", 1)
    b = b_keep + swap(b_send, "tok", 1)
    a, b = a + swap(a, "tok", 1), b + swap(b, "lay", 1)
    a = after(a, lower)
    stack = jnp.concatenate([a, swap(a, "lay", 1), b, swap(b, "tok", 1)])
    return stack, swap(stack, "head", 1)


def place_block(stack_ref, lower_ref, block_ref):
    mine, _, lay, _ = pair_sides()
    count = stack_ref.shape[0] // 4
    half = count // 2
    block = product(stack_ref[...], lower_ref[...], ((1,), (1,)))
    for i in range(2):
        for piece in range(2):
            to = (piece ^ mine) * 2 * count + (lay ^ i) * half
            at = i * count + piece * half
            block_ref[pl.ds(pl.multiple_of(to, half), half), :] = block[at : at + half]
        at = (2 + i) * count
        block_ref[pl.ds((2 * i + 1) * count, count), :] = block[at : at + count]


def half_projection(far, own_ref, other_ref, block_ref):
    _, _, _, head = pair_sides()
    half = own_ref.shape[0] // 2
    rows = lanes(head ^ int(far), half)
    return product(own_ref[rows, :], block_ref[pl.ds(0, half), :], ((0,), (0,))) + product(
        other_ref[rows, :], block_ref[pl.ds(half, half), :], ((0,), (0,))
    )


def near_kernel(stack_ref, lower_ref, own_ref, other_ref, block_ref, gram_ref, proj_ref, scratch_ref):
    place_block(stack_ref, lower_ref, block_ref)
    gram_share(block_ref, scratch_ref, gram_ref)
    proj_ref[...] = half_projection(False, own_ref, other_ref, block_ref)


def far_kernel(stack_ref, lower_ref, part_ref, block_ref, gram_ref, scratch_ref):
    place_block(stack_ref, lower_ref, block_ref)
    gram_share(block_ref, scratch_ref, gram_ref)
    gram_ref[...] += part_ref[...]


def project_kernel(own_ref, other_ref, block_ref, part_ref, proj_ref):
    proj_ref[...] = part_ref[...] + half_projection(True, own_ref, other_ref, block_ref)


def attend_kernel(
    query_ref,
    near_ref,
    far_ref,
    first_ref,
    second_ref,
    lower_ref,
    own_ref,
    low_ref,
    high_ref,
    length_ref,
    keep_ref,
    send_ref,
    basis_ref,
):
    mine, upper, _, head = pair_sides()
    group = QH // KVH
    tokens = own_ref.shape[0]
    half, width = tokens // 2, length_ref.shape[1]
    for i, block_ref in enumerate((near_ref, far_ref)):
        basis_ref[pl.ds(i * tokens, tokens), :] = product(
            block_ref[...], lower_ref[...], ((1,), (1,))
        )
    coef = product(first_ref[...] + second_ref[...], lower_ref[...], ((1,), (1,)))
    reduced = []
    for which in range(2):
        quer = jnp.concatenate(
            [query_ref[:, lanes((2 * which + mine) * group + i)] for i in range(group)]
        )
        factor = coef[which * HD : (which + 1) * HD]
        reduced.append(product(quer, factor, ((1,), (0,))) / math.sqrt(HD))
    scores = product(basis_ref[...], jnp.concatenate(reduced), ((1,), (1,)))
    at = lax.broadcasted_iota(jnp.int32, (half, width), 0)
    tok = lax.axis_index("tok")
    valid = jnp.concatenate(
        [
            (tok ^ piece) * tokens + (head ^ far) * half + at < length_ref[...]
            for far in range(2)
            for piece in range(2)
        ]
    )
    peak = jnp.max(jnp.where(valid, scores, NEG), axis=0, keepdims=True)
    weight = jnp.where(valid, jnp.exp(scores - peak), 0.0)
    total = jnp.sum(weight, axis=0, keepdims=True)
    lane = width // 2
    for which, there_ref in enumerate((low_ref, high_ref)):
        here = slice(which * lane, (which + 1) * lane)
        parts = []
        for i in range(4):
            rows = lanes(head ^ (i // 2), half)
            if i % 2 == 0:
                value = own_ref[rows, pl.ds(which * HD, HD)]
            else:
                value = there_ref[rows, :]
            parts.append(product(value, weight[i * half : (i + 1) * half, here], ((0,), (0,))))
        acc = parts[0] + parts[1] + parts[2] + parts[3]

        def give(ref):
            ref[pl.ds(0, HD), :] = acc
            ref[pl.ds(HD, 8), :] = jnp.broadcast_to(peak[:, here], (8, lane))
            ref[pl.ds(HD + 8, 8), :] = jnp.broadcast_to(total[:, here], (8, lane))

        pl.when(upper == which)(lambda: give(keep_ref))
        pl.when(upper != which)(lambda: give(send_ref))


def merge_kernel(first_ref, second_ref, out_ref):
    rows = out_ref.shape[1]
    top = jnp.maximum(first_ref[pl.ds(HD, 1), :], second_ref[pl.ds(HD, 1), :])
    one = jnp.exp(first_ref[pl.ds(HD, 1), :] - top)
    two = jnp.exp(second_ref[pl.ds(HD, 1), :] - top)
    total = first_ref[pl.ds(HD + 8, 1), :] * one + second_ref[pl.ds(HD + 8, 1), :] * two
    acc = first_ref[pl.ds(0, HD), :] * one + second_ref[pl.ds(0, HD), :] * two
    result = (acc / total).T
    for i in range(QH // KVH):
        out_ref[0, :, 0, pl.ds(i * HD, HD)] = result[i * rows : (i + 1) * rows, :]


def gathered(share):
    beside = swap(share, "lay", 1)
    return share, beside, swap(share, "head", 1), swap(beside, "head", 1)


def after(x, *others):
    return lax.optimization_barrier((x, *others))[0]


def split_kernel(values_ref, kept_ref, first_ref, second_ref):
    mine, _, _, _ = pair_sides()
    for i, ref in enumerate((first_ref, second_ref)):
        kept_ref[:, pl.ds(i * HD, HD)] = values_ref[:, lanes(2 * i + mine)]
        ref[...] = values_ref[:, lanes(2 * i + 1 - mine)]


def paired_body(keys, values, queries, start_block, lengths):
    _, tokens, width = keys.shape
    keys, values, queries = keys[0], values[0], queries[0]
    rank = start_block.shape[1]
    rows = queries.shape[0]
    half, share = width // 2, rank // 4

    gram = call(
        gram_kernel,
        vmem(share, rank),
        start_block,
        scratch=[(rank // 2, rank)],
        flops=400_000_000,
    )
    keep, send, keys_own, keys_send = call(
        start_kernel,
        [vmem(half, rank)] * 2 + [vmem(tokens, half)] * 2,
        keys,
        after(start_block, gram),
        flops=900_000_000,
    )
    gram = gram + swap(gram, "tok", 1)
    proj = keep + swap(after(send, gram), "tok", 1)
    values_own, *values_send = call(
        split_kernel,
        [vmem(tokens, half)] + [vmem(tokens, HD)] * 2,
        after(values, proj),
    )
    values_other = []
    lower = None
    for step in range(ITERS + 1):
        gram = gram + swap(gram, "tok", 2)
        last = step == ITERS
        if step != 1:
            proj = after(proj, gram)
            if step == 0:
                keys_other = swap(after(keys_send, proj), "tok", 1)
        first, second = proj, swap(proj, "tok", 2)
        if step > 0 and len(values_other) < 2:
            values_other.append(swap(after(values_send[len(values_other)], proj, gram), "tok", 1))
        parts = gathered(gram)
        if step == 0 or last:
            lower = inverse_factor(*parts)
            first = after(first, lower, values_own)
        else:
            halves = inverse_factor_low(*parts)
            first = after(first, halves[0], *values_other)
            lower = inverse_factor_high(*halves)
        if last:
            break
        mix = (keys_own, keys_other, first, second)
        z_send, z_keep = (
            call(functools.partial(mix_kernel, sent), vmem(tokens, rank), *mix, flops=400_000_000)
            for sent in (True, False)
        )
        stack, far = summed_streams(z_keep, z_send, lower)
        near_block, gram, proj = call(
            near_kernel,
            [vmem(tokens, rank), vmem(share, rank), vmem(half, rank)],
            stack,
            lower,
            keys_own,
            keys_other,
            scratch=[(rank // 2, rank)],
            flops=900_000_000,
        )
        far_block, gram = call(
            far_kernel,
            [vmem(tokens, rank), vmem(share, rank)],
            far,
            lower,
            gram,
            scratch=[(rank // 2, rank)],
            flops=600_000_000,
        )
        proj = call(
            project_kernel,
            vmem(half, rank),
            keys_own,
            keys_other,
            far_block,
            proj,
            flops=400_000_000,
        )
    keep, send = call(
        attend_kernel,
        [vmem(HD + 16, HD)] * 2,
        queries,
        near_block,
        far_block,
        first,
        second,
        lower,
        values_own,
        *values_other,
        jnp.tile(lengths, 2 * (QH // KVH))[None, :],
        scratch=[(2 * tokens, rank)],
        flops=3_000_000_000,
    )
    return call(merge_kernel, vmem(1, rows, 1, half * 4), keep, swap(send, "tok", 2))


def solution(mesh):
    paired = (mesh.shape["tok"], mesh.shape["lay"], mesh.shape["head"]) == (4, 2, 2)
    body = paired_body if paired else spread_body
    return jax.shard_map(
        body,
        mesh=mesh,
        in_specs=(
            P("lay", ("groups", "tok"), "head"),
            P("lay", ("groups", "tok"), "head"),
            P("lay", "groups", "head"),
            P(("groups", "tok"), None),
            P("groups"),
        ),
        out_specs=P("lay", "groups", "head", "tok"),
        check_vma=False,
    )
```

```python
import functools
import math

import jax
import jax.numpy as jnp
from jax import lax
from jax.experimental import pallas as pl
from jax.experimental.pallas import tpu as pltpu
from jax.sharding import PartitionSpec as P

KVH = 8
HD = 128
QH = 64
ITERS = 2

NEG = -1e30
HIGHEST = lax.Precision.HIGHEST


def product(left, right, dims):
    return lax.dot_general(
        left, right, (dims, ((), ())), precision=HIGHEST, preferred_element_type=jnp.float32
    )


def diagonal_inverse(tile, step=8):
    size = tile.shape[0]
    rows = lax.broadcasted_iota(jnp.int32, (size, 2 * size), 0)
    cols = lax.broadcasted_iota(jnp.int32, (size, 2 * size), 1)
    state = jnp.concatenate([tile, jnp.zeros_like(tile)], axis=1)
    state = state + jnp.where(cols == rows + size, 1.0, 0.0)
    done = []
    for start in range(0, size, step):
        col = [
            jnp.broadcast_to(state[:, start + i : start + i + 1], state.shape) for i in range(step)
        ]
        row = [state[i : i + 1, :] for i in range(step)]
        state = state[step:]
        for i in range(step):
            pivot = col[i][i : i + 1, :]
            inverse = 1.0 / pivot
            for k in range(i + 1, step):
                ratio = col[i][k : k + 1, :] * inverse
                row[k] = row[k] - ratio * row[i]
                col[k] = col[k] - ratio * col[i]
            if start + step < size:
                state = state - col[i][step:] * (row[i] * inverse)
            done.append(row[i] * lax.rsqrt(pivot))
    return jnp.concatenate(done)[:, size:]


def vmem(*shape):
    return jax.ShapeDtypeStruct(shape, jnp.float32)


def call(kernel, out_shape, *args, scratch=(), flops=0):
    spec = pl.BlockSpec(memory_space=pltpu.VMEM)
    single = not isinstance(out_shape, (tuple, list))
    moved = sum(4 * math.prod(a.shape) for a in (*args, *((out_shape,) if single else out_shape)))
    return pl.pallas_call(
        kernel,
        out_shape=out_shape,
        in_specs=[spec] * len(args),
        out_specs=spec if single else [spec] * len(out_shape),
        scratch_shapes=[pltpu.VMEM(s, jnp.float32) for s in scratch],
        compiler_params=pltpu.CompilerParams(vmem_limit_bytes=40 << 20),
        cost_estimate=pl.CostEstimate(flops=flops, bytes_accessed=moved, transcendentals=0),
    )(*args)


def whole_gram(own_ref, part_refs, gram_ref):
    if not part_refs:
        gram_ref[...] = own_ref[...]
        return
    lay, head = lax.axis_index("lay"), lax.axis_index("head")
    half = own_ref.shape[1]
    rows = own_ref.shape[0] // 3
    for i, ref in enumerate((own_ref, *part_refs)):
        at = (2 * (head ^ (i // 2)) + (lay ^ (i % 2))) * rows
        for block, (down, right) in enumerate(((0, 0), (0, 1), (1, 1))):
            to = pl.ds(pl.multiple_of(down * half + at, rows), rows)
            gram_ref[to, pl.ds(right * half, half)] = ref[pl.ds(block * rows, rows), :]


def factor_kernel(own_ref, *refs):
    *part_refs, out_ref, gram_ref, tile_ref, cross_ref = refs
    whole_gram(own_ref, part_refs, gram_ref)
    half = tile_ref.shape[0]
    low, high = pl.ds(0, half), pl.ds(half, half)

    @pl.loop(0, 2)
    def _(i):
        here = pl.ds(pl.multiple_of(i * half, half), half)
        tile_ref[...] = diagonal_inverse(gram_ref[here, here])
        out_ref[here, here] = tile_ref[...]

        @pl.when(i == 0)
        def _():
            panel = product(tile_ref[...], gram_ref[low, high], ((1,), (0,)))
            gram_ref[high, high] = gram_ref[high, high] - product(panel, panel, ((0,), (0,)))
            cross_ref[...] = product(panel, tile_ref[...], ((0,), (0,)))
            out_ref[low, high] = jnp.zeros((half, half), jnp.float32)

        @pl.when(i == 1)
        def _():
            out_ref[high, low] = -product(tile_ref[...], cross_ref[...], ((1,), (0,)))


def factor_low_kernel(own_ref, *refs):
    *part_refs, tile_ref, cross_ref, left_ref, gram_ref = refs
    whole_gram(own_ref, part_refs, gram_ref)
    half = tile_ref.shape[0]
    low, high = pl.ds(0, half), pl.ds(half, half)
    tile_ref[...] = diagonal_inverse(gram_ref[low, low])
    panel = product(tile_ref[...], gram_ref[low, high], ((1,), (0,)))
    left_ref[...] = gram_ref[high, high] - product(panel, panel, ((0,), (0,)))
    cross_ref[...] = product(panel, tile_ref[...], ((0,), (0,)))


def factor_high_kernel(tile_ref, cross_ref, left_ref, out_ref):
    half = tile_ref.shape[0]
    low, high = pl.ds(0, half), pl.ds(half, half)
    out_ref[low, low] = tile_ref[...]
    out_ref[low, high] = jnp.zeros((half, half), jnp.float32)
    out_ref[high, high] = diagonal_inverse(left_ref[...])
    out_ref[high, low] = -product(out_ref[high, high], cross_ref[...], ((1,), (0,)))


FACTOR_FLOPS = 1_000_000_000


def inverse_factor(*parts):
    rank = parts[0].shape[1] * min(2, len(parts))
    half = rank // 2
    return call(
        factor_kernel,
        vmem(rank, rank),
        *parts,
        scratch=[(rank, rank), (half, half), (half, half)],
        flops=FACTOR_FLOPS,
    )


def inverse_factor_low(*parts):
    rank = parts[0].shape[1] * min(2, len(parts))
    half = rank // 2
    return call(
        factor_low_kernel, [vmem(half, half)] * 3, *parts, scratch=[(rank, rank)], flops=FACTOR_FLOPS
    )


def inverse_factor_high(*halves):
    rank = 2 * halves[0].shape[0]
    return call(factor_high_kernel, vmem(rank, rank), *halves, flops=FACTOR_FLOPS)


def distances(axis):
    size = lax.axis_size(axis)
    return [1 << i for i in range(size.bit_length() - 1)]


def side(axis, distance):
    return lax.axis_index(axis) // distance % 2


def swap(x, axis, distance):
    pairs = [(i, i ^ distance) for i in range(lax.axis_size(axis))]
    return lax.ppermute(x, axis, pairs)


def halve(x, axis, distance):
    half = x.shape[0] // 2
    mine = side(axis, distance)
    keep = lax.dynamic_slice_in_dim(x, mine * half, half, 0)
    send = lax.dynamic_slice_in_dim(x, (1 - mine) * half, half, 0)
    return keep + swap(send, axis, distance)


def double(x, axis, distance):
    other = swap(x, axis, distance)
    first = side(axis, distance) == 0
    return jnp.concatenate([jnp.where(first, x, other), jnp.where(first, other, x)])


def summed_rows(x, hops):
    for hop in hops:
        x = halve(x, *hop)
    for hop in reversed(hops):
        x = double(x, *hop)
    return x


def spread_body(keys, values, queries, start_block, lengths):
    _, tok_dev, kv_dev = keys.shape
    keys, values = keys[0], values[0]
    rank = start_block.shape[1]
    rows = queries.shape[1]
    local_heads = queries.shape[2] // HD
    group = QH // KVH
    kv_local = kv_dev // HD
    tok_hops = [("tok", d) for d in distances("tok")]
    wide_hops = [("head", d) for d in distances("head")] + [("lay", d) for d in distances("lay")]

    def whole_gram(block):
        share = rank
        at = 0
        for axis, distance in reversed(wide_hops):
            share //= 2
            at = at + side(axis, distance) * share
        part = lax.dynamic_slice_in_dim(block, at, share, 1)
        gram = product(part, block, ((0,), (0,)))
        for hop in tok_hops:
            gram = gram + swap(gram, *hop)
        for hop in wide_hops:
            gram = double(gram, *hop)
        return gram

    def project(block):
        return summed_rows(product(keys, block, ((0,), (0,))), tok_hops)

    def mix(coef):
        return summed_rows(product(keys, coef, ((1,), (0,))), wide_hops)

    block = start_block
    for step in range(ITERS):
        lower = inverse_factor(whole_gram(block))
        block = product(mix(project(block)), lower, ((1,), (1,)))
    lower = inverse_factor(whole_gram(block))
    coef = product(project(block), lower, ((1,), (1,)))
    basis = product(block, lower, ((1,), (1,)))

    quer = queries.reshape(rows, kv_local, group, HD)
    factor = coef.reshape(kv_local, HD, rank)
    reduced = jnp.einsum("bgid,gdr->gibr", quer, factor, precision=HIGHEST) / math.sqrt(HD)
    reduced = reduced.reshape(kv_local, group * rows, rank)
    scores = jnp.einsum("tr,gxr->tgx", basis, reduced, precision=HIGHEST)
    position = lax.axis_index("tok") * tok_dev + jnp.arange(tok_dev, dtype=jnp.int32)
    valid = position[:, None] < lengths[None, :]
    valid = jnp.tile(valid, (1, group))[:, None, :]
    peak = jnp.max(jnp.where(valid, scores, NEG), axis=0)
    weight = jnp.where(valid, jnp.exp(scores - peak[None]), 0.0)
    total = jnp.sum(weight, axis=0)
    vals = values.reshape(tok_dev, kv_local, HD)
    summed = jnp.einsum("tgx,tgd->gxd", weight, vals, precision=HIGHEST)
    peak = peak.reshape(local_heads, rows)
    total = total.reshape(local_heads, rows)
    summed = summed.reshape(local_heads, rows, HD)

    share = local_heads // lax.axis_size("tok")
    peak, total, summed = jax.tree.map(
        lambda a: a.reshape((-1, share) + a.shape[1:]), (peak, total, summed)
    )

    def pack(part):
        top, tot, acc = part
        blank = jnp.zeros(top.shape[:-1] + (HD - 2 * rows,), jnp.float32)
        extra = jnp.concatenate([top, tot, blank], axis=-1).reshape(-1, HD)
        return jnp.concatenate([acc.reshape(-1, HD), extra])

    def unpack(buffer, like):
        count = like[0].shape[0] * share
        extra = buffer[count * rows :]
        return (
            extra[:, :rows].reshape(like[0].shape),
            extra[:, rows : 2 * rows].reshape(like[0].shape),
            buffer[: count * rows].reshape(like[2].shape),
        )

    state = (peak, total, summed)
    for hop in tok_hops:
        mine = side(*hop)
        pairs = jax.tree.map(lambda a: a.reshape((-1, 2) + a.shape[1:]), state)
        keep = jax.tree.map(lambda a: lax.dynamic_index_in_dim(a, mine, 1, False), pairs)
        send = jax.tree.map(lambda a: lax.dynamic_index_in_dim(a, 1 - mine, 1, False), pairs)
        got = unpack(swap(pack(send), *hop), keep)
        top = jnp.maximum(keep[0], got[0])
        one, two = jnp.exp(keep[0] - top), jnp.exp(got[0] - top)
        state = (
            top,
            keep[1] * one + got[1] * two,
            keep[2] * one[..., None] + got[2] * two[..., None],
        )
    result = state[2][0] / state[1][0][..., None]
    return result.transpose(1, 0, 2).reshape(1, rows, 1, share * HD)


def pair_sides():
    return side("tok", 1), side("tok", 2), lax.axis_index("lay"), lax.axis_index("head")


def lanes(index, size=HD):
    return pl.ds(pl.multiple_of(index * size, size), size)


def gram_share(block_ref, scratch_ref, out_ref):
    _, _, lay, head = pair_sides()
    half, rows = scratch_ref.shape[1], out_ref.shape[0] // 3
    low, high = pl.ds(0, half), pl.ds(half, half)
    for i, (left, right) in enumerate(((low, low), (low, high), (high, high))):
        at = pl.ds(i * half, half)
        scratch_ref[at, :] = product(block_ref[:, left], block_ref[:, right], ((0,), (0,)))
    for i in range(3):
        at = pl.ds(pl.multiple_of(i * half + (2 * head + lay) * rows, rows), rows)
        out_ref[pl.ds(i * rows, rows), :] = scratch_ref[at, :]


def gram_kernel(block_ref, out_ref, scratch_ref):
    gram_share(block_ref, scratch_ref, out_ref)


def start_kernel(keys_ref, block_ref, keep_ref, send_ref, kept_ref, sent_ref):
    mine, _, _, _ = pair_sides()
    for i in range(2):
        at = pl.ds(i * HD, HD)
        kept_ref[:, at] = keys_ref[:, lanes(2 * i + mine)]
        sent_ref[:, at] = keys_ref[:, lanes(2 * i + 1 - mine)]
    send_ref[...] = product(sent_ref[...], block_ref[...], ((0,), (0,)))
    keep_ref[...] = product(kept_ref[...], block_ref[...], ((0,), (0,)))


def mix_kernel(sent, own_ref, other_ref, first_ref, second_ref, out_ref):
    mine, _, _, head = pair_sides()
    coef = first_ref[...] + second_ref[...]
    half = own_ref.shape[0] // 2
    rows = lanes(head ^ int(sent), half)
    for keys_ref, piece in ((own_ref, mine), (other_ref, 1 - mine)):
        out_ref[lanes(piece, half), :] = product(keys_ref[rows, :], coef, ((1,), (0,)))


def streams_kernel(first_ref, second_ref, a_keep, a_send, b_keep, b_send):
    mine, _, lay, _ = pair_sides()
    half = first_ref.shape[0] // 2
    quarter, eighth = half // 2, half // 4

    def rows(piece, at, count):
        here = pl.ds(pl.multiple_of(piece * half + at, count), count)
        return first_ref[here, :] + second_ref[here, :]

    for piece in range(2):
        to = pl.ds(piece * eighth, eighth)
        a_keep[to, :] = rows(piece, lay * eighth, eighth)
        a_send[to, :] = rows(piece, (1 - lay) * eighth, eighth)
    b_keep[...] = rows(mine, quarter, quarter)
    b_send[...] = rows(1 - mine, quarter, quarter)


def summed_streams(keep, send, lower):
    got = swap(send, "head", 1)
    quarter = vmem(keep.shape[0] // 4, keep.shape[1])
    a_keep, a_send, b_keep, b_send = call(streams_kernel, [quarter] * 4, keep, got)
    a = a_keep + swap(a_send, "lay", 1)
    b = b_keep + swap(b_send, "tok", 1)
    a, b = a + swap(a, "tok", 1), b + swap(b, "lay", 1)
    a = after(a, lower)
    stack = jnp.concatenate([a, swap(a, "lay", 1), b, swap(b, "tok", 1)])
    return stack, swap(stack, "head", 1)


def place_block(stack_ref, lower_ref, block_ref):
    mine, _, lay, _ = pair_sides()
    count = stack_ref.shape[0] // 4
    half = count // 2
    block = product(stack_ref[...], lower_ref[...], ((1,), (1,)))
    for i in range(2):
        for piece in range(2):
            to = (piece ^ mine) * 2 * count + (lay ^ i) * half
            at = i * count + piece * half
            block_ref[pl.ds(pl.multiple_of(to, half), half), :] = block[at : at + half]
        at = (2 + i) * count
        block_ref[pl.ds((2 * i + 1) * count, count), :] = block[at : at + count]


def half_projection(far, own_ref, other_ref, block_ref):
    _, _, _, head = pair_sides()
    half = own_ref.shape[0] // 2
    rows = lanes(head ^ int(far), half)
    return product(own_ref[rows, :], block_ref[pl.ds(0, half), :], ((0,), (0,))) + product(
        other_ref[rows, :], block_ref[pl.ds(half, half), :], ((0,), (0,))
    )


def near_kernel(stack_ref, lower_ref, own_ref, other_ref, block_ref, gram_ref, proj_ref, scratch_ref):
    place_block(stack_ref, lower_ref, block_ref)
    gram_share(block_ref, scratch_ref, gram_ref)
    proj_ref[...] = half_projection(False, own_ref, other_ref, block_ref)


def far_kernel(stack_ref, lower_ref, part_ref, block_ref, gram_ref, scratch_ref):
    place_block(stack_ref, lower_ref, block_ref)
    gram_share(block_ref, scratch_ref, gram_ref)
    gram_ref[...] += part_ref[...]


def project_kernel(own_ref, other_ref, block_ref, part_ref, proj_ref):
    proj_ref[...] = part_ref[...] + half_projection(True, own_ref, other_ref, block_ref)


def attend_kernel(
    query_ref,
    near_ref,
    far_ref,
    first_ref,
    second_ref,
    lower_ref,
    own_ref,
    low_ref,
    high_ref,
    length_ref,
    keep_ref,
    send_ref,
    basis_ref,
):
    mine, upper, _, head = pair_sides()
    group = QH // KVH
    tokens = own_ref.shape[1]
    half, width = tokens // 2, length_ref.shape[1]
    for i, block_ref in enumerate((near_ref, far_ref)):
        basis = product(block_ref[...], lower_ref[...], ((1,), (1,)))
        for piece in range(2):
            to = pl.multiple_of(piece * tokens + (head ^ i) * half, half)
            basis_ref[pl.ds(to, half), :] = basis[piece * half : (piece + 1) * half]
    coef = product(first_ref[...] + second_ref[...], lower_ref[...], ((1,), (1,)))
    reduced = []
    for which in range(2):
        quer = jnp.concatenate(
            [query_ref[:, lanes((2 * which + mine) * group + i)] for i in range(group)]
        )
        factor = coef[which * HD : (which + 1) * HD]
        reduced.append(product(quer, factor, ((1,), (0,))) / math.sqrt(HD))
    scores = product(basis_ref[...], jnp.concatenate(reduced), ((1,), (1,)))
    at = lax.broadcasted_iota(jnp.int32, (tokens, width), 0)
    tok = lax.axis_index("tok")
    valid = jnp.concatenate(
        [(tok ^ piece) * tokens + at < length_ref[...] for piece in range(2)]
    )
    peak = jnp.max(jnp.where(valid, scores, NEG), axis=0, keepdims=True)
    weight = jnp.where(valid, jnp.exp(scores - peak), 0.0)
    total = jnp.sum(weight, axis=0, keepdims=True)
    lane = width // 2
    for which, there_ref in enumerate((low_ref, high_ref)):
        here = slice(which * lane, (which + 1) * lane)
        own = own_ref[pl.ds(which * HD, HD), :]
        acc = product(own, weight[:tokens, here], ((1,), (0,)))
        acc = acc + product(there_ref[...], weight[tokens:, here], ((1,), (0,)))

        def give(ref):
            ref[pl.ds(0, HD), :] = acc
            ref[pl.ds(HD, 8), :] = jnp.broadcast_to(peak[:, here], (8, lane))
            ref[pl.ds(HD + 8, 8), :] = jnp.broadcast_to(total[:, here], (8, lane))

        pl.when(upper == which)(lambda: give(keep_ref))
        pl.when(upper != which)(lambda: give(send_ref))


def merge_kernel(first_ref, second_ref, out_ref):
    rows = out_ref.shape[1]
    top = jnp.maximum(first_ref[pl.ds(HD, 1), :], second_ref[pl.ds(HD, 1), :])
    one = jnp.exp(first_ref[pl.ds(HD, 1), :] - top)
    two = jnp.exp(second_ref[pl.ds(HD, 1), :] - top)
    total = first_ref[pl.ds(HD + 8, 1), :] * one + second_ref[pl.ds(HD + 8, 1), :] * two
    acc = first_ref[pl.ds(0, HD), :] * one + second_ref[pl.ds(0, HD), :] * two
    result = (acc / total).T
    for i in range(QH // KVH):
        out_ref[0, :, 0, pl.ds(i * HD, HD)] = result[i * rows : (i + 1) * rows, :]


def gathered(share):
    beside = swap(share, "lay", 1)
    return share, beside, swap(share, "head", 1), swap(beside, "head", 1)


def after(x, *others):
    return lax.optimization_barrier((x, *others))[0]


def split_kernel(values_ref, kept_ref, first_ref, second_ref):
    mine, _, _, _ = pair_sides()
    for i, ref in enumerate((first_ref, second_ref)):
        kept_ref[pl.ds(i * HD, HD), :] = values_ref[:, lanes(2 * i + mine)].T
        ref[...] = values_ref[:, lanes(2 * i + 1 - mine)].T


def paired_body(keys, values, queries, start_block, lengths):
    _, tokens, width = keys.shape
    keys, values, queries = keys[0], values[0], queries[0]
    rank = start_block.shape[1]
    rows = queries.shape[0]
    half = width // 2
    share = vmem(3 * rank // 8, rank // 2)
    gram_scratch = (3 * rank // 2, rank // 2)

    gram = call(
        gram_kernel,
        share,
        start_block,
        scratch=[gram_scratch],
        flops=400_000_000,
    )
    keep, send, keys_own, keys_send = call(
        start_kernel,
        [vmem(half, rank)] * 2 + [vmem(tokens, half)] * 2,
        keys,
        after(start_block, gram),
        flops=900_000_000,
    )
    gram = gram + swap(gram, "tok", 1)
    proj = keep + swap(after(send, gram), "tok", 1)
    values_own, *values_send = call(
        split_kernel,
        [vmem(half, tokens)] + [vmem(HD, tokens)] * 2,
        after(values, proj),
    )
    values_other = []
    lower = None
    for step in range(ITERS + 1):
        gram = gram + swap(gram, "tok", 2)
        last = step == ITERS
        if step != 1:
            proj = after(proj, gram)
            if step == 0:
                keys_other = swap(after(keys_send, proj), "tok", 1)
        first, second = proj, swap(proj, "tok", 2)
        parts = gathered(gram)
        if step > 0:
            values_other.append(swap(after(values_send[step - 1], proj, parts[1]), "tok", 1))
        if step == 0 or last:
            lower = inverse_factor(*parts)
            first = after(first, lower, values_own)
        else:
            halves = inverse_factor_low(*parts)
            first = after(first, halves[0], *values_other)
            lower = inverse_factor_high(*halves)
        if last:
            break
        mix = (keys_own, keys_other, first, second)
        z_send, z_keep = (
            call(functools.partial(mix_kernel, sent), vmem(tokens, rank), *mix, flops=400_000_000)
            for sent in (True, False)
        )
        stack, far = summed_streams(z_keep, z_send, lower)
        near_block, gram, proj = call(
            near_kernel,
            [vmem(tokens, rank), share, vmem(half, rank)],
            stack,
            lower,
            keys_own,
            keys_other,
            scratch=[gram_scratch],
            flops=900_000_000,
        )
        far_block, gram = call(
            far_kernel,
            [vmem(tokens, rank), share],
            far,
            lower,
            gram,
            scratch=[gram_scratch],
            flops=600_000_000,
        )
        proj = call(
            project_kernel,
            vmem(half, rank),
            keys_own,
            keys_other,
            far_block,
            proj,
            flops=400_000_000,
        )
    keep, send = call(
        attend_kernel,
        [vmem(HD + 16, HD)] * 2,
        queries,
        near_block,
        far_block,
        first,
        second,
        lower,
        values_own,
        *values_other,
        jnp.tile(lengths, 2 * (QH // KVH))[None, :],
        scratch=[(2 * tokens, rank)],
        flops=3_000_000_000,
    )
    return call(merge_kernel, vmem(1, rows, 1, half * 4), keep, swap(send, "tok", 2))


def solution(mesh):
    paired = (mesh.shape["tok"], mesh.shape["lay"], mesh.shape["head"]) == (4, 2, 2)
    body = paired_body if paired else spread_body
    return jax.shard_map(
        body,
        mesh=mesh,
        in_specs=(
            P("lay", ("groups", "tok"), "head"),
            P("lay", ("groups", "tok"), "head"),
            P("lay", "groups", "head"),
            P(("groups", "tok"), None),
            P("groups"),
        ),
        out_specs=P("lay", "groups", "head", "tok"),
        check_vma=False,
    )
```

```python
import functools
import math

import jax
import jax.numpy as jnp
from jax import lax
from jax.experimental import pallas as pl
from jax.experimental.pallas import tpu as pltpu
from jax.sharding import PartitionSpec as P

KVH = 8
HD = 128
QH = 64
ITERS = 2

NEG = -1e30
HIGHEST = lax.Precision.HIGHEST


def product(left, right, dims):
    return lax.dot_general(
        left, right, (dims, ((), ())), precision=HIGHEST, preferred_element_type=jnp.float32
    )


def diagonal_inverse(tile, step=8):
    size = tile.shape[0]
    rows = lax.broadcasted_iota(jnp.int32, (size, 2 * size), 0)
    cols = lax.broadcasted_iota(jnp.int32, (size, 2 * size), 1)
    state = jnp.concatenate([tile, jnp.zeros_like(tile)], axis=1)
    state = state + jnp.where(cols == rows + size, 1.0, 0.0)
    done = []
    for start in range(0, size, step):
        col = [
            jnp.broadcast_to(state[:, start + i : start + i + 1], state.shape) for i in range(step)
        ]
        row = [state[i : i + 1, :] for i in range(step)]
        state = state[step:]
        for i in range(step):
            pivot = col[i][i : i + 1, :]
            inverse = 1.0 / pivot
            for k in range(i + 1, step):
                ratio = col[i][k : k + 1, :] * inverse
                row[k] = row[k] - ratio * row[i]
                col[k] = col[k] - ratio * col[i]
            if start + step < size:
                state = state - col[i][step:] * (row[i] * inverse)
            done.append(row[i] * lax.rsqrt(pivot))
    return jnp.concatenate(done)[:, size:]


def vmem(*shape):
    return jax.ShapeDtypeStruct(shape, jnp.float32)


def call(kernel, out_shape, *args, scratch=(), flops=0):
    spec = pl.BlockSpec(memory_space=pltpu.VMEM)
    single = not isinstance(out_shape, (tuple, list))
    moved = sum(4 * math.prod(a.shape) for a in (*args, *((out_shape,) if single else out_shape)))
    return pl.pallas_call(
        kernel,
        out_shape=out_shape,
        in_specs=[spec] * len(args),
        out_specs=spec if single else [spec] * len(out_shape),
        scratch_shapes=[pltpu.VMEM(s, jnp.float32) for s in scratch],
        compiler_params=pltpu.CompilerParams(vmem_limit_bytes=40 << 20),
        cost_estimate=pl.CostEstimate(flops=flops, bytes_accessed=moved, transcendentals=0),
    )(*args)


def whole_gram(own_ref, part_refs, gram_ref):
    if not part_refs:
        gram_ref[...] = own_ref[...]
        return
    lay, head = lax.axis_index("lay"), lax.axis_index("head")
    rows = own_ref.shape[0]
    for i, ref in enumerate((own_ref, *part_refs)):
        at = (2 * (head ^ (i // 2)) + (lay ^ (i % 2))) * rows
        gram_ref[pl.ds(pl.multiple_of(at, rows), rows), :] = ref[...]


def factor_kernel(own_ref, *refs):
    *part_refs, out_ref, gram_ref, tile_ref, cross_ref = refs
    whole_gram(own_ref, part_refs, gram_ref)
    half = tile_ref.shape[0]
    low, high = pl.ds(0, half), pl.ds(half, half)

    @pl.loop(0, 2)
    def _(i):
        here = pl.ds(pl.multiple_of(i * half, half), half)
        tile_ref[...] = diagonal_inverse(gram_ref[here, here])
        out_ref[here, here] = tile_ref[...]

        @pl.when(i == 0)
        def _():
            panel = product(tile_ref[...], gram_ref[low, high], ((1,), (0,)))
            gram_ref[high, high] = gram_ref[high, high] - product(panel, panel, ((0,), (0,)))
            cross_ref[...] = product(panel, tile_ref[...], ((0,), (0,)))
            out_ref[low, high] = jnp.zeros((half, half), jnp.float32)

        @pl.when(i == 1)
        def _():
            out_ref[high, low] = -product(tile_ref[...], cross_ref[...], ((1,), (0,)))


def factor_low_kernel(own_ref, *refs):
    *part_refs, tile_ref, cross_ref, left_ref, gram_ref = refs
    whole_gram(own_ref, part_refs, gram_ref)
    half = tile_ref.shape[0]
    low, high = pl.ds(0, half), pl.ds(half, half)
    tile_ref[...] = diagonal_inverse(gram_ref[low, low])
    panel = product(tile_ref[...], gram_ref[low, high], ((1,), (0,)))
    left_ref[...] = gram_ref[high, high] - product(panel, panel, ((0,), (0,)))
    cross_ref[...] = product(panel, tile_ref[...], ((0,), (0,)))


def factor_high_kernel(tile_ref, cross_ref, left_ref, out_ref):
    half = tile_ref.shape[0]
    low, high = pl.ds(0, half), pl.ds(half, half)
    out_ref[low, low] = tile_ref[...]
    out_ref[low, high] = jnp.zeros((half, half), jnp.float32)
    out_ref[high, high] = diagonal_inverse(left_ref[...])
    out_ref[high, low] = -product(out_ref[high, high], cross_ref[...], ((1,), (0,)))


FACTOR_FLOPS = 1_000_000_000


def inverse_factor(*parts):
    rank = parts[0].shape[1]
    half = rank // 2
    return call(
        factor_kernel,
        vmem(rank, rank),
        *parts,
        scratch=[(rank, rank), (half, half), (half, half)],
        flops=FACTOR_FLOPS,
    )


def inverse_factor_low(*parts):
    rank = parts[0].shape[1]
    half = rank // 2
    return call(
        factor_low_kernel, [vmem(half, half)] * 3, *parts, scratch=[(rank, rank)], flops=FACTOR_FLOPS
    )


def inverse_factor_high(*halves):
    rank = 2 * halves[0].shape[0]
    return call(factor_high_kernel, vmem(rank, rank), *halves, flops=FACTOR_FLOPS)


def distances(axis):
    size = lax.axis_size(axis)
    return [1 << i for i in range(size.bit_length() - 1)]


def side(axis, distance):
    return lax.axis_index(axis) // distance % 2


def swap(x, axis, distance):
    pairs = [(i, i ^ distance) for i in range(lax.axis_size(axis))]
    return lax.ppermute(x, axis, pairs)


def halve(x, axis, distance):
    half = x.shape[0] // 2
    mine = side(axis, distance)
    keep = lax.dynamic_slice_in_dim(x, mine * half, half, 0)
    send = lax.dynamic_slice_in_dim(x, (1 - mine) * half, half, 0)
    return keep + swap(send, axis, distance)


def double(x, axis, distance):
    other = swap(x, axis, distance)
    first = side(axis, distance) == 0
    return jnp.concatenate([jnp.where(first, x, other), jnp.where(first, other, x)])


def summed_rows(x, hops):
    for hop in hops:
        x = halve(x, *hop)
    for hop in reversed(hops):
        x = double(x, *hop)
    return x


def spread_body(keys, values, queries, start_block, lengths):
    _, tok_dev, kv_dev = keys.shape
    keys, values = keys[0], values[0]
    rank = start_block.shape[1]
    rows = queries.shape[1]
    local_heads = queries.shape[2] // HD
    group = QH // KVH
    kv_local = kv_dev // HD
    tok_hops = [("tok", d) for d in distances("tok")]
    wide_hops = [("head", d) for d in distances("head")] + [("lay", d) for d in distances("lay")]

    def whole_gram(block):
        share = rank
        at = 0
        for axis, distance in reversed(wide_hops):
            share //= 2
            at = at + side(axis, distance) * share
        part = lax.dynamic_slice_in_dim(block, at, share, 1)
        gram = product(part, block, ((0,), (0,)))
        for hop in tok_hops:
            gram = gram + swap(gram, *hop)
        for hop in wide_hops:
            gram = double(gram, *hop)
        return gram

    def project(block):
        return summed_rows(product(keys, block, ((0,), (0,))), tok_hops)

    def mix(coef):
        return summed_rows(product(keys, coef, ((1,), (0,))), wide_hops)

    block = start_block
    for step in range(ITERS):
        lower = inverse_factor(whole_gram(block))
        block = product(mix(project(block)), lower, ((1,), (1,)))
    lower = inverse_factor(whole_gram(block))
    coef = product(project(block), lower, ((1,), (1,)))
    basis = product(block, lower, ((1,), (1,)))

    quer = queries.reshape(rows, kv_local, group, HD)
    factor = coef.reshape(kv_local, HD, rank)
    reduced = jnp.einsum("bgid,gdr->gibr", quer, factor, precision=HIGHEST) / math.sqrt(HD)
    reduced = reduced.reshape(kv_local, group * rows, rank)
    scores = jnp.einsum("tr,gxr->tgx", basis, reduced, precision=HIGHEST)
    position = lax.axis_index("tok") * tok_dev + jnp.arange(tok_dev, dtype=jnp.int32)
    valid = position[:, None] < lengths[None, :]
    valid = jnp.tile(valid, (1, group))[:, None, :]
    peak = jnp.max(jnp.where(valid, scores, NEG), axis=0)
    weight = jnp.where(valid, jnp.exp(scores - peak[None]), 0.0)
    total = jnp.sum(weight, axis=0)
    vals = values.reshape(tok_dev, kv_local, HD)
    summed = jnp.einsum("tgx,tgd->gxd", weight, vals, precision=HIGHEST)
    peak = peak.reshape(local_heads, rows)
    total = total.reshape(local_heads, rows)
    summed = summed.reshape(local_heads, rows, HD)

    share = local_heads // lax.axis_size("tok")
    peak, total, summed = jax.tree.map(
        lambda a: a.reshape((-1, share) + a.shape[1:]), (peak, total, summed)
    )

    def pack(part):
        top, tot, acc = part
        blank = jnp.zeros(top.shape[:-1] + (HD - 2 * rows,), jnp.float32)
        extra = jnp.concatenate([top, tot, blank], axis=-1).reshape(-1, HD)
        return jnp.concatenate([acc.reshape(-1, HD), extra])

    def unpack(buffer, like):
        count = like[0].shape[0] * share
        extra = buffer[count * rows :]
        return (
            extra[:, :rows].reshape(like[0].shape),
            extra[:, rows : 2 * rows].reshape(like[0].shape),
            buffer[: count * rows].reshape(like[2].shape),
        )

    state = (peak, total, summed)
    for hop in tok_hops:
        mine = side(*hop)
        pairs = jax.tree.map(lambda a: a.reshape((-1, 2) + a.shape[1:]), state)
        keep = jax.tree.map(lambda a: lax.dynamic_index_in_dim(a, mine, 1, False), pairs)
        send = jax.tree.map(lambda a: lax.dynamic_index_in_dim(a, 1 - mine, 1, False), pairs)
        got = unpack(swap(pack(send), *hop), keep)
        top = jnp.maximum(keep[0], got[0])
        one, two = jnp.exp(keep[0] - top), jnp.exp(got[0] - top)
        state = (
            top,
            keep[1] * one + got[1] * two,
            keep[2] * one[..., None] + got[2] * two[..., None],
        )
    result = state[2][0] / state[1][0][..., None]
    return result.transpose(1, 0, 2).reshape(1, rows, 1, share * HD)


def pair_sides():
    return side("tok", 1), side("tok", 2), lax.axis_index("lay"), lax.axis_index("head")


def lanes(index, size=HD):
    return pl.ds(pl.multiple_of(index * size, size), size)


def gram_share(block_ref, scratch_ref, out_ref):
    _, _, lay, head = pair_sides()
    rows, half = out_ref.shape[0], scratch_ref.shape[0]
    scratch_ref[...] = product(block_ref[:, lanes(head, half)], block_ref[...], ((0,), (0,)))
    out_ref[...] = scratch_ref[lanes(lay, rows), :]


def gram_kernel(block_ref, out_ref, scratch_ref):
    gram_share(block_ref, scratch_ref, out_ref)


def start_kernel(keys_ref, block_ref, gram_ref, keep_ref, send_ref, kept_ref, sent_ref):
    del gram_ref
    mine, _, _, _ = pair_sides()
    for i in range(2):
        at = pl.ds(i * HD, HD)
        kept_ref[:, at] = keys_ref[:, lanes(2 * i + mine)]
        sent_ref[:, at] = keys_ref[:, lanes(2 * i + 1 - mine)]
    send_ref[...] = product(sent_ref[...], block_ref[...], ((0,), (0,)))
    keep_ref[...] = product(kept_ref[...], block_ref[...], ((0,), (0,)))


def mix_kernel(sent, own_ref, other_ref, first_ref, second_ref, out_ref):
    mine, _, _, head = pair_sides()
    coef = first_ref[...] + second_ref[...]
    half = own_ref.shape[0] // 2
    rows = lanes(head ^ int(sent), half)
    for keys_ref, piece in ((own_ref, mine), (other_ref, 1 - mine)):
        out_ref[lanes(piece, half), :] = product(keys_ref[rows, :], coef, ((1,), (0,)))


def streams_kernel(first_ref, second_ref, a_keep, a_send, b_keep, b_send):
    mine, _, lay, _ = pair_sides()
    half = first_ref.shape[0] // 2
    quarter, eighth = half // 2, half // 4

    def rows(piece, at, count):
        here = pl.ds(pl.multiple_of(piece * half + at, count), count)
        return first_ref[here, :] + second_ref[here, :]

    for piece in range(2):
        to = pl.ds(piece * eighth, eighth)
        a_keep[to, :] = rows(piece, lay * eighth, eighth)
        a_send[to, :] = rows(piece, (1 - lay) * eighth, eighth)
    b_keep[...] = rows(mine, quarter, quarter)
    b_send[...] = rows(1 - mine, quarter, quarter)


def summed_streams(keep, send, lower):
    got = swap(send, "head", 1)
    quarter = vmem(keep.shape[0] // 4, keep.shape[1])
    a_keep, a_send, b_keep, b_send = call(streams_kernel, [quarter] * 4, keep, got)
    a = a_keep + swap(a_send, "lay", 1)
    b = b_keep + swap(b_send, "tok", 1)
    a, b = a + swap(a, "tok", 1), b + swap(b, "lay", 1)
    a = after(a, lower)
    stack = jnp.concatenate([a, swap(a, "lay", 1), b, swap(b, "tok", 1)])
    return stack, swap(stack, "head", 1)


def place_block(stack_ref, lower_ref, block_ref):
    mine, _, lay, _ = pair_sides()
    count = stack_ref.shape[0] // 4
    half = count // 2
    block = product(stack_ref[...], lower_ref[...], ((1,), (1,)))
    for i in range(2):
        for piece in range(2):
            to = (piece ^ mine) * 2 * count + (lay ^ i) * half
            at = i * count + piece * half
            block_ref[pl.ds(pl.multiple_of(to, half), half), :] = block[at : at + half]
        at = (2 + i) * count
        block_ref[pl.ds((2 * i + 1) * count, count), :] = block[at : at + count]


def half_projection(far, own_ref, other_ref, block_ref):
    _, _, _, head = pair_sides()
    half = own_ref.shape[0] // 2
    rows = lanes(head ^ int(far), half)
    return product(own_ref[rows, :], block_ref[pl.ds(0, half), :], ((0,), (0,))) + product(
        other_ref[rows, :], block_ref[pl.ds(half, half), :], ((0,), (0,))
    )


def near_kernel(stack_ref, lower_ref, own_ref, other_ref, block_ref, gram_ref, proj_ref, scratch_ref):
    place_block(stack_ref, lower_ref, block_ref)
    gram_share(block_ref, scratch_ref, gram_ref)
    proj_ref[...] = half_projection(False, own_ref, other_ref, block_ref)


def far_kernel(stack_ref, lower_ref, part_ref, block_ref, gram_ref, scratch_ref):
    place_block(stack_ref, lower_ref, block_ref)
    gram_share(block_ref, scratch_ref, gram_ref)
    gram_ref[...] += part_ref[...]


def project_kernel(own_ref, other_ref, block_ref, part_ref, proj_ref):
    proj_ref[...] = part_ref[...] + half_projection(True, own_ref, other_ref, block_ref)


def attend_kernel(
    query_ref,
    near_ref,
    far_ref,
    first_ref,
    second_ref,
    lower_ref,
    own_ref,
    low_ref,
    high_ref,
    length_ref,
    keep_ref,
    send_ref,
    score_ref,
):
    mine, upper, _, head = pair_sides()
    group = QH // KVH
    tokens = own_ref.shape[1]
    half, width = tokens // 2, length_ref.shape[1]
    coef = product(first_ref[...] + second_ref[...], lower_ref[...], ((1,), (1,)))
    reduced = []
    for which in range(2):
        quer = jnp.concatenate(
            [query_ref[:, lanes((2 * which + mine) * group + i)] for i in range(group)]
        )
        factor = coef[which * HD : (which + 1) * HD]
        reduced.append(product(quer, factor, ((1,), (0,))) / math.sqrt(HD))
    reduced = product(jnp.concatenate(reduced), lower_ref[...], ((1,), (0,)))
    for i, block_ref in enumerate((near_ref, far_ref)):
        part = product(block_ref[...], reduced, ((1,), (1,)))
        for piece in range(2):
            to = pl.multiple_of(piece * tokens + (head ^ i) * half, half)
            score_ref[pl.ds(to, half), :] = part[piece * half : (piece + 1) * half]
    scores = score_ref[...]
    at = lax.broadcasted_iota(jnp.int32, (tokens, width), 0)
    tok = lax.axis_index("tok")
    valid = jnp.concatenate(
        [(tok ^ piece) * tokens + at < length_ref[...] for piece in range(2)]
    )
    peak = jnp.max(jnp.where(valid, scores, NEG), axis=0, keepdims=True)
    weight = jnp.where(valid, jnp.exp(scores - peak), 0.0)
    total = jnp.sum(weight, axis=0, keepdims=True)
    lane = width // 2
    for which, there_ref in enumerate((low_ref, high_ref)):
        here = slice(which * lane, (which + 1) * lane)
        own = own_ref[pl.ds(which * HD, HD), :]
        acc = product(own, weight[:tokens, here], ((1,), (0,)))
        acc = acc + product(there_ref[...], weight[tokens:, here], ((1,), (0,)))

        def give(ref):
            ref[pl.ds(0, HD), :] = acc
            ref[pl.ds(HD, 8), :] = jnp.broadcast_to(peak[:, here], (8, lane))
            ref[pl.ds(HD + 8, 8), :] = jnp.broadcast_to(total[:, here], (8, lane))

        pl.when(upper == which)(lambda: give(keep_ref))
        pl.when(upper != which)(lambda: give(send_ref))


def merge_kernel(first_ref, second_ref, out_ref):
    rows = out_ref.shape[1]
    top = jnp.maximum(first_ref[pl.ds(HD, 1), :], second_ref[pl.ds(HD, 1), :])
    one = jnp.exp(first_ref[pl.ds(HD, 1), :] - top)
    two = jnp.exp(second_ref[pl.ds(HD, 1), :] - top)
    total = first_ref[pl.ds(HD + 8, 1), :] * one + second_ref[pl.ds(HD + 8, 1), :] * two
    acc = first_ref[pl.ds(0, HD), :] * one + second_ref[pl.ds(0, HD), :] * two
    result = (acc / total).T
    for i in range(QH // KVH):
        out_ref[0, :, 0, pl.ds(i * HD, HD)] = result[i * rows : (i + 1) * rows, :]


def gathered(share):
    beside = swap(share, "lay", 1)
    return share, beside, swap(share, "head", 1), swap(beside, "head", 1)


def after(x, *others):
    return lax.optimization_barrier((x, *others))[0]


def split_kernel(values_ref, kept_ref, first_ref, second_ref):
    mine, _, _, _ = pair_sides()
    for i, ref in enumerate((first_ref, second_ref)):
        kept_ref[pl.ds(i * HD, HD), :] = values_ref[:, lanes(2 * i + mine)].T
        ref[...] = values_ref[:, lanes(2 * i + 1 - mine)].T


def paired_body(keys, values, queries, start_block, lengths):
    _, tokens, width = keys.shape
    keys, values, queries = keys[0], values[0], queries[0]
    rank = start_block.shape[1]
    rows = queries.shape[0]
    half, share = width // 2, rank // 4

    gram = call(
        gram_kernel,
        vmem(share, rank),
        start_block,
        scratch=[(rank // 2, rank)],
        flops=400_000_000,
    )
    keep, send, keys_own, keys_send = call(
        start_kernel,
        [vmem(half, rank)] * 2 + [vmem(tokens, half)] * 2,
        keys,
        start_block,
        gram,
        flops=900_000_000,
    )
    gram = gram + swap(gram, "tok", 1)
    proj = keep + swap(after(send, gram), "tok", 1)
    values_own, *values_send = call(
        split_kernel,
        [vmem(half, tokens)] + [vmem(HD, tokens)] * 2,
        after(values, proj),
    )
    values_other = []
    lower = None
    for step in range(ITERS + 1):
        gram = gram + swap(gram, "tok", 2)
        last = step == ITERS
        if step != 1:
            proj = after(proj, gram)
            if step == 0:
                keys_other = swap(after(keys_send, proj), "tok", 1)
        first, second = proj, swap(proj, "tok", 2)
        if step > 0 and len(values_other) < 2:
            values_other.append(swap(after(values_send[len(values_other)], proj, gram), "tok", 1))
        parts = gathered(gram)
        if step == 0 or last:
            lower = inverse_factor(*parts)
            first = after(first, lower, values_own)
        else:
            halves = inverse_factor_low(*parts)
            first = after(first, halves[0], *values_other)
            lower = inverse_factor_high(*halves)
        if last:
            break
        mix = (keys_own, keys_other, first, second)
        z_send, z_keep = (
            call(functools.partial(mix_kernel, sent), vmem(tokens, rank), *mix, flops=400_000_000)
            for sent in (True, False)
        )
        stack, far = summed_streams(z_keep, z_send, lower)
        near_block, gram, proj = call(
            near_kernel,
            [vmem(tokens, rank), vmem(share, rank), vmem(half, rank)],
            stack,
            lower,
            keys_own,
            keys_other,
            scratch=[(rank // 2, rank)],
            flops=900_000_000,
        )
        far_block, gram = call(
            far_kernel,
            [vmem(tokens, rank), vmem(share, rank)],
            far,
            lower,
            gram,
            scratch=[(rank // 2, rank)],
            flops=600_000_000,
        )
        proj = call(
            project_kernel,
            vmem(half, rank),
            keys_own,
            keys_other,
            far_block,
            proj,
            flops=400_000_000,
        )
    keep, send = call(
        attend_kernel,
        [vmem(HD + 16, HD)] * 2,
        queries,
        near_block,
        far_block,
        first,
        second,
        lower,
        values_own,
        *values_other,
        jnp.tile(lengths, 2 * (QH // KVH))[None, :],
        scratch=[(2 * tokens, 2 * (QH // KVH) * rows)],
        flops=3_000_000_000,
    )
    return call(merge_kernel, vmem(1, rows, 1, half * 4), keep, swap(send, "tok", 2))


def solution(mesh):
    paired = (mesh.shape["tok"], mesh.shape["lay"], mesh.shape["head"]) == (4, 2, 2)
    body = paired_body if paired else spread_body
    return jax.shard_map(
        body,
        mesh=mesh,
        in_specs=(
            P("lay", ("groups", "tok"), "head"),
            P("lay", ("groups", "tok"), "head"),
            P("lay", "groups", "head"),
            P(("groups", "tok"), None),
            P("groups"),
        ),
        out_specs=P("lay", "groups", "head", "tok"),
        check_vma=False,
    )
```

```python
import functools
import math

import jax
import jax.numpy as jnp
from jax import lax
from jax.experimental import pallas as pl
from jax.experimental.pallas import tpu as pltpu
from jax.sharding import PartitionSpec as P

KVH = 8
HD = 128
QH = 64
ITERS = 2

NEG = -1e30
HIGHEST = lax.Precision.HIGHEST


def product(left, right, dims):
    return lax.dot_general(
        left, right, (dims, ((), ())), precision=HIGHEST, preferred_element_type=jnp.float32
    )


def diagonal_inverse(tile, step=8):
    size = tile.shape[0]
    rows = lax.broadcasted_iota(jnp.int32, (size, 2 * size), 0)
    cols = lax.broadcasted_iota(jnp.int32, (size, 2 * size), 1)
    state = jnp.concatenate([tile, jnp.zeros_like(tile)], axis=1)
    state = state + jnp.where(cols == rows + size, 1.0, 0.0)
    done = []
    for start in range(0, size, step):
        col = [
            jnp.broadcast_to(state[:, start + i : start + i + 1], state.shape) for i in range(step)
        ]
        row = [state[i : i + 1, :] for i in range(step)]
        state = state[step:]
        for i in range(step):
            pivot = col[i][i : i + 1, :]
            inverse = 1.0 / pivot
            for k in range(i + 1, step):
                ratio = col[i][k : k + 1, :] * inverse
                row[k] = row[k] - ratio * row[i]
                col[k] = col[k] - ratio * col[i]
            if start + step < size:
                state = state - col[i][step:] * (row[i] * inverse)
            done.append(row[i] * lax.rsqrt(pivot))
    return jnp.concatenate(done)[:, size:]


def vmem(*shape):
    return jax.ShapeDtypeStruct(shape, jnp.float32)


def call(kernel, out_shape, *args, scratch=(), flops=0):
    spec = pl.BlockSpec(memory_space=pltpu.VMEM)
    single = not isinstance(out_shape, (tuple, list))
    moved = sum(4 * math.prod(a.shape) for a in (*args, *((out_shape,) if single else out_shape)))
    return pl.pallas_call(
        kernel,
        out_shape=out_shape,
        in_specs=[spec] * len(args),
        out_specs=spec if single else [spec] * len(out_shape),
        scratch_shapes=[pltpu.VMEM(s, jnp.float32) for s in scratch],
        compiler_params=pltpu.CompilerParams(vmem_limit_bytes=40 << 20),
        cost_estimate=pl.CostEstimate(flops=flops, bytes_accessed=moved, transcendentals=0),
    )(*args)


def whole_gram(own_ref, part_refs, gram_ref):
    if not part_refs:
        gram_ref[...] = own_ref[...]
        return
    lay, head = lax.axis_index("lay"), lax.axis_index("head")
    rows = own_ref.shape[0]
    for i, ref in enumerate((own_ref, *part_refs)):
        at = (2 * (head ^ (i // 2)) + (lay ^ (i % 2))) * rows
        gram_ref[pl.ds(pl.multiple_of(at, rows), rows), :] = ref[...]


def factor_kernel(own_ref, *refs):
    *part_refs, out_ref, gram_ref, tile_ref, cross_ref = refs
    whole_gram(own_ref, part_refs, gram_ref)
    half = tile_ref.shape[0]
    low, high = pl.ds(0, half), pl.ds(half, half)

    @pl.loop(0, 2)
    def _(i):
        here = pl.ds(pl.multiple_of(i * half, half), half)
        tile_ref[...] = diagonal_inverse(gram_ref[here, here])
        out_ref[here, here] = tile_ref[...]

        @pl.when(i == 0)
        def _():
            panel = product(tile_ref[...], gram_ref[low, high], ((1,), (0,)))
            gram_ref[high, high] = gram_ref[high, high] - product(panel, panel, ((0,), (0,)))
            cross_ref[...] = product(panel, tile_ref[...], ((0,), (0,)))
            out_ref[low, high] = jnp.zeros((half, half), jnp.float32)

        @pl.when(i == 1)
        def _():
            out_ref[high, low] = -product(tile_ref[...], cross_ref[...], ((1,), (0,)))


def factor_low_kernel(own_ref, *refs):
    *part_refs, tile_ref, cross_ref, left_ref, gram_ref = refs
    whole_gram(own_ref, part_refs, gram_ref)
    half = tile_ref.shape[0]
    low, high = pl.ds(0, half), pl.ds(half, half)
    tile_ref[...] = diagonal_inverse(gram_ref[low, low])
    panel = product(tile_ref[...], gram_ref[low, high], ((1,), (0,)))
    left_ref[...] = gram_ref[high, high] - product(panel, panel, ((0,), (0,)))
    cross_ref[...] = product(panel, tile_ref[...], ((0,), (0,)))


def factor_high_kernel(tile_ref, cross_ref, left_ref, out_ref):
    half = tile_ref.shape[0]
    low, high = pl.ds(0, half), pl.ds(half, half)
    out_ref[low, low] = tile_ref[...]
    out_ref[low, high] = jnp.zeros((half, half), jnp.float32)
    out_ref[high, high] = diagonal_inverse(left_ref[...])
    out_ref[high, low] = -product(out_ref[high, high], cross_ref[...], ((1,), (0,)))


FACTOR_FLOPS = 1_000_000_000


def inverse_factor(*parts):
    rank = parts[0].shape[1]
    half = rank // 2
    return call(
        factor_kernel,
        vmem(rank, rank),
        *parts,
        scratch=[(rank, rank), (half, half), (half, half)],
        flops=FACTOR_FLOPS,
    )


def inverse_factor_low(*parts):
    rank = parts[0].shape[1]
    half = rank // 2
    return call(
        factor_low_kernel, [vmem(half, half)] * 3, *parts, scratch=[(rank, rank)], flops=FACTOR_FLOPS
    )


def inverse_factor_high(*halves):
    rank = 2 * halves[0].shape[0]
    return call(factor_high_kernel, vmem(rank, rank), *halves, flops=FACTOR_FLOPS)


def distances(axis):
    size = lax.axis_size(axis)
    return [1 << i for i in range(size.bit_length() - 1)]


def side(axis, distance):
    return lax.axis_index(axis) // distance % 2


def swap(x, axis, distance):
    pairs = [(i, i ^ distance) for i in range(lax.axis_size(axis))]
    return lax.ppermute(x, axis, pairs)


def halve(x, axis, distance):
    half = x.shape[0] // 2
    mine = side(axis, distance)
    keep = lax.dynamic_slice_in_dim(x, mine * half, half, 0)
    send = lax.dynamic_slice_in_dim(x, (1 - mine) * half, half, 0)
    return keep + swap(send, axis, distance)


def double(x, axis, distance):
    other = swap(x, axis, distance)
    first = side(axis, distance) == 0
    return jnp.concatenate([jnp.where(first, x, other), jnp.where(first, other, x)])


def summed_rows(x, hops):
    for hop in hops:
        x = halve(x, *hop)
    for hop in reversed(hops):
        x = double(x, *hop)
    return x


def spread_body(keys, values, queries, start_block, lengths):
    _, tok_dev, kv_dev = keys.shape
    keys, values = keys[0], values[0]
    rank = start_block.shape[1]
    rows = queries.shape[1]
    local_heads = queries.shape[2] // HD
    group = QH // KVH
    kv_local = kv_dev // HD
    tok_hops = [("tok", d) for d in distances("tok")]
    wide_hops = [("head", d) for d in distances("head")] + [("lay", d) for d in distances("lay")]

    def whole_gram(block):
        share = rank
        at = 0
        for axis, distance in reversed(wide_hops):
            share //= 2
            at = at + side(axis, distance) * share
        part = lax.dynamic_slice_in_dim(block, at, share, 1)
        gram = product(part, block, ((0,), (0,)))
        for hop in tok_hops:
            gram = gram + swap(gram, *hop)
        for hop in wide_hops:
            gram = double(gram, *hop)
        return gram

    def project(block):
        return summed_rows(product(keys, block, ((0,), (0,))), tok_hops)

    def mix(coef):
        return summed_rows(product(keys, coef, ((1,), (0,))), wide_hops)

    block = start_block
    for step in range(ITERS):
        lower = inverse_factor(whole_gram(block))
        block = product(mix(project(block)), lower, ((1,), (1,)))
    lower = inverse_factor(whole_gram(block))
    coef = product(project(block), lower, ((1,), (1,)))
    basis = product(block, lower, ((1,), (1,)))

    quer = queries.reshape(rows, kv_local, group, HD)
    factor = coef.reshape(kv_local, HD, rank)
    reduced = jnp.einsum("bgid,gdr->gibr", quer, factor, precision=HIGHEST) / math.sqrt(HD)
    reduced = reduced.reshape(kv_local, group * rows, rank)
    scores = jnp.einsum("tr,gxr->tgx", basis, reduced, precision=HIGHEST)
    position = lax.axis_index("tok") * tok_dev + jnp.arange(tok_dev, dtype=jnp.int32)
    valid = position[:, None] < lengths[None, :]
    valid = jnp.tile(valid, (1, group))[:, None, :]
    peak = jnp.max(jnp.where(valid, scores, NEG), axis=0)
    weight = jnp.where(valid, jnp.exp(scores - peak[None]), 0.0)
    total = jnp.sum(weight, axis=0)
    vals = values.reshape(tok_dev, kv_local, HD)
    summed = jnp.einsum("tgx,tgd->gxd", weight, vals, precision=HIGHEST)
    peak = peak.reshape(local_heads, rows)
    total = total.reshape(local_heads, rows)
    summed = summed.reshape(local_heads, rows, HD)

    share = local_heads // lax.axis_size("tok")
    peak, total, summed = jax.tree.map(
        lambda a: a.reshape((-1, share) + a.shape[1:]), (peak, total, summed)
    )

    def pack(part):
        top, tot, acc = part
        blank = jnp.zeros(top.shape[:-1] + (HD - 2 * rows,), jnp.float32)
        extra = jnp.concatenate([top, tot, blank], axis=-1).reshape(-1, HD)
        return jnp.concatenate([acc.reshape(-1, HD), extra])

    def unpack(buffer, like):
        count = like[0].shape[0] * share
        extra = buffer[count * rows :]
        return (
            extra[:, :rows].reshape(like[0].shape),
            extra[:, rows : 2 * rows].reshape(like[0].shape),
            buffer[: count * rows].reshape(like[2].shape),
        )

    state = (peak, total, summed)
    for hop in tok_hops:
        mine = side(*hop)
        pairs = jax.tree.map(lambda a: a.reshape((-1, 2) + a.shape[1:]), state)
        keep = jax.tree.map(lambda a: lax.dynamic_index_in_dim(a, mine, 1, False), pairs)
        send = jax.tree.map(lambda a: lax.dynamic_index_in_dim(a, 1 - mine, 1, False), pairs)
        got = unpack(swap(pack(send), *hop), keep)
        top = jnp.maximum(keep[0], got[0])
        one, two = jnp.exp(keep[0] - top), jnp.exp(got[0] - top)
        state = (
            top,
            keep[1] * one + got[1] * two,
            keep[2] * one[..., None] + got[2] * two[..., None],
        )
    result = state[2][0] / state[1][0][..., None]
    return result.transpose(1, 0, 2).reshape(1, rows, 1, share * HD)


def pair_sides():
    return side("tok", 1), side("tok", 2), lax.axis_index("lay"), lax.axis_index("head")


def lanes(index, size=HD):
    return pl.ds(pl.multiple_of(index * size, size), size)


def gram_share(block_ref, scratch_ref, out_ref):
    _, _, lay, head = pair_sides()
    rows, half = out_ref.shape[0], scratch_ref.shape[0]
    scratch_ref[...] = product(block_ref[:, lanes(head, half)], block_ref[...], ((0,), (0,)))
    out_ref[...] = scratch_ref[lanes(lay, rows), :]


def gram_kernel(block_ref, out_ref, scratch_ref):
    gram_share(block_ref, scratch_ref, out_ref)


def start_kernel(keys_ref, block_ref, gram_ref, keep_ref, send_ref, kept_ref, sent_ref):
    del gram_ref
    mine, _, _, _ = pair_sides()
    for i in range(2):
        at = pl.ds(i * HD, HD)
        kept_ref[:, at] = keys_ref[:, lanes(2 * i + mine)]
        sent_ref[:, at] = keys_ref[:, lanes(2 * i + 1 - mine)]
    send_ref[...] = product(sent_ref[...], block_ref[...], ((0,), (0,)))
    keep_ref[...] = product(kept_ref[...], block_ref[...], ((0,), (0,)))


def mix_kernel(sent, own_ref, other_ref, first_ref, second_ref, out_ref):
    mine, _, _, head = pair_sides()
    coef = first_ref[...] + second_ref[...]
    half = own_ref.shape[0] // 2
    rows = lanes(head ^ int(sent), half)
    for keys_ref, piece in ((own_ref, mine), (other_ref, 1 - mine)):
        out_ref[lanes(piece, half), :] = product(keys_ref[rows, :], coef, ((1,), (0,)))


def streams_kernel(first_ref, second_ref, a_keep, a_send, b_keep, b_send):
    mine, _, lay, _ = pair_sides()
    half = first_ref.shape[0] // 2
    quarter, eighth = half // 2, half // 4

    def rows(piece, at, count):
        here = pl.ds(pl.multiple_of(piece * half + at, count), count)
        return first_ref[here, :] + second_ref[here, :]

    for piece in range(2):
        to = pl.ds(piece * eighth, eighth)
        a_keep[to, :] = rows(piece, lay * eighth, eighth)
        a_send[to, :] = rows(piece, (1 - lay) * eighth, eighth)
    b_keep[...] = rows(mine, quarter, quarter)
    b_send[...] = rows(1 - mine, quarter, quarter)


def summed_streams(keep, send, lower):
    got = swap(send, "head", 1)
    quarter = vmem(keep.shape[0] // 4, keep.shape[1])
    a_keep, a_send, b_keep, b_send = call(streams_kernel, [quarter] * 4, keep, got)
    a = a_keep + swap(a_send, "lay", 1)
    b = b_keep + swap(b_send, "tok", 1)
    a, b = a + swap(a, "tok", 1), b + swap(b, "lay", 1)
    a = after(a, lower)
    here = jnp.concatenate([a, b])
    return here, (swap(a, "lay", 1), swap(b, "tok", 1))


def stack_rows(far, beside, size):
    _, _, lay, head = pair_sides()
    count = size // 2
    first = (head ^ far) * size
    return first + (lay ^ beside) * (count // 2), first + count


def project_stack(far, beside, own_ref, other_ref, block_ref, rows_ref):
    mine, _, _, _ = pair_sides()
    size = block_ref.shape[0]
    half, quarter = size // 2, size // 4
    low, high = stack_rows(far, beside, size)
    low = pl.ds(pl.multiple_of(low, quarter), quarter)
    rows_ref[lanes(mine, quarter), :] = own_ref[low, :]
    rows_ref[lanes(1 - mine, quarter), :] = other_ref[low, :]
    high = pl.ds(pl.multiple_of(high, half), half)
    rows_ref[pl.ds(half, half), :] = (other_ref if beside else own_ref)[high, :]
    return product(rows_ref[...], block_ref[...], ((0,), (0,)))


def stack_kernel(far, beside, stack_ref, lower_ref, own_ref, other_ref, *refs):
    *part_refs, block_ref, gram_ref, proj_ref, rows_ref, scratch_ref = refs
    block_ref[...] = product(stack_ref[...], lower_ref[...], ((1,), (1,)))
    gram_share(block_ref, scratch_ref, gram_ref)
    proj_ref[...] = project_stack(far, beside, own_ref, other_ref, block_ref, rows_ref)
    for part_ref, ref in zip(part_refs, (gram_ref, proj_ref)):
        ref[...] += part_ref[...]


def last_stack_kernel(stack_ref, lower_ref, part_ref, block_ref, gram_ref, scratch_ref):
    block_ref[...] = product(stack_ref[...], lower_ref[...], ((1,), (1,)))
    gram_share(block_ref, scratch_ref, gram_ref)
    gram_ref[...] += part_ref[...]


def project_kernel(own_ref, other_ref, block_ref, part_ref, proj_ref, rows_ref):
    proj_ref[...] = part_ref[...] + project_stack(1, 1, own_ref, other_ref, block_ref, rows_ref)


def attend_kernel(
    query_ref,
    *refs,
):
    *block_refs, first_ref, second_ref, lower_ref, own_ref, low_ref, high_ref, length_ref = refs[:-3]
    keep_ref, send_ref, score_ref = refs[-3:]
    mine, upper, _, _ = pair_sides()
    group = QH // KVH
    tokens = own_ref.shape[1]
    half, width = tokens // 2, length_ref.shape[1]
    coef = product(first_ref[...] + second_ref[...], lower_ref[...], ((1,), (1,)))
    reduced = []
    for which in range(2):
        quer = jnp.concatenate(
            [query_ref[:, lanes((2 * which + mine) * group + i)] for i in range(group)]
        )
        factor = coef[which * HD : (which + 1) * HD]
        reduced.append(product(quer, factor, ((1,), (0,))) / math.sqrt(HD))
    reduced = product(jnp.concatenate(reduced), lower_ref[...], ((1,), (0,)))
    for i, block_ref in enumerate(block_refs):
        far, beside = i % 2, i // 2
        part = product(block_ref[...], reduced, ((1,), (1,)))
        low, high = stack_rows(far, beside, half)
        quarter = half // 4
        for piece in range(2):
            to = pl.multiple_of((piece ^ mine) * tokens + low, quarter)
            score_ref[pl.ds(to, quarter), :] = part[piece * quarter : (piece + 1) * quarter]
        to = pl.multiple_of(beside * tokens + high, half // 2)
        score_ref[pl.ds(to, half // 2), :] = part[half // 2 :]
    scores = score_ref[...]
    at = lax.broadcasted_iota(jnp.int32, (tokens, width), 0)
    tok = lax.axis_index("tok")
    valid = jnp.concatenate(
        [(tok ^ piece) * tokens + at < length_ref[...] for piece in range(2)]
    )
    peak = jnp.max(jnp.where(valid, scores, NEG), axis=0, keepdims=True)
    weight = jnp.where(valid, jnp.exp(scores - peak), 0.0)
    total = jnp.sum(weight, axis=0, keepdims=True)
    lane = width // 2
    for which, there_ref in enumerate((low_ref, high_ref)):
        here = slice(which * lane, (which + 1) * lane)
        own = own_ref[pl.ds(which * HD, HD), :]
        acc = product(own, weight[:tokens, here], ((1,), (0,)))
        acc = acc + product(there_ref[...], weight[tokens:, here], ((1,), (0,)))

        def give(ref):
            ref[pl.ds(0, HD), :] = acc
            ref[pl.ds(HD, 8), :] = jnp.broadcast_to(peak[:, here], (8, lane))
            ref[pl.ds(HD + 8, 8), :] = jnp.broadcast_to(total[:, here], (8, lane))

        pl.when(upper == which)(lambda: give(keep_ref))
        pl.when(upper != which)(lambda: give(send_ref))


def merge_kernel(first_ref, second_ref, out_ref):
    rows = out_ref.shape[1]
    top = jnp.maximum(first_ref[pl.ds(HD, 1), :], second_ref[pl.ds(HD, 1), :])
    one = jnp.exp(first_ref[pl.ds(HD, 1), :] - top)
    two = jnp.exp(second_ref[pl.ds(HD, 1), :] - top)
    total = first_ref[pl.ds(HD + 8, 1), :] * one + second_ref[pl.ds(HD + 8, 1), :] * two
    acc = first_ref[pl.ds(0, HD), :] * one + second_ref[pl.ds(0, HD), :] * two
    result = (acc / total).T
    for i in range(QH // KVH):
        out_ref[0, :, 0, pl.ds(i * HD, HD)] = result[i * rows : (i + 1) * rows, :]


def gathered(share):
    beside = swap(share, "lay", 1)
    return share, beside, swap(share, "head", 1), swap(beside, "head", 1)


def after(x, *others):
    return lax.optimization_barrier((x, *others))[0]


def split_kernel(values_ref, kept_ref, first_ref, second_ref):
    mine, _, _, _ = pair_sides()
    for i, ref in enumerate((first_ref, second_ref)):
        kept_ref[pl.ds(i * HD, HD), :] = values_ref[:, lanes(2 * i + mine)].T
        ref[...] = values_ref[:, lanes(2 * i + 1 - mine)].T


def paired_body(keys, values, queries, start_block, lengths):
    _, tokens, width = keys.shape
    keys, values, queries = keys[0], values[0], queries[0]
    rank = start_block.shape[1]
    rows = queries.shape[0]
    half, share = width // 2, rank // 4

    gram = call(
        gram_kernel,
        vmem(share, rank),
        start_block,
        scratch=[(rank // 2, rank)],
        flops=400_000_000,
    )
    keep, send, keys_own, keys_send = call(
        start_kernel,
        [vmem(half, rank)] * 2 + [vmem(tokens, half)] * 2,
        keys,
        start_block,
        gram,
        flops=900_000_000,
    )
    gram = gram + swap(gram, "tok", 1)
    proj = keep + swap(after(send, gram), "tok", 1)
    values_own, *values_send = call(
        split_kernel,
        [vmem(half, tokens)] + [vmem(HD, tokens)] * 2,
        after(values, proj),
    )
    values_other = []
    lower = None
    for step in range(ITERS + 1):
        gram = gram + swap(gram, "tok", 2)
        last = step == ITERS
        if step != 1:
            proj = after(proj, gram)
            if step == 0:
                keys_other = swap(after(keys_send, proj), "tok", 1)
        first, second = proj, swap(proj, "tok", 2)
        if step > 0 and len(values_other) < 2:
            values_other.append(swap(after(values_send[len(values_other)], proj, gram), "tok", 1))
        parts = gathered(gram)
        if step == 0 or last:
            lower = inverse_factor(*parts)
            first = after(first, lower, values_own)
        else:
            halves = inverse_factor_low(*parts)
            first = after(first, halves[0], *values_other)
            lower = inverse_factor_high(*halves)
        if last:
            break
        mix = (keys_own, keys_other, first, second)
        z_send, z_keep = (
            call(functools.partial(mix_kernel, sent), vmem(tokens, rank), *mix, flops=400_000_000)
            for sent in (True, False)
        )
        here, there = summed_streams(z_keep, z_send, lower)
        block, parts = vmem(tokens // 2, rank), ()
        blocks = []
        stacks = [here, swap(here, "head", 1)]
        for i in range(3):
            if i == 2:
                there = jnp.concatenate([after(x, *parts) for x in there])
                stacks += [there, swap(there, "head", 1)]
            done, *parts = call(
                functools.partial(stack_kernel, i % 2, i // 2),
                [block, vmem(share, rank), vmem(half, rank)],
                stacks[i],
                lower,
                keys_own,
                keys_other,
                *parts,
                scratch=[(tokens // 2, half), (rank // 2, rank)],
                flops=900_000_000,
            )
            blocks.append(done)
        done, gram = call(
            last_stack_kernel,
            [block, vmem(share, rank)],
            stacks[3],
            lower,
            parts[0],
            scratch=[(rank // 2, rank)],
            flops=600_000_000,
        )
        blocks.append(done)
        proj = call(
            project_kernel,
            vmem(half, rank),
            keys_own,
            keys_other,
            done,
            parts[1],
            scratch=[(tokens // 2, half)],
            flops=400_000_000,
        )
    keep, send = call(
        attend_kernel,
        [vmem(HD + 16, HD)] * 2,
        queries,
        *blocks,
        first,
        second,
        lower,
        values_own,
        *values_other,
        jnp.tile(lengths, 2 * (QH // KVH))[None, :],
        scratch=[(2 * tokens, 2 * (QH // KVH) * rows)],
        flops=3_000_000_000,
    )
    return call(merge_kernel, vmem(1, rows, 1, half * 4), keep, swap(send, "tok", 2))


def solution(mesh):
    paired = (mesh.shape["tok"], mesh.shape["lay"], mesh.shape["head"]) == (4, 2, 2)
    body = paired_body if paired else spread_body
    return jax.shard_map(
        body,
        mesh=mesh,
        in_specs=(
            P("lay", ("groups", "tok"), "head"),
            P("lay", ("groups", "tok"), "head"),
            P("lay", "groups", "head"),
            P(("groups", "tok"), None),
            P("groups"),
        ),
        out_specs=P("lay", "groups", "head", "tok"),
        check_vma=False,
    )
```

```python
import functools
import math

import jax
import jax.numpy as jnp
from jax import lax
from jax.experimental import pallas as pl
from jax.experimental.pallas import tpu as pltpu
from jax.sharding import PartitionSpec as P

KVH = 8
HD = 128
QH = 64
ITERS = 2

NEG = -1e30
HIGHEST = lax.Precision.HIGHEST


def product(left, right, dims):
    return lax.dot_general(
        left, right, (dims, ((), ())), precision=HIGHEST, preferred_element_type=jnp.float32
    )


def diagonal_inverse(tile, step=8):
    size = tile.shape[0]
    rows = lax.broadcasted_iota(jnp.int32, (size, 2 * size), 0)
    cols = lax.broadcasted_iota(jnp.int32, (size, 2 * size), 1)
    state = jnp.concatenate([tile, jnp.zeros_like(tile)], axis=1)
    state = state + jnp.where(cols == rows + size, 1.0, 0.0)
    done = []
    for start in range(0, size, step):
        col = [
            jnp.broadcast_to(state[:, start + i : start + i + 1], state.shape) for i in range(step)
        ]
        row = [state[i : i + 1, :] for i in range(step)]
        state = state[step:]
        for i in range(step):
            pivot = col[i][i : i + 1, :]
            inverse = 1.0 / pivot
            for k in range(i + 1, step):
                ratio = col[i][k : k + 1, :] * inverse
                row[k] = row[k] - ratio * row[i]
                col[k] = col[k] - ratio * col[i]
            if start + step < size:
                state = state - col[i][step:] * (row[i] * inverse)
            done.append(row[i] * lax.rsqrt(pivot))
    return jnp.concatenate(done)[:, size:]


def vmem(*shape):
    return jax.ShapeDtypeStruct(shape, jnp.float32)


def call(kernel, out_shape, *args, scratch=(), flops=0):
    spec = pl.BlockSpec(memory_space=pltpu.VMEM)
    single = not isinstance(out_shape, (tuple, list))
    moved = sum(4 * math.prod(a.shape) for a in (*args, *((out_shape,) if single else out_shape)))
    return pl.pallas_call(
        kernel,
        out_shape=out_shape,
        in_specs=[spec] * len(args),
        out_specs=spec if single else [spec] * len(out_shape),
        scratch_shapes=[pltpu.VMEM(s, jnp.float32) for s in scratch],
        compiler_params=pltpu.CompilerParams(vmem_limit_bytes=40 << 20),
        cost_estimate=pl.CostEstimate(flops=flops, bytes_accessed=moved, transcendentals=0),
    )(*args)


def whole_gram(own_ref, part_refs, gram_ref):
    if not part_refs:
        gram_ref[...] = own_ref[...]
        return
    lay, head = lax.axis_index("lay"), lax.axis_index("head")
    rows = own_ref.shape[0]
    for i, ref in enumerate((own_ref, *part_refs)):
        at = (2 * (head ^ (i // 2)) + (lay ^ (i % 2))) * rows
        gram_ref[pl.ds(pl.multiple_of(at, rows), rows), :] = ref[...]


def factor_kernel(own_ref, *refs):
    *part_refs, out_ref, gram_ref, tile_ref, cross_ref = refs
    whole_gram(own_ref, part_refs, gram_ref)
    half = tile_ref.shape[0]
    low, high = pl.ds(0, half), pl.ds(half, half)

    @pl.loop(0, 2)
    def _(i):
        here = pl.ds(pl.multiple_of(i * half, half), half)
        tile_ref[...] = diagonal_inverse(gram_ref[here, here])
        out_ref[here, here] = tile_ref[...]

        @pl.when(i == 0)
        def _():
            panel = product(tile_ref[...], gram_ref[low, high], ((1,), (0,)))
            gram_ref[high, high] = gram_ref[high, high] - product(panel, panel, ((0,), (0,)))
            cross_ref[...] = product(panel, tile_ref[...], ((0,), (0,)))
            out_ref[low, high] = jnp.zeros((half, half), jnp.float32)

        @pl.when(i == 1)
        def _():
            out_ref[high, low] = -product(tile_ref[...], cross_ref[...], ((1,), (0,)))


def factor_low_kernel(own_ref, *refs):
    *part_refs, tile_ref, cross_ref, left_ref, gram_ref = refs
    whole_gram(own_ref, part_refs, gram_ref)
    half = tile_ref.shape[0]
    low, high = pl.ds(0, half), pl.ds(half, half)
    tile_ref[...] = diagonal_inverse(gram_ref[low, low])
    panel = product(tile_ref[...], gram_ref[low, high], ((1,), (0,)))
    left_ref[...] = gram_ref[high, high] - product(panel, panel, ((0,), (0,)))
    cross_ref[...] = product(panel, tile_ref[...], ((0,), (0,)))


def factor_high_kernel(tile_ref, cross_ref, left_ref, out_ref):
    half = tile_ref.shape[0]
    low, high = pl.ds(0, half), pl.ds(half, half)
    out_ref[low, low] = tile_ref[...]
    out_ref[low, high] = jnp.zeros((half, half), jnp.float32)
    out_ref[high, high] = diagonal_inverse(left_ref[...])
    out_ref[high, low] = -product(out_ref[high, high], cross_ref[...], ((1,), (0,)))


FACTOR_FLOPS = 1_000_000_000


def inverse_factor(*parts):
    rank = parts[0].shape[1]
    half = rank // 2
    return call(
        factor_kernel,
        vmem(rank, rank),
        *parts,
        scratch=[(rank, rank), (half, half), (half, half)],
        flops=FACTOR_FLOPS,
    )


def inverse_factor_low(*parts):
    rank = parts[0].shape[1]
    half = rank // 2
    return call(
        factor_low_kernel, [vmem(half, half)] * 3, *parts, scratch=[(rank, rank)], flops=FACTOR_FLOPS
    )


def inverse_factor_high(*halves):
    rank = 2 * halves[0].shape[0]
    return call(factor_high_kernel, vmem(rank, rank), *halves, flops=FACTOR_FLOPS)


def distances(axis):
    size = lax.axis_size(axis)
    return [1 << i for i in range(size.bit_length() - 1)]


def side(axis, distance):
    return lax.axis_index(axis) // distance % 2


def swap(x, axis, distance):
    pairs = [(i, i ^ distance) for i in range(lax.axis_size(axis))]
    return lax.ppermute(x, axis, pairs)


def halve(x, axis, distance):
    half = x.shape[0] // 2
    mine = side(axis, distance)
    keep = lax.dynamic_slice_in_dim(x, mine * half, half, 0)
    send = lax.dynamic_slice_in_dim(x, (1 - mine) * half, half, 0)
    return keep + swap(send, axis, distance)


def double(x, axis, distance):
    other = swap(x, axis, distance)
    first = side(axis, distance) == 0
    return jnp.concatenate([jnp.where(first, x, other), jnp.where(first, other, x)])


def summed_rows(x, hops):
    for hop in hops:
        x = halve(x, *hop)
    for hop in reversed(hops):
        x = double(x, *hop)
    return x


def spread_body(keys, values, queries, start_block, lengths):
    _, tok_dev, kv_dev = keys.shape
    keys, values = keys[0], values[0]
    rank = start_block.shape[1]
    rows = queries.shape[1]
    local_heads = queries.shape[2] // HD
    group = QH // KVH
    kv_local = kv_dev // HD
    tok_hops = [("tok", d) for d in distances("tok")]
    wide_hops = [("head", d) for d in distances("head")] + [("lay", d) for d in distances("lay")]

    def whole_gram(block):
        share = rank
        at = 0
        for axis, distance in reversed(wide_hops):
            share //= 2
            at = at + side(axis, distance) * share
        part = lax.dynamic_slice_in_dim(block, at, share, 1)
        gram = product(part, block, ((0,), (0,)))
        for hop in tok_hops:
            gram = gram + swap(gram, *hop)
        for hop in wide_hops:
            gram = double(gram, *hop)
        return gram

    def project(block):
        return summed_rows(product(keys, block, ((0,), (0,))), tok_hops)

    def mix(coef):
        return summed_rows(product(keys, coef, ((1,), (0,))), wide_hops)

    block = start_block
    for step in range(ITERS):
        lower = inverse_factor(whole_gram(block))
        block = product(mix(project(block)), lower, ((1,), (1,)))
    lower = inverse_factor(whole_gram(block))
    coef = product(project(block), lower, ((1,), (1,)))
    basis = product(block, lower, ((1,), (1,)))

    quer = queries.reshape(rows, kv_local, group, HD)
    factor = coef.reshape(kv_local, HD, rank)
    reduced = jnp.einsum("bgid,gdr->gibr", quer, factor, precision=HIGHEST) / math.sqrt(HD)
    reduced = reduced.reshape(kv_local, group * rows, rank)
    scores = jnp.einsum("tr,gxr->tgx", basis, reduced, precision=HIGHEST)
    position = lax.axis_index("tok") * tok_dev + jnp.arange(tok_dev, dtype=jnp.int32)
    valid = position[:, None] < lengths[None, :]
    valid = jnp.tile(valid, (1, group))[:, None, :]
    peak = jnp.max(jnp.where(valid, scores, NEG), axis=0)
    weight = jnp.where(valid, jnp.exp(scores - peak[None]), 0.0)
    total = jnp.sum(weight, axis=0)
    vals = values.reshape(tok_dev, kv_local, HD)
    summed = jnp.einsum("tgx,tgd->gxd", weight, vals, precision=HIGHEST)
    peak = peak.reshape(local_heads, rows)
    total = total.reshape(local_heads, rows)
    summed = summed.reshape(local_heads, rows, HD)

    share = local_heads // lax.axis_size("tok")
    peak, total, summed = jax.tree.map(
        lambda a: a.reshape((-1, share) + a.shape[1:]), (peak, total, summed)
    )

    def pack(part):
        top, tot, acc = part
        blank = jnp.zeros(top.shape[:-1] + (HD - 2 * rows,), jnp.float32)
        extra = jnp.concatenate([top, tot, blank], axis=-1).reshape(-1, HD)
        return jnp.concatenate([acc.reshape(-1, HD), extra])

    def unpack(buffer, like):
        count = like[0].shape[0] * share
        extra = buffer[count * rows :]
        return (
            extra[:, :rows].reshape(like[0].shape),
            extra[:, rows : 2 * rows].reshape(like[0].shape),
            buffer[: count * rows].reshape(like[2].shape),
        )

    state = (peak, total, summed)
    for hop in tok_hops:
        mine = side(*hop)
        pairs = jax.tree.map(lambda a: a.reshape((-1, 2) + a.shape[1:]), state)
        keep = jax.tree.map(lambda a: lax.dynamic_index_in_dim(a, mine, 1, False), pairs)
        send = jax.tree.map(lambda a: lax.dynamic_index_in_dim(a, 1 - mine, 1, False), pairs)
        got = unpack(swap(pack(send), *hop), keep)
        top = jnp.maximum(keep[0], got[0])
        one, two = jnp.exp(keep[0] - top), jnp.exp(got[0] - top)
        state = (
            top,
            keep[1] * one + got[1] * two,
            keep[2] * one[..., None] + got[2] * two[..., None],
        )
    result = state[2][0] / state[1][0][..., None]
    return result.transpose(1, 0, 2).reshape(1, rows, 1, share * HD)


def pair_sides():
    return side("tok", 1), side("tok", 2), lax.axis_index("lay"), lax.axis_index("head")


def lanes(index, size=HD):
    return pl.ds(pl.multiple_of(index * size, size), size)


def gram_share(block_ref, scratch_ref, out_ref):
    _, _, lay, head = pair_sides()
    rows, half = out_ref.shape[0], scratch_ref.shape[0]
    scratch_ref[...] = product(block_ref[:, lanes(head, half)], block_ref[...], ((0,), (0,)))
    out_ref[...] = scratch_ref[lanes(lay, rows), :]


def gram_kernel(block_ref, out_ref, scratch_ref):
    gram_share(block_ref, scratch_ref, out_ref)


def start_kernel(keys_ref, block_ref, gram_ref, keep_ref, send_ref, kept_ref, sent_ref):
    del gram_ref
    mine, _, _, _ = pair_sides()
    for i in range(2):
        at = pl.ds(i * HD, HD)
        kept_ref[:, at] = keys_ref[:, lanes(2 * i + mine)]
        sent_ref[:, at] = keys_ref[:, lanes(2 * i + 1 - mine)]
    send_ref[...] = product(sent_ref[...], block_ref[...], ((0,), (0,)))
    keep_ref[...] = product(kept_ref[...], block_ref[...], ((0,), (0,)))


def mix_kernel(sent, own_ref, other_ref, first_ref, second_ref, out_ref):
    mine, _, _, head = pair_sides()
    held = pl.ds(0, own_ref.shape[1])
    coef = first_ref[held, :] + second_ref[held, :]
    half = own_ref.shape[0] // 2
    rows = lanes(head ^ int(sent), half)
    for keys_ref, piece in ((own_ref, mine), (other_ref, 1 - mine)):
        out_ref[lanes(piece, half), :] = product(keys_ref[rows, :], coef, ((1,), (0,)))


def streams_kernel(first_ref, second_ref, a_keep, a_send, b_keep, b_send):
    mine, _, lay, _ = pair_sides()
    half = first_ref.shape[0] // 2
    quarter, eighth = half // 2, half // 4

    def rows(piece, at, count):
        here = pl.ds(pl.multiple_of(piece * half + at, count), count)
        return first_ref[here, :] + second_ref[here, :]

    for piece in range(2):
        to = pl.ds(piece * eighth, eighth)
        a_keep[to, :] = rows(piece, lay * eighth, eighth)
        a_send[to, :] = rows(piece, (1 - lay) * eighth, eighth)
    b_keep[...] = rows(mine, quarter, quarter)
    b_send[...] = rows(1 - mine, quarter, quarter)


def summed_streams(keep, send, ready, lower):
    got = swap(send, "head", 1)
    quarter = vmem(keep.shape[0] // 4, keep.shape[1])
    a_keep, a_send, b_keep, b_send = call(streams_kernel, [quarter] * 4, keep, got)
    a = after(a_keep + swap(a_send, "lay", 1), ready)
    b = b_keep + swap(b_send, "tok", 1)
    a, b = a + swap(a, "tok", 1), b + swap(b, "lay", 1)
    a = after(a, lower)
    here = jnp.concatenate([a, b])
    return here, (swap(a, "lay", 1), swap(b, "tok", 1))


def stack_rows(far, beside, size):
    _, _, lay, head = pair_sides()
    count = size // 2
    first = (head ^ far) * size
    return first + (lay ^ beside) * (count // 2), first + count


def project_stack(far, beside, own_ref, other_ref, block_ref, rows_ref):
    mine, _, _, _ = pair_sides()
    size = block_ref.shape[0]
    half, quarter = size // 2, size // 4
    low, high = stack_rows(far, beside, size)
    low = pl.ds(pl.multiple_of(low, quarter), quarter)
    rows_ref[lanes(mine, quarter), :] = own_ref[low, :]
    rows_ref[lanes(1 - mine, quarter), :] = other_ref[low, :]
    high = pl.ds(pl.multiple_of(high, half), half)
    rows_ref[pl.ds(half, half), :] = (other_ref if beside else own_ref)[high, :]
    return product(rows_ref[...], block_ref[...], ((0,), (0,)))


def stack_kernel(far, beside, stack_ref, lower_ref, own_ref, other_ref, *refs):
    *part_refs, block_ref, gram_ref, proj_ref, rows_ref, scratch_ref = refs
    block_ref[...] = product(stack_ref[...], lower_ref[...], ((1,), (1,)))
    gram_share(block_ref, scratch_ref, gram_ref)
    proj_ref[...] = project_stack(far, beside, own_ref, other_ref, block_ref, rows_ref)
    for part_ref, ref in zip(part_refs, (gram_ref, proj_ref)):
        ref[...] += part_ref[...]


def last_stack_kernel(stack_ref, lower_ref, part_ref, block_ref, gram_ref, scratch_ref):
    block_ref[...] = product(stack_ref[...], lower_ref[...], ((1,), (1,)))
    gram_share(block_ref, scratch_ref, gram_ref)
    gram_ref[...] += part_ref[...]


def project_kernel(own_ref, other_ref, block_ref, part_ref, proj_ref, rows_ref):
    proj_ref[...] = part_ref[...] + project_stack(1, 1, own_ref, other_ref, block_ref, rows_ref)


def project_and_pack_kernel(own_ref, other_ref, block_ref, part_ref, gram_ref, proj_ref, rows_ref):
    count = part_ref.shape[0]
    proj_ref[pl.ds(0, count), :] = part_ref[...] + project_stack(
        1, 1, own_ref, other_ref, block_ref, rows_ref
    )
    proj_ref[pl.ds(count, gram_ref.shape[0]), :] = gram_ref[...]


def attend_kernel(
    query_ref,
    *refs,
):
    *block_refs, first_ref, second_ref, lower_ref, own_ref, low_ref, high_ref, length_ref = refs[:-3]
    keep_ref, send_ref, score_ref = refs[-3:]
    mine, upper, _, _ = pair_sides()
    group = QH // KVH
    tokens = own_ref.shape[1]
    half, width = tokens // 2, length_ref.shape[1]
    coef = product(first_ref[...] + second_ref[...], lower_ref[...], ((1,), (1,)))
    reduced = []
    for which in range(2):
        quer = jnp.concatenate(
            [query_ref[:, lanes((2 * which + mine) * group + i)] for i in range(group)]
        )
        factor = coef[which * HD : (which + 1) * HD]
        reduced.append(product(quer, factor, ((1,), (0,))) / math.sqrt(HD))
    reduced = product(jnp.concatenate(reduced), lower_ref[...], ((1,), (0,)))
    for i, block_ref in enumerate(block_refs):
        far, beside = i % 2, i // 2
        part = product(block_ref[...], reduced, ((1,), (1,)))
        low, high = stack_rows(far, beside, half)
        quarter = half // 4
        for piece in range(2):
            to = pl.multiple_of((piece ^ mine) * tokens + low, quarter)
            score_ref[pl.ds(to, quarter), :] = part[piece * quarter : (piece + 1) * quarter]
        to = pl.multiple_of(beside * tokens + high, half // 2)
        score_ref[pl.ds(to, half // 2), :] = part[half // 2 :]
    scores = score_ref[...]
    at = lax.broadcasted_iota(jnp.int32, (tokens, width), 0)
    tok = lax.axis_index("tok")
    valid = jnp.concatenate(
        [(tok ^ piece) * tokens + at < length_ref[...] for piece in range(2)]
    )
    peak = jnp.max(jnp.where(valid, scores, NEG), axis=0, keepdims=True)
    weight = jnp.where(valid, jnp.exp(scores - peak), 0.0)
    total = jnp.sum(weight, axis=0, keepdims=True)
    lane = width // 2
    for which, there_ref in enumerate((low_ref, high_ref)):
        here = slice(which * lane, (which + 1) * lane)
        own = own_ref[pl.ds(which * HD, HD), :]
        acc = product(own, weight[:tokens, here], ((1,), (0,)))
        acc = acc + product(there_ref[...], weight[tokens:, here], ((1,), (0,)))

        def give(ref):
            ref[pl.ds(0, HD), :] = acc
            ref[pl.ds(HD, 8), :] = jnp.broadcast_to(peak[:, here], (8, lane))
            ref[pl.ds(HD + 8, 8), :] = jnp.broadcast_to(total[:, here], (8, lane))

        pl.when(upper == which)(lambda: give(keep_ref))
        pl.when(upper != which)(lambda: give(send_ref))


def merge_kernel(first_ref, second_ref, out_ref):
    rows = out_ref.shape[1]
    top = jnp.maximum(first_ref[pl.ds(HD, 1), :], second_ref[pl.ds(HD, 1), :])
    one = jnp.exp(first_ref[pl.ds(HD, 1), :] - top)
    two = jnp.exp(second_ref[pl.ds(HD, 1), :] - top)
    total = first_ref[pl.ds(HD + 8, 1), :] * one + second_ref[pl.ds(HD + 8, 1), :] * two
    acc = first_ref[pl.ds(0, HD), :] * one + second_ref[pl.ds(0, HD), :] * two
    result = (acc / total).T
    for i in range(QH // KVH):
        out_ref[0, :, 0, pl.ds(i * HD, HD)] = result[i * rows : (i + 1) * rows, :]


def gathered(share):
    beside = swap(share, "lay", 1)
    return share, beside, swap(share, "head", 1), swap(beside, "head", 1)


def after(x, *others):
    return lax.optimization_barrier((x, *others))[0]


def split_kernel(values_ref, kept_ref, first_ref, second_ref):
    mine, _, _, _ = pair_sides()
    for i, ref in enumerate((first_ref, second_ref)):
        kept_ref[pl.ds(i * HD, HD), :] = values_ref[:, lanes(2 * i + mine)].T
        ref[...] = values_ref[:, lanes(2 * i + 1 - mine)].T


def paired_body(keys, values, queries, start_block, lengths):
    _, tokens, width = keys.shape
    keys, values, queries = keys[0], values[0], queries[0]
    rank = start_block.shape[1]
    rows = queries.shape[0]
    half, share = width // 2, rank // 4

    gram = call(
        gram_kernel,
        vmem(share, rank),
        start_block,
        scratch=[(rank // 2, rank)],
        flops=400_000_000,
    )
    keep, send, keys_own, keys_send = call(
        start_kernel,
        [vmem(half, rank)] * 2 + [vmem(tokens, half)] * 2,
        keys,
        start_block,
        gram,
        flops=900_000_000,
    )
    gram = gram + swap(gram, "tok", 1)
    proj = keep + swap(after(send, gram), "tok", 1)
    values_own, *values_send = call(
        split_kernel,
        [vmem(half, tokens)] + [vmem(HD, tokens)] * 2,
        after(values, proj),
    )
    values_other = []
    lower = None
    for step in range(ITERS + 1):
        last = step == ITERS
        if step != 1:
            gram = gram + swap(gram, "tok", 2)
            proj = after(proj, gram)
        if step == 0:
            keys_other = swap(after(keys_send, proj), "tok", 1)
        first, second = proj, swap(proj, "tok", 2)
        if step > 0:
            values_other.append(swap(after(values_send[step - 1], proj), "tok", 1))
        if step == 1:
            halves = inverse_factor_low(*gathered(first[half:] + second[half:]))
            ready, lower = halves[0], inverse_factor_high(*halves)
            first = after(first, *values_other)
        else:
            ready = lower = inverse_factor(*gathered(gram))
            first = after(first, lower, values_own)
        if last:
            break
        mix = (keys_own, keys_other, first, second)
        z_send, z_keep = (
            call(functools.partial(mix_kernel, sent), vmem(tokens, rank), *mix, flops=400_000_000)
            for sent in (True, False)
        )
        here, there = summed_streams(z_keep, z_send, ready, lower)
        block, parts = vmem(tokens // 2, rank), ()
        blocks = []
        stacks = [here, swap(here, "head", 1)]
        for i in range(3):
            if i == 2:
                there = jnp.concatenate([after(x, *parts) for x in there])
                stacks += [there, swap(there, "head", 1)]
            done, *parts = call(
                functools.partial(stack_kernel, i % 2, i // 2),
                [block, vmem(share, rank), vmem(half, rank)],
                stacks[i],
                lower,
                keys_own,
                keys_other,
                *parts,
                scratch=[(tokens // 2, half), (rank // 2, rank)],
                flops=900_000_000,
            )
            blocks.append(done)
        done, gram = call(
            last_stack_kernel,
            [block, vmem(share, rank)],
            stacks[3],
            lower,
            parts[0],
            scratch=[(rank // 2, rank)],
            flops=600_000_000,
        )
        blocks.append(done)
        packed = step == 0
        proj = call(
            project_and_pack_kernel if packed else project_kernel,
            vmem(half + share if packed else half, rank),
            keys_own,
            keys_other,
            done,
            parts[1],
            *((gram,) if packed else ()),
            scratch=[(tokens // 2, half)],
            flops=400_000_000,
        )
    keep, send = call(
        attend_kernel,
        [vmem(HD + 16, HD)] * 2,
        queries,
        *blocks,
        first,
        second,
        lower,
        values_own,
        *values_other,
        jnp.tile(lengths, 2 * (QH // KVH))[None, :],
        scratch=[(2 * tokens, 2 * (QH // KVH) * rows)],
        flops=3_000_000_000,
    )
    return call(merge_kernel, vmem(1, rows, 1, half * 4), keep, swap(send, "tok", 2))


def solution(mesh):
    paired = (mesh.shape["tok"], mesh.shape["lay"], mesh.shape["head"]) == (4, 2, 2)
    body = paired_body if paired else spread_body
    return jax.shard_map(
        body,
        mesh=mesh,
        in_specs=(
            P("lay", ("groups", "tok"), "head"),
            P("lay", ("groups", "tok"), "head"),
            P("lay", "groups", "head"),
            P(("groups", "tok"), None),
            P("groups"),
        ),
        out_specs=P("lay", "groups", "head", "tok"),
        check_vma=False,
    )
```

```python
import functools
import math

import jax
import jax.numpy as jnp
from jax import lax
from jax.experimental import pallas as pl
from jax.experimental.pallas import tpu as pltpu
from jax.sharding import PartitionSpec as P

KVH = 8
HD = 128
QH = 64
ITERS = 2

NEG = -1e30
HIGHEST = lax.Precision.HIGHEST


def product(left, right, dims):
    return lax.dot_general(
        left, right, (dims, ((), ())), precision=HIGHEST, preferred_element_type=jnp.float32
    )


def diagonal_inverse(tile, step=8):
    size = tile.shape[0]
    rows = lax.broadcasted_iota(jnp.int32, (size, 2 * size), 0)
    cols = lax.broadcasted_iota(jnp.int32, (size, 2 * size), 1)
    state = jnp.concatenate([tile, jnp.zeros_like(tile)], axis=1)
    state = state + jnp.where(cols == rows + size, 1.0, 0.0)
    done = []
    for start in range(0, size, step):
        col = [
            jnp.broadcast_to(state[:, start + i : start + i + 1], state.shape) for i in range(step)
        ]
        row = [state[i : i + 1, :] for i in range(step)]
        state = state[step:]
        for i in range(step):
            pivot = col[i][i : i + 1, :]
            inverse = 1.0 / pivot
            for k in range(i + 1, step):
                ratio = col[i][k : k + 1, :] * inverse
                row[k] = row[k] - ratio * row[i]
                col[k] = col[k] - ratio * col[i]
            if start + step < size:
                state = state - col[i][step:] * (row[i] * inverse)
            done.append(row[i] * lax.rsqrt(pivot))
    return jnp.concatenate(done)[:, size:]


def vmem(*shape):
    return jax.ShapeDtypeStruct(shape, jnp.float32)


def call(kernel, out_shape, *args, scratch=(), flops=0):
    spec = pl.BlockSpec(memory_space=pltpu.VMEM)
    single = not isinstance(out_shape, (tuple, list))
    moved = sum(4 * math.prod(a.shape) for a in (*args, *((out_shape,) if single else out_shape)))
    return pl.pallas_call(
        kernel,
        out_shape=out_shape,
        in_specs=[spec] * len(args),
        out_specs=spec if single else [spec] * len(out_shape),
        scratch_shapes=[pltpu.VMEM(s, jnp.float32) for s in scratch],
        compiler_params=pltpu.CompilerParams(vmem_limit_bytes=40 << 20),
        cost_estimate=pl.CostEstimate(flops=flops, bytes_accessed=moved, transcendentals=0),
    )(*args)


def whole_gram(own_ref, part_refs, gram_ref):
    if not part_refs:
        gram_ref[...] = own_ref[...]
        return
    lay, head = lax.axis_index("lay"), lax.axis_index("head")
    rows = own_ref.shape[0]
    for i, ref in enumerate((own_ref, *part_refs)):
        at = (2 * (head ^ (i // 2)) + (lay ^ (i % 2))) * rows
        gram_ref[pl.ds(pl.multiple_of(at, rows), rows), :] = ref[...]


def factor_kernel(own_ref, *refs):
    *part_refs, out_ref, gram_ref, tile_ref, cross_ref = refs
    whole_gram(own_ref, part_refs, gram_ref)
    half = tile_ref.shape[0]
    low, high = pl.ds(0, half), pl.ds(half, half)

    @pl.loop(0, 2)
    def _(i):
        here = pl.ds(pl.multiple_of(i * half, half), half)
        tile_ref[...] = diagonal_inverse(gram_ref[here, here])
        out_ref[here, here] = tile_ref[...]

        @pl.when(i == 0)
        def _():
            panel = product(tile_ref[...], gram_ref[low, high], ((1,), (0,)))
            gram_ref[high, high] = gram_ref[high, high] - product(panel, panel, ((0,), (0,)))
            cross_ref[...] = product(panel, tile_ref[...], ((0,), (0,)))
            out_ref[low, high] = jnp.zeros((half, half), jnp.float32)

        @pl.when(i == 1)
        def _():
            out_ref[high, low] = -product(tile_ref[...], cross_ref[...], ((1,), (0,)))


def factor_low_kernel(own_ref, *refs):
    *part_refs, tile_ref, cross_ref, left_ref, gram_ref = refs
    whole_gram(own_ref, part_refs, gram_ref)
    half = tile_ref.shape[0]
    low, high = pl.ds(0, half), pl.ds(half, half)
    tile_ref[...] = diagonal_inverse(gram_ref[low, low])
    panel = product(tile_ref[...], gram_ref[low, high], ((1,), (0,)))
    left_ref[...] = gram_ref[high, high] - product(panel, panel, ((0,), (0,)))
    cross_ref[...] = product(panel, tile_ref[...], ((0,), (0,)))


def factor_high_kernel(tile_ref, cross_ref, left_ref, out_ref):
    half = tile_ref.shape[0]
    low, high = pl.ds(0, half), pl.ds(half, half)
    out_ref[low, low] = tile_ref[...]
    out_ref[low, high] = jnp.zeros((half, half), jnp.float32)
    out_ref[high, high] = diagonal_inverse(left_ref[...])
    out_ref[high, low] = -product(out_ref[high, high], cross_ref[...], ((1,), (0,)))


FACTOR_FLOPS = 1_000_000_000


def inverse_factor(*parts):
    rank = parts[0].shape[1]
    half = rank // 2
    return call(
        factor_kernel,
        vmem(rank, rank),
        *parts,
        scratch=[(rank, rank), (half, half), (half, half)],
        flops=FACTOR_FLOPS,
    )


def inverse_factor_low(*parts):
    rank = parts[0].shape[1]
    half = rank // 2
    return call(
        factor_low_kernel, [vmem(half, half)] * 3, *parts, scratch=[(rank, rank)], flops=FACTOR_FLOPS
    )


def inverse_factor_high(*halves):
    rank = 2 * halves[0].shape[0]
    return call(factor_high_kernel, vmem(rank, rank), *halves, flops=FACTOR_FLOPS)


def distances(axis):
    size = lax.axis_size(axis)
    return [1 << i for i in range(size.bit_length() - 1)]


def side(axis, distance):
    return lax.axis_index(axis) // distance % 2


def swap(x, axis, distance):
    pairs = [(i, i ^ distance) for i in range(lax.axis_size(axis))]
    return lax.ppermute(x, axis, pairs)


def halve(x, axis, distance):
    half = x.shape[0] // 2
    mine = side(axis, distance)
    keep = lax.dynamic_slice_in_dim(x, mine * half, half, 0)
    send = lax.dynamic_slice_in_dim(x, (1 - mine) * half, half, 0)
    return keep + swap(send, axis, distance)


def double(x, axis, distance):
    other = swap(x, axis, distance)
    first = side(axis, distance) == 0
    return jnp.concatenate([jnp.where(first, x, other), jnp.where(first, other, x)])


def summed_rows(x, hops):
    for hop in hops:
        x = halve(x, *hop)
    for hop in reversed(hops):
        x = double(x, *hop)
    return x


def spread_body(keys, values, queries, start_block, lengths):
    _, tok_dev, kv_dev = keys.shape
    keys, values = keys[0], values[0]
    rank = start_block.shape[1]
    rows = queries.shape[1]
    local_heads = queries.shape[2] // HD
    group = QH // KVH
    kv_local = kv_dev // HD
    tok_hops = [("tok", d) for d in distances("tok")]
    wide_hops = [("head", d) for d in distances("head")] + [("lay", d) for d in distances("lay")]

    def whole_gram(block):
        share = rank
        at = 0
        for axis, distance in reversed(wide_hops):
            share //= 2
            at = at + side(axis, distance) * share
        part = lax.dynamic_slice_in_dim(block, at, share, 1)
        gram = product(part, block, ((0,), (0,)))
        for hop in tok_hops:
            gram = gram + swap(gram, *hop)
        for hop in wide_hops:
            gram = double(gram, *hop)
        return gram

    def project(block):
        return summed_rows(product(keys, block, ((0,), (0,))), tok_hops)

    def mix(coef):
        return summed_rows(product(keys, coef, ((1,), (0,))), wide_hops)

    block = start_block
    for step in range(ITERS):
        lower = inverse_factor(whole_gram(block))
        block = product(mix(project(block)), lower, ((1,), (1,)))
    lower = inverse_factor(whole_gram(block))
    coef = product(project(block), lower, ((1,), (1,)))
    basis = product(block, lower, ((1,), (1,)))

    quer = queries.reshape(rows, kv_local, group, HD)
    factor = coef.reshape(kv_local, HD, rank)
    reduced = jnp.einsum("bgid,gdr->gibr", quer, factor, precision=HIGHEST) / math.sqrt(HD)
    reduced = reduced.reshape(kv_local, group * rows, rank)
    scores = jnp.einsum("tr,gxr->tgx", basis, reduced, precision=HIGHEST)
    position = lax.axis_index("tok") * tok_dev + jnp.arange(tok_dev, dtype=jnp.int32)
    valid = position[:, None] < lengths[None, :]
    valid = jnp.tile(valid, (1, group))[:, None, :]
    peak = jnp.max(jnp.where(valid, scores, NEG), axis=0)
    weight = jnp.where(valid, jnp.exp(scores - peak[None]), 0.0)
    total = jnp.sum(weight, axis=0)
    vals = values.reshape(tok_dev, kv_local, HD)
    summed = jnp.einsum("tgx,tgd->gxd", weight, vals, precision=HIGHEST)
    peak = peak.reshape(local_heads, rows)
    total = total.reshape(local_heads, rows)
    summed = summed.reshape(local_heads, rows, HD)

    share = local_heads // lax.axis_size("tok")
    peak, total, summed = jax.tree.map(
        lambda a: a.reshape((-1, share) + a.shape[1:]), (peak, total, summed)
    )

    def pack(part):
        top, tot, acc = part
        blank = jnp.zeros(top.shape[:-1] + (HD - 2 * rows,), jnp.float32)
        extra = jnp.concatenate([top, tot, blank], axis=-1).reshape(-1, HD)
        return jnp.concatenate([acc.reshape(-1, HD), extra])

    def unpack(buffer, like):
        count = like[0].shape[0] * share
        extra = buffer[count * rows :]
        return (
            extra[:, :rows].reshape(like[0].shape),
            extra[:, rows : 2 * rows].reshape(like[0].shape),
            buffer[: count * rows].reshape(like[2].shape),
        )

    state = (peak, total, summed)
    for hop in tok_hops:
        mine = side(*hop)
        pairs = jax.tree.map(lambda a: a.reshape((-1, 2) + a.shape[1:]), state)
        keep = jax.tree.map(lambda a: lax.dynamic_index_in_dim(a, mine, 1, False), pairs)
        send = jax.tree.map(lambda a: lax.dynamic_index_in_dim(a, 1 - mine, 1, False), pairs)
        got = unpack(swap(pack(send), *hop), keep)
        top = jnp.maximum(keep[0], got[0])
        one, two = jnp.exp(keep[0] - top), jnp.exp(got[0] - top)
        state = (
            top,
            keep[1] * one + got[1] * two,
            keep[2] * one[..., None] + got[2] * two[..., None],
        )
    result = state[2][0] / state[1][0][..., None]
    return result.transpose(1, 0, 2).reshape(1, rows, 1, share * HD)


def pair_sides():
    return side("tok", 1), side("tok", 2), lax.axis_index("lay"), lax.axis_index("head")


def lanes(index, size=HD):
    return pl.ds(pl.multiple_of(index * size, size), size)


def gram_share(block_ref, scratch_ref, out_ref):
    _, _, lay, head = pair_sides()
    rows, half = out_ref.shape[0], scratch_ref.shape[0]
    scratch_ref[...] = product(block_ref[:, lanes(head, half)], block_ref[...], ((0,), (0,)))
    out_ref[...] = scratch_ref[lanes(lay, rows), :]


def gram_kernel(block_ref, out_ref, scratch_ref):
    gram_share(block_ref, scratch_ref, out_ref)


def start_kernel(keys_ref, block_ref, gram_ref, keep_ref, send_ref, kept_ref, sent_ref):
    del gram_ref
    mine, _, _, _ = pair_sides()
    for i in range(2):
        at = pl.ds(i * HD, HD)
        kept_ref[:, at] = keys_ref[:, lanes(2 * i + mine)]
        sent_ref[:, at] = keys_ref[:, lanes(2 * i + 1 - mine)]
    send_ref[...] = product(sent_ref[...], block_ref[...], ((0,), (0,)))
    keep_ref[...] = product(kept_ref[...], block_ref[...], ((0,), (0,)))


def mix_kernel(sent, own_ref, other_ref, first_ref, second_ref, out_ref):
    mine, _, _, head = pair_sides()
    coef = first_ref[...] + second_ref[...]
    half = own_ref.shape[0] // 2
    rows = lanes(head ^ int(sent), half)
    for keys_ref, piece in ((own_ref, mine), (other_ref, 1 - mine)):
        out_ref[lanes(piece, half), :] = product(keys_ref[rows, :], coef, ((1,), (0,)))


def streams_kernel(first_ref, second_ref, a_keep, a_send, b_keep, b_send):
    mine, _, lay, _ = pair_sides()
    half = first_ref.shape[0] // 2
    quarter, eighth = half // 2, half // 4

    def rows(piece, at, count):
        here = pl.ds(pl.multiple_of(piece * half + at, count), count)
        return first_ref[here, :] + second_ref[here, :]

    for piece in range(2):
        to = pl.ds(piece * eighth, eighth)
        a_keep[to, :] = rows(piece, lay * eighth, eighth)
        a_send[to, :] = rows(piece, (1 - lay) * eighth, eighth)
    b_keep[...] = rows(mine, quarter, quarter)
    b_send[...] = rows(1 - mine, quarter, quarter)


def summed_streams(keep, send, lower):
    got = swap(send, "head", 1)
    quarter = vmem(keep.shape[0] // 4, keep.shape[1])
    a_keep, a_send, b_keep, b_send = call(streams_kernel, [quarter] * 4, keep, got)
    a = a_keep + swap(a_send, "lay", 1)
    b = b_keep + swap(b_send, "tok", 1)
    a, b = a + swap(a, "tok", 1), b + swap(b, "lay", 1)
    a = after(a, lower)
    here = jnp.concatenate([a, b])
    return here, (swap(a, "lay", 1), swap(b, "tok", 1))


def stack_rows(far, beside, size):
    _, _, lay, head = pair_sides()
    count = size // 2
    first = (head ^ far) * size
    return first + (lay ^ beside) * (count // 2), first + count


def project_stack(far, beside, own_ref, other_ref, block_ref, rows_ref):
    mine, _, _, _ = pair_sides()
    size = block_ref.shape[0]
    half, quarter = size // 2, size // 4
    low, high = stack_rows(far, beside, size)
    low = pl.ds(pl.multiple_of(low, quarter), quarter)
    rows_ref[lanes(mine, quarter), :] = own_ref[low, :]
    rows_ref[lanes(1 - mine, quarter), :] = other_ref[low, :]
    high = pl.ds(pl.multiple_of(high, half), half)
    rows_ref[pl.ds(half, half), :] = (other_ref if beside else own_ref)[high, :]
    return product(rows_ref[...], block_ref[...], ((0,), (0,)))


def stack_kernel(far, beside, stack_ref, lower_ref, own_ref, other_ref, *refs):
    *part_refs, block_ref, gram_ref, proj_ref, rows_ref, scratch_ref = refs
    block_ref[...] = product(stack_ref[...], lower_ref[...], ((1,), (1,)))
    gram_share(block_ref, scratch_ref, gram_ref)
    proj_ref[...] = project_stack(far, beside, own_ref, other_ref, block_ref, rows_ref)
    for part_ref, ref in zip(part_refs, (gram_ref, proj_ref)):
        ref[...] += part_ref[...]


def last_stack_kernel(stack_ref, lower_ref, part_ref, block_ref, gram_ref, scratch_ref):
    block_ref[...] = product(stack_ref[...], lower_ref[...], ((1,), (1,)))
    gram_share(block_ref, scratch_ref, gram_ref)
    gram_ref[...] += part_ref[...]


def project_kernel(own_ref, other_ref, block_ref, part_ref, proj_ref, rows_ref):
    proj_ref[...] = part_ref[...] + project_stack(1, 1, own_ref, other_ref, block_ref, rows_ref)


def attend_kernel(sent, query_ref, *refs):
    *block_refs, first_ref, second_ref, lower_ref, own_ref, low_ref, high_ref, length_ref = refs[:-2]
    out_ref, score_ref = refs[-2:]
    mine, upper, _, _ = pair_sides()
    which = upper ^ int(sent)
    group = QH // KVH
    tokens = own_ref.shape[1]
    half, width = tokens // 2, length_ref.shape[1]
    local = lanes(which)
    coef = product(first_ref[local, :] + second_ref[local, :], lower_ref[...], ((1,), (1,)))
    quer = jnp.concatenate(
        [query_ref[:, lanes((2 * which + mine) * group + i)] for i in range(group)]
    )
    reduced = product(quer, coef, ((1,), (0,))) / math.sqrt(HD)
    reduced = product(reduced, lower_ref[...], ((1,), (0,)))
    for i, block_ref in enumerate(block_refs):
        far, beside = i % 2, i // 2
        part = product(block_ref[...], reduced, ((1,), (1,)))
        low, high = stack_rows(far, beside, half)
        quarter = half // 4
        for piece in range(2):
            to = pl.multiple_of((piece ^ mine) * tokens + low, quarter)
            score_ref[pl.ds(to, quarter), :] = part[piece * quarter : (piece + 1) * quarter]
        to = pl.multiple_of(beside * tokens + high, half // 2)
        score_ref[pl.ds(to, half // 2), :] = part[half // 2 :]
    scores = score_ref[...]
    at = lax.broadcasted_iota(jnp.int32, (tokens, width), 0)
    tok = lax.axis_index("tok")
    valid = jnp.concatenate(
        [(tok ^ piece) * tokens + at < length_ref[...] for piece in range(2)]
    )
    peak = jnp.max(jnp.where(valid, scores, NEG), axis=0, keepdims=True)
    weight = jnp.where(valid, jnp.exp(scores - peak), 0.0)
    total = jnp.sum(weight, axis=0, keepdims=True)
    other = jnp.where(which == 0, low_ref[...], high_ref[...])
    acc = product(own_ref[local, :], weight[:tokens], ((1,), (0,)))
    out_ref[pl.ds(0, HD), :] = acc + product(other, weight[tokens:], ((1,), (0,)))
    out_ref[pl.ds(HD, 8), :] = jnp.broadcast_to(peak, (8, width))
    out_ref[pl.ds(HD + 8, 8), :] = jnp.broadcast_to(total, (8, width))


def merge_kernel(first_ref, second_ref, out_ref):
    rows = out_ref.shape[1]
    top = jnp.maximum(first_ref[pl.ds(HD, 1), :], second_ref[pl.ds(HD, 1), :])
    one = jnp.exp(first_ref[pl.ds(HD, 1), :] - top)
    two = jnp.exp(second_ref[pl.ds(HD, 1), :] - top)
    total = first_ref[pl.ds(HD + 8, 1), :] * one + second_ref[pl.ds(HD + 8, 1), :] * two
    acc = first_ref[pl.ds(0, HD), :] * one + second_ref[pl.ds(0, HD), :] * two
    result = (acc / total).T
    for i in range(QH // KVH):
        out_ref[0, :, 0, pl.ds(i * HD, HD)] = result[i * rows : (i + 1) * rows, :]


def gathered(share):
    beside = swap(share, "lay", 1)
    return share, beside, swap(share, "head", 1), swap(beside, "head", 1)


def after(x, *others):
    return lax.optimization_barrier((x, *others))[0]


def split_kernel(values_ref, kept_ref, first_ref, second_ref):
    mine, _, _, _ = pair_sides()
    for i, ref in enumerate((first_ref, second_ref)):
        kept_ref[pl.ds(i * HD, HD), :] = values_ref[:, lanes(2 * i + mine)].T
        ref[...] = values_ref[:, lanes(2 * i + 1 - mine)].T


def paired_body(keys, values, queries, start_block, lengths):
    _, tokens, width = keys.shape
    keys, values, queries = keys[0], values[0], queries[0]
    rank = start_block.shape[1]
    rows = queries.shape[0]
    half, share = width // 2, rank // 4

    gram = call(
        gram_kernel,
        vmem(share, rank),
        start_block,
        scratch=[(rank // 2, rank)],
        flops=400_000_000,
    )
    keep, send, keys_own, keys_send = call(
        start_kernel,
        [vmem(half, rank)] * 2 + [vmem(tokens, half)] * 2,
        keys,
        start_block,
        gram,
        flops=900_000_000,
    )
    gram = gram + swap(gram, "tok", 1)
    proj = keep + swap(after(send, gram), "tok", 1)
    values_own, *values_send = call(
        split_kernel,
        [vmem(half, tokens)] + [vmem(HD, tokens)] * 2,
        after(values, proj),
    )
    values_other = []
    lower = None
    for step in range(ITERS + 1):
        gram = gram + swap(gram, "tok", 2)
        last = step == ITERS
        if step != 1:
            proj = after(proj, gram)
            if step == 0:
                keys_other = swap(after(keys_send, proj), "tok", 1)
        first, second = proj, swap(proj, "tok", 2)
        if step > 0 and len(values_other) < 2:
            values_other.append(swap(after(values_send[len(values_other)], proj, gram), "tok", 1))
        parts = gathered(gram)
        if step == 0 or last:
            lower = inverse_factor(after(parts[0], values_own), *parts[1:])
            first = after(first, lower)
        else:
            halves = inverse_factor_low(*parts)
            first = after(first, halves[0], *values_other)
            lower = inverse_factor_high(*halves)
        if last:
            break
        mix = (keys_own, keys_other, first, second)
        z_send, z_keep = (
            call(functools.partial(mix_kernel, sent), vmem(tokens, rank), *mix, flops=400_000_000)
            for sent in (True, False)
        )
        here, there = summed_streams(z_keep, z_send, lower)
        block, parts = vmem(tokens // 2, rank), ()
        blocks = []
        stacks = [here, swap(here, "head", 1)]
        for i in range(3):
            if i == 2:
                there = jnp.concatenate([after(x, *parts) for x in there])
                stacks += [there, swap(there, "head", 1)]
            done, *parts = call(
                functools.partial(stack_kernel, i % 2, i // 2),
                [block, vmem(share, rank), vmem(half, rank)],
                stacks[i],
                lower,
                keys_own,
                keys_other,
                *parts,
                scratch=[(tokens // 2, half), (rank // 2, rank)],
                flops=900_000_000,
            )
            blocks.append(done)
        done, gram = call(
            last_stack_kernel,
            [block, vmem(share, rank)],
            stacks[3],
            lower,
            parts[0],
            scratch=[(rank // 2, rank)],
            flops=600_000_000,
        )
        blocks.append(done)
        proj = call(
            project_kernel,
            vmem(half, rank),
            keys_own,
            keys_other,
            done,
            parts[1],
            scratch=[(tokens // 2, half)],
            flops=400_000_000,
        )
    operands = (
        queries,
        *blocks,
        first,
        second,
        lower,
        values_own,
        *values_other,
        jnp.tile(lengths, QH // KVH)[None, :],
    )
    send, keep = (
        call(
            functools.partial(attend_kernel, sent),
            vmem(HD + 16, HD),
            *operands,
            scratch=[(2 * tokens, QH // KVH * rows)],
            flops=1_500_000_000,
        )
        for sent in (True, False)
    )
    return call(merge_kernel, vmem(1, rows, 1, half * 4), keep, swap(send, "tok", 2))


def solution(mesh):
    paired = (mesh.shape["tok"], mesh.shape["lay"], mesh.shape["head"]) == (4, 2, 2)
    body = paired_body if paired else spread_body
    return jax.shard_map(
        body,
        mesh=mesh,
        in_specs=(
            P("lay", ("groups", "tok"), "head"),
            P("lay", ("groups", "tok"), "head"),
            P("lay", "groups", "head"),
            P(("groups", "tok"), None),
            P("groups"),
        ),
        out_specs=P("lay", "groups", "head", "tok"),
        check_vma=False,
    )
```

```python
import functools
import math

import jax
import jax.numpy as jnp
from jax import lax
from jax.experimental import pallas as pl
from jax.experimental.pallas import tpu as pltpu
from jax.sharding import PartitionSpec as P

KVH = 8
HD = 128
QH = 64
ITERS = 2

NEG = -1e30
HIGHEST = lax.Precision.HIGHEST


def product(left, right, dims):
    return lax.dot_general(
        left, right, (dims, ((), ())), precision=HIGHEST, preferred_element_type=jnp.float32
    )


def diagonal_inverse(tile, step=8):
    size = tile.shape[0]
    rows = lax.broadcasted_iota(jnp.int32, (size, 2 * size), 0)
    cols = lax.broadcasted_iota(jnp.int32, (size, 2 * size), 1)
    state = jnp.concatenate([tile, jnp.zeros_like(tile)], axis=1)
    state = state + jnp.where(cols == rows + size, 1.0, 0.0)
    done = []
    for start in range(0, size, step):
        col = [
            jnp.broadcast_to(state[:, start + i : start + i + 1], state.shape) for i in range(step)
        ]
        row = [state[i : i + 1, :] for i in range(step)]
        state = state[step:]
        for i in range(step):
            pivot = col[i][i : i + 1, :]
            inverse = 1.0 / pivot
            for k in range(i + 1, step):
                ratio = col[i][k : k + 1, :] * inverse
                row[k] = row[k] - ratio * row[i]
                col[k] = col[k] - ratio * col[i]
            if start + step < size:
                state = state - col[i][step:] * (row[i] * inverse)
            done.append(row[i] * lax.rsqrt(pivot))
    return jnp.concatenate(done)[:, size:]


def vmem(*shape):
    return jax.ShapeDtypeStruct(shape, jnp.float32)


def call(kernel, out_shape, *args, scratch=(), flops=0):
    spec = pl.BlockSpec(memory_space=pltpu.VMEM)
    single = not isinstance(out_shape, (tuple, list))
    moved = sum(4 * math.prod(a.shape) for a in (*args, *((out_shape,) if single else out_shape)))
    return pl.pallas_call(
        kernel,
        out_shape=out_shape,
        in_specs=[spec] * len(args),
        out_specs=spec if single else [spec] * len(out_shape),
        scratch_shapes=[pltpu.VMEM(s, jnp.float32) for s in scratch],
        compiler_params=pltpu.CompilerParams(vmem_limit_bytes=40 << 20),
        cost_estimate=pl.CostEstimate(flops=flops, bytes_accessed=moved, transcendentals=0),
    )(*args)


def whole_gram(own_ref, part_refs, gram_ref):
    if not part_refs:
        gram_ref[...] = own_ref[...]
        return
    lay, head = lax.axis_index("lay"), lax.axis_index("head")
    rows = own_ref.shape[0]
    for i, ref in enumerate((own_ref, *part_refs)):
        at = (2 * (head ^ (i // 2)) + (lay ^ (i % 2))) * rows
        gram_ref[pl.ds(pl.multiple_of(at, rows), rows), :] = ref[...]


def factor_kernel(own_ref, *refs):
    *part_refs, out_ref, gram_ref, tile_ref, cross_ref = refs
    whole_gram(own_ref, part_refs, gram_ref)
    half = tile_ref.shape[0]
    low, high = pl.ds(0, half), pl.ds(half, half)

    @pl.loop(0, 2)
    def _(i):
        here = pl.ds(pl.multiple_of(i * half, half), half)
        tile_ref[...] = diagonal_inverse(gram_ref[here, here])
        out_ref[here, here] = tile_ref[...]

        @pl.when(i == 0)
        def _():
            panel = product(tile_ref[...], gram_ref[low, high], ((1,), (0,)))
            gram_ref[high, high] = gram_ref[high, high] - product(panel, panel, ((0,), (0,)))
            cross_ref[...] = product(panel, tile_ref[...], ((0,), (0,)))
            out_ref[low, high] = jnp.zeros((half, half), jnp.float32)

        @pl.when(i == 1)
        def _():
            out_ref[high, low] = -product(tile_ref[...], cross_ref[...], ((1,), (0,)))


def factor_low_kernel(own_ref, *refs):
    *part_refs, tile_ref, cross_ref, left_ref, gram_ref = refs
    whole_gram(own_ref, part_refs, gram_ref)
    half = tile_ref.shape[0]
    low, high = pl.ds(0, half), pl.ds(half, half)
    tile_ref[...] = diagonal_inverse(gram_ref[low, low])
    panel = product(tile_ref[...], gram_ref[low, high], ((1,), (0,)))
    left_ref[...] = gram_ref[high, high] - product(panel, panel, ((0,), (0,)))
    cross_ref[...] = product(panel, tile_ref[...], ((0,), (0,)))


def factor_high_kernel(tile_ref, cross_ref, left_ref, out_ref):
    half = tile_ref.shape[0]
    low, high = pl.ds(0, half), pl.ds(half, half)
    out_ref[low, low] = tile_ref[...]
    out_ref[low, high] = jnp.zeros((half, half), jnp.float32)
    out_ref[high, high] = diagonal_inverse(left_ref[...])
    out_ref[high, low] = -product(out_ref[high, high], cross_ref[...], ((1,), (0,)))


FACTOR_FLOPS = 1_000_000_000


def inverse_factor(*parts):
    rank = parts[0].shape[1]
    half = rank // 2
    return call(
        factor_kernel,
        vmem(rank, rank),
        *parts,
        scratch=[(rank, rank), (half, half), (half, half)],
        flops=FACTOR_FLOPS,
    )


def inverse_factor_low(*parts):
    rank = parts[0].shape[1]
    half = rank // 2
    return call(
        factor_low_kernel, [vmem(half, half)] * 3, *parts, scratch=[(rank, rank)], flops=FACTOR_FLOPS
    )


def inverse_factor_high(*halves):
    rank = 2 * halves[0].shape[0]
    return call(factor_high_kernel, vmem(rank, rank), *halves, flops=FACTOR_FLOPS)


def distances(axis):
    size = lax.axis_size(axis)
    return [1 << i for i in range(size.bit_length() - 1)]


def side(axis, distance):
    return lax.axis_index(axis) // distance % 2


def swap(x, axis, distance):
    pairs = [(i, i ^ distance) for i in range(lax.axis_size(axis))]
    return lax.ppermute(x, axis, pairs)


def halve(x, axis, distance):
    half = x.shape[0] // 2
    mine = side(axis, distance)
    keep = lax.dynamic_slice_in_dim(x, mine * half, half, 0)
    send = lax.dynamic_slice_in_dim(x, (1 - mine) * half, half, 0)
    return keep + swap(send, axis, distance)


def double(x, axis, distance):
    other = swap(x, axis, distance)
    first = side(axis, distance) == 0
    return jnp.concatenate([jnp.where(first, x, other), jnp.where(first, other, x)])


def summed_rows(x, hops):
    for hop in hops:
        x = halve(x, *hop)
    for hop in reversed(hops):
        x = double(x, *hop)
    return x


def spread_body(keys, values, queries, start_block, lengths):
    _, tok_dev, kv_dev = keys.shape
    keys, values = keys[0], values[0]
    rank = start_block.shape[1]
    rows = queries.shape[1]
    local_heads = queries.shape[2] // HD
    group = QH // KVH
    kv_local = kv_dev // HD
    tok_hops = [("tok", d) for d in distances("tok")]
    wide_hops = [("head", d) for d in distances("head")] + [("lay", d) for d in distances("lay")]

    def whole_gram(block):
        share = rank
        at = 0
        for axis, distance in reversed(wide_hops):
            share //= 2
            at = at + side(axis, distance) * share
        part = lax.dynamic_slice_in_dim(block, at, share, 1)
        gram = product(part, block, ((0,), (0,)))
        for hop in tok_hops:
            gram = gram + swap(gram, *hop)
        for hop in wide_hops:
            gram = double(gram, *hop)
        return gram

    def project(block):
        return summed_rows(product(keys, block, ((0,), (0,))), tok_hops)

    def mix(coef):
        return summed_rows(product(keys, coef, ((1,), (0,))), wide_hops)

    block = start_block
    for step in range(ITERS):
        lower = inverse_factor(whole_gram(block))
        block = product(mix(project(block)), lower, ((1,), (1,)))
    lower = inverse_factor(whole_gram(block))
    coef = product(project(block), lower, ((1,), (1,)))
    basis = product(block, lower, ((1,), (1,)))

    quer = queries.reshape(rows, kv_local, group, HD)
    factor = coef.reshape(kv_local, HD, rank)
    reduced = jnp.einsum("bgid,gdr->gibr", quer, factor, precision=HIGHEST) / math.sqrt(HD)
    reduced = reduced.reshape(kv_local, group * rows, rank)
    scores = jnp.einsum("tr,gxr->tgx", basis, reduced, precision=HIGHEST)
    position = lax.axis_index("tok") * tok_dev + jnp.arange(tok_dev, dtype=jnp.int32)
    valid = position[:, None] < lengths[None, :]
    valid = jnp.tile(valid, (1, group))[:, None, :]
    peak = jnp.max(jnp.where(valid, scores, NEG), axis=0)
    weight = jnp.where(valid, jnp.exp(scores - peak[None]), 0.0)
    total = jnp.sum(weight, axis=0)
    vals = values.reshape(tok_dev, kv_local, HD)
    summed = jnp.einsum("tgx,tgd->gxd", weight, vals, precision=HIGHEST)
    peak = peak.reshape(local_heads, rows)
    total = total.reshape(local_heads, rows)
    summed = summed.reshape(local_heads, rows, HD)

    share = local_heads // lax.axis_size("tok")
    peak, total, summed = jax.tree.map(
        lambda a: a.reshape((-1, share) + a.shape[1:]), (peak, total, summed)
    )

    def pack(part):
        top, tot, acc = part
        blank = jnp.zeros(top.shape[:-1] + (HD - 2 * rows,), jnp.float32)
        extra = jnp.concatenate([top, tot, blank], axis=-1).reshape(-1, HD)
        return jnp.concatenate([acc.reshape(-1, HD), extra])

    def unpack(buffer, like):
        count = like[0].shape[0] * share
        extra = buffer[count * rows :]
        return (
            extra[:, :rows].reshape(like[0].shape),
            extra[:, rows : 2 * rows].reshape(like[0].shape),
            buffer[: count * rows].reshape(like[2].shape),
        )

    state = (peak, total, summed)
    for hop in tok_hops:
        mine = side(*hop)
        pairs = jax.tree.map(lambda a: a.reshape((-1, 2) + a.shape[1:]), state)
        keep = jax.tree.map(lambda a: lax.dynamic_index_in_dim(a, mine, 1, False), pairs)
        send = jax.tree.map(lambda a: lax.dynamic_index_in_dim(a, 1 - mine, 1, False), pairs)
        got = unpack(swap(pack(send), *hop), keep)
        top = jnp.maximum(keep[0], got[0])
        one, two = jnp.exp(keep[0] - top), jnp.exp(got[0] - top)
        state = (
            top,
            keep[1] * one + got[1] * two,
            keep[2] * one[..., None] + got[2] * two[..., None],
        )
    result = state[2][0] / state[1][0][..., None]
    return result.transpose(1, 0, 2).reshape(1, rows, 1, share * HD)


def pair_sides():
    return side("tok", 1), side("tok", 2), lax.axis_index("lay"), lax.axis_index("head")


def lanes(index, size=HD):
    return pl.ds(pl.multiple_of(index * size, size), size)


def gram_share(block_ref, scratch_ref, out_ref):
    _, _, lay, head = pair_sides()
    rows, half = out_ref.shape[0], scratch_ref.shape[0]
    scratch_ref[...] = product(block_ref[:, lanes(head, half)], block_ref[...], ((0,), (0,)))
    out_ref[...] = scratch_ref[lanes(lay, rows), :]


def gram_kernel(block_ref, out_ref, scratch_ref):
    gram_share(block_ref, scratch_ref, out_ref)


def start_kernel(keys_ref, block_ref, gram_ref, keep_ref, send_ref, kept_ref, sent_ref):
    del gram_ref
    mine, _, _, _ = pair_sides()
    for i in range(2):
        at = pl.ds(i * HD, HD)
        kept_ref[:, at] = keys_ref[:, lanes(2 * i + mine)]
        sent_ref[:, at] = keys_ref[:, lanes(2 * i + 1 - mine)]
    send_ref[...] = product(sent_ref[...], block_ref[...], ((0,), (0,)))
    keep_ref[...] = product(kept_ref[...], block_ref[...], ((0,), (0,)))


def mix_kernel(sent, own_ref, other_ref, first_ref, second_ref, out_ref):
    mine, _, _, head = pair_sides()
    coef = first_ref[...] + second_ref[...]
    half = own_ref.shape[0] // 2
    rows = lanes(head ^ int(sent), half)
    for keys_ref, piece in ((own_ref, mine), (other_ref, 1 - mine)):
        out_ref[lanes(piece, half), :] = product(keys_ref[rows, :], coef, ((1,), (0,)))


def streams_kernel(first_ref, second_ref, a_keep, a_send, b_keep, b_send):
    mine, _, lay, _ = pair_sides()
    half = first_ref.shape[0] // 2
    quarter, eighth = half // 2, half // 4

    def rows(piece, at, count):
        here = pl.ds(pl.multiple_of(piece * half + at, count), count)
        return first_ref[here, :] + second_ref[here, :]

    for piece in range(2):
        to = pl.ds(piece * eighth, eighth)
        a_keep[to, :] = rows(piece, lay * eighth, eighth)
        a_send[to, :] = rows(piece, (1 - lay) * eighth, eighth)
    b_keep[...] = rows(mine, quarter, quarter)
    b_send[...] = rows(1 - mine, quarter, quarter)


def summed_streams(keep, send, lower):
    got = swap(send, "head", 1)
    quarter = vmem(keep.shape[0] // 4, keep.shape[1])
    a_keep, a_send, b_keep, b_send = call(streams_kernel, [quarter] * 4, keep, got)
    a = a_keep + swap(a_send, "lay", 1)
    b = b_keep + swap(b_send, "tok", 1)
    a, b = a + swap(a, "tok", 1), b + swap(b, "lay", 1)
    a = after(a, lower)
    here = jnp.concatenate([a, b])
    return here, (swap(a, "lay", 1), swap(b, "tok", 1))


def stack_rows(far, beside, size):
    _, _, lay, head = pair_sides()
    count = size // 2
    first = (head ^ far) * size
    return first + (lay ^ beside) * (count // 2), first + count


def project_stack(far, beside, own_ref, other_ref, block_ref, rows_ref):
    mine, _, _, _ = pair_sides()
    size = block_ref.shape[0]
    half, quarter = size // 2, size // 4
    low, high = stack_rows(far, beside, size)
    low = pl.ds(pl.multiple_of(low, quarter), quarter)
    rows_ref[lanes(mine, quarter), :] = own_ref[low, :]
    rows_ref[lanes(1 - mine, quarter), :] = other_ref[low, :]
    high = pl.ds(pl.multiple_of(high, half), half)
    rows_ref[pl.ds(half, half), :] = (other_ref if beside else own_ref)[high, :]
    return product(rows_ref[...], block_ref[...], ((0,), (0,)))


def stack_kernel(far, beside, stack_ref, lower_ref, own_ref, other_ref, *refs):
    *part_refs, block_ref, gram_ref, proj_ref, rows_ref, scratch_ref = refs
    block_ref[...] = product(stack_ref[...], lower_ref[...], ((1,), (1,)))
    gram_share(block_ref, scratch_ref, gram_ref)
    proj_ref[...] = project_stack(far, beside, own_ref, other_ref, block_ref, rows_ref)
    for part_ref, ref in zip(part_refs, (gram_ref, proj_ref)):
        ref[...] += part_ref[...]


def last_stack_kernel(stack_ref, lower_ref, part_ref, block_ref, gram_ref, scratch_ref):
    block_ref[...] = product(stack_ref[...], lower_ref[...], ((1,), (1,)))
    gram_share(block_ref, scratch_ref, gram_ref)
    gram_ref[...] += part_ref[...]


def project_kernel(own_ref, other_ref, block_ref, part_ref, proj_ref, rows_ref):
    proj_ref[...] = part_ref[...] + project_stack(1, 1, own_ref, other_ref, block_ref, rows_ref)


def attend_kernel(sent, query_ref, *refs):
    *block_refs, first_ref, second_ref, lower_ref, own_ref, low_ref, high_ref, length_ref = refs[:-2]
    out_ref, score_ref = refs[-2:]
    mine, upper, _, _ = pair_sides()
    which = upper ^ int(sent)
    tokens = own_ref.shape[1]
    half, width = tokens // 2, length_ref.shape[1]
    local = lanes(which)
    coef = product(first_ref[local, :] + second_ref[local, :], lower_ref[...], ((1,), (1,)))
    reduced = product(query_ref[lanes(which, width), :], coef, ((1,), (0,))) / math.sqrt(HD)
    reduced = product(reduced, lower_ref[...], ((1,), (0,)))
    for i, block_ref in enumerate(block_refs):
        far, beside = i % 2, i // 2
        part = product(block_ref[...], reduced, ((1,), (1,)))
        low, high = stack_rows(far, beside, half)
        quarter = half // 4
        for piece in range(2):
            to = pl.multiple_of((piece ^ mine) * tokens + low, quarter)
            score_ref[pl.ds(to, quarter), :] = part[piece * quarter : (piece + 1) * quarter]
        to = pl.multiple_of(beside * tokens + high, half // 2)
        score_ref[pl.ds(to, half // 2), :] = part[half // 2 :]
    scores = score_ref[...]
    at = lax.broadcasted_iota(jnp.int32, (tokens, width), 0)
    tok = lax.axis_index("tok")
    valid = jnp.concatenate(
        [(tok ^ piece) * tokens + at < length_ref[...] for piece in range(2)]
    )
    peak = jnp.max(jnp.where(valid, scores, NEG), axis=0, keepdims=True)
    weight = jnp.where(valid, jnp.exp(scores - peak), 0.0)
    total = jnp.sum(weight, axis=0, keepdims=True)
    other = jnp.where(which == 0, low_ref[...], high_ref[...])
    acc = product(own_ref[local, :], weight[:tokens], ((1,), (0,)))
    out_ref[pl.ds(0, HD), :] = acc + product(other, weight[tokens:], ((1,), (0,)))
    out_ref[pl.ds(HD, 8), :] = jnp.broadcast_to(peak, (8, width))
    out_ref[pl.ds(HD + 8, 8), :] = jnp.broadcast_to(total, (8, width))


def merge_kernel(first_ref, second_ref, out_ref):
    top = jnp.maximum(first_ref[pl.ds(HD, 1), :], second_ref[pl.ds(HD, 1), :])
    one = jnp.exp(first_ref[pl.ds(HD, 1), :] - top)
    two = jnp.exp(second_ref[pl.ds(HD, 1), :] - top)
    total = first_ref[pl.ds(HD + 8, 1), :] * one + second_ref[pl.ds(HD + 8, 1), :] * two
    acc = first_ref[pl.ds(0, HD), :] * one + second_ref[pl.ds(0, HD), :] * two
    out_ref[...] = (acc / total).T


def gathered(share):
    beside = swap(share, "lay", 1)
    return share, beside, swap(share, "head", 1), swap(beside, "head", 1)


def after(x, *others):
    return lax.optimization_barrier((x, *others))[0]


def split_kernel(values_ref, query_ref, kept_ref, first_ref, second_ref, order_ref):
    mine, _, _, _ = pair_sides()
    rows, group = query_ref.shape[0], QH // KVH
    for i, ref in enumerate((first_ref, second_ref)):
        for k in range(group):
            order_ref[pl.ds(i * rows * group + k, rows, stride=group), :] = query_ref[
                :, lanes((2 * i + mine) * group + k)
            ]
        kept_ref[pl.ds(i * HD, HD), :] = values_ref[:, lanes(2 * i + mine)].T
        ref[...] = values_ref[:, lanes(2 * i + 1 - mine)].T


def paired_body(keys, values, queries, start_block, lengths):
    _, tokens, width = keys.shape
    keys, values, queries = keys[0], values[0], queries[0]
    rank = start_block.shape[1]
    rows = queries.shape[0]
    half, share = width // 2, rank // 4

    gram = call(
        gram_kernel,
        vmem(share, rank),
        start_block,
        scratch=[(rank // 2, rank)],
        flops=400_000_000,
    )
    keep, send, keys_own, keys_send = call(
        start_kernel,
        [vmem(half, rank)] * 2 + [vmem(tokens, half)] * 2,
        keys,
        start_block,
        gram,
        flops=900_000_000,
    )
    gram = gram + swap(gram, "tok", 1)
    proj = keep + swap(after(send, gram), "tok", 1)
    group = QH // KVH
    values_own, *values_send, ordered = call(
        split_kernel,
        [vmem(half, tokens)] + [vmem(HD, tokens)] * 2 + [vmem(2 * rows * group, HD)],
        after(values, proj),
        queries,
    )
    values_other = []
    lower = None
    for step in range(ITERS + 1):
        gram = gram + swap(gram, "tok", 2)
        last = step == ITERS
        if last:
            proj, gram = lax.optimization_barrier((proj, gram))
        elif step == 0:
            proj = after(proj, gram)
            if step == 0:
                keys_other = swap(after(keys_send, proj), "tok", 1)
        first, second = proj, swap(proj, "tok", 2)
        parts = gathered(gram)
        if step > 0:
            ready = parts[1] if last else gram
            values_other.append(swap(after(values_send[step - 1], proj, ready), "tok", 1))
        if step == 0 or last:
            lower = inverse_factor(after(parts[0], values_own), *parts[1:])
            first = after(first, lower)
        else:
            halves = inverse_factor_low(*parts)
            first = after(first, halves[0], *values_other)
            lower = inverse_factor_high(*halves)
        if last:
            break
        mix = (keys_own, keys_other, first, second)
        z_send, z_keep = (
            call(functools.partial(mix_kernel, sent), vmem(tokens, rank), *mix, flops=400_000_000)
            for sent in (True, False)
        )
        here, there = summed_streams(z_keep, z_send, lower)
        block, parts = vmem(tokens // 2, rank), ()
        blocks = []
        stacks = [here, swap(here, "head", 1)]
        for i in range(3):
            if i == 2:
                there = jnp.concatenate([after(x, *parts) for x in there])
                stacks += [there, swap(there, "head", 1)]
            done, *parts = call(
                functools.partial(stack_kernel, i % 2, i // 2),
                [block, vmem(share, rank), vmem(half, rank)],
                stacks[i],
                lower,
                keys_own,
                keys_other,
                *parts,
                scratch=[(tokens // 2, half), (rank // 2, rank)],
                flops=900_000_000,
            )
            blocks.append(done)
        done, gram = call(
            last_stack_kernel,
            [block, vmem(share, rank)],
            stacks[3],
            lower,
            parts[0],
            scratch=[(rank // 2, rank)],
            flops=600_000_000,
        )
        blocks.append(done)
        proj = call(
            project_kernel,
            vmem(half, rank),
            keys_own,
            keys_other,
            done,
            parts[1],
            scratch=[(tokens // 2, half)],
            flops=400_000_000,
        )
    operands = (
        ordered,
        *blocks,
        first,
        second,
        lower,
        values_own,
        *values_other,
        jnp.repeat(lengths, group)[None, :],
    )
    send, keep = (
        call(
            functools.partial(attend_kernel, sent),
            vmem(HD + 16, HD),
            *operands,
            scratch=[(2 * tokens, group * rows)],
            flops=1_500_000_000,
        )
        for sent in (True, False)
    )
    result = call(merge_kernel, vmem(group * rows, HD), keep, swap(send, "tok", 2))
    return result.reshape(1, rows, 1, group * HD)


def solution(mesh):
    paired = (mesh.shape["tok"], mesh.shape["lay"], mesh.shape["head"]) == (4, 2, 2)
    body = paired_body if paired else spread_body
    return jax.shard_map(
        body,
        mesh=mesh,
        in_specs=(
            P("lay", ("groups", "tok"), "head"),
            P("lay", ("groups", "tok"), "head"),
            P("lay", "groups", "head"),
            P(("groups", "tok"), None),
            P("groups"),
        ),
        out_specs=P("lay", "groups", "head", "tok"),
        check_vma=False,
    )
```

```python
import functools
import math

import jax
import jax.numpy as jnp
from jax import lax
from jax.experimental import pallas as pl
from jax.experimental.pallas import tpu as pltpu
from jax.sharding import PartitionSpec as P

KVH = 8
HD = 128
QH = 64
ITERS = 2

NEG = -1e30
HIGHEST = lax.Precision.HIGHEST


def product(left, right, dims):
    return lax.dot_general(
        left, right, (dims, ((), ())), precision=HIGHEST, preferred_element_type=jnp.float32
    )


def diagonal_inverse(tile, step=8):
    size = tile.shape[0]
    rows = lax.broadcasted_iota(jnp.int32, (size, 2 * size), 0)
    cols = lax.broadcasted_iota(jnp.int32, (size, 2 * size), 1)
    state = jnp.concatenate([tile, jnp.zeros_like(tile)], axis=1)
    state = state + jnp.where(cols == rows + size, 1.0, 0.0)
    done = []
    for start in range(0, size, step):
        col = [
            jnp.broadcast_to(state[:, start + i : start + i + 1], state.shape) for i in range(step)
        ]
        row = [state[i : i + 1, :] for i in range(step)]
        state = state[step:]
        for i in range(step):
            pivot = col[i][i : i + 1, :]
            inverse = 1.0 / pivot
            for k in range(i + 1, step):
                ratio = col[i][k : k + 1, :] * inverse
                row[k] = row[k] - ratio * row[i]
                col[k] = col[k] - ratio * col[i]
            if start + step < size:
                state = state - col[i][step:] * (row[i] * inverse)
            done.append(row[i] * lax.rsqrt(pivot))
    return jnp.concatenate(done)[:, size:]


def vmem(*shape):
    return jax.ShapeDtypeStruct(shape, jnp.float32)


def call(kernel, out_shape, *args, scratch=(), flops=0):
    spec = pl.BlockSpec(memory_space=pltpu.VMEM)
    single = not isinstance(out_shape, (tuple, list))
    moved = sum(4 * math.prod(a.shape) for a in (*args, *((out_shape,) if single else out_shape)))
    return pl.pallas_call(
        kernel,
        out_shape=out_shape,
        in_specs=[spec] * len(args),
        out_specs=spec if single else [spec] * len(out_shape),
        scratch_shapes=[pltpu.VMEM(s, jnp.float32) for s in scratch],
        compiler_params=pltpu.CompilerParams(vmem_limit_bytes=40 << 20),
        cost_estimate=pl.CostEstimate(flops=flops, bytes_accessed=moved, transcendentals=0),
    )(*args)


def whole_gram(own_ref, part_refs, gram_ref):
    if not part_refs:
        gram_ref[...] = own_ref[...]
        return
    lay, head = lax.axis_index("lay"), lax.axis_index("head")
    rows = own_ref.shape[0]
    for i, ref in enumerate((own_ref, *part_refs)):
        at = (2 * (head ^ (i // 2)) + (lay ^ (i % 2))) * rows
        gram_ref[pl.ds(pl.multiple_of(at, rows), rows), :] = ref[...]


def factor_kernel(own_ref, *refs):
    *part_refs, out_ref, gram_ref, tile_ref, cross_ref = refs
    whole_gram(own_ref, part_refs, gram_ref)
    half = tile_ref.shape[0]
    low, high = pl.ds(0, half), pl.ds(half, half)

    @pl.loop(0, 2)
    def _(i):
        here = pl.ds(pl.multiple_of(i * half, half), half)
        tile_ref[...] = diagonal_inverse(gram_ref[here, here])
        out_ref[here, here] = tile_ref[...]

        @pl.when(i == 0)
        def _():
            panel = product(tile_ref[...], gram_ref[low, high], ((1,), (0,)))
            gram_ref[high, high] = gram_ref[high, high] - product(panel, panel, ((0,), (0,)))
            cross_ref[...] = product(panel, tile_ref[...], ((0,), (0,)))
            out_ref[low, high] = jnp.zeros((half, half), jnp.float32)

        @pl.when(i == 1)
        def _():
            out_ref[high, low] = -product(tile_ref[...], cross_ref[...], ((1,), (0,)))


def factor_low_kernel(own_ref, *refs):
    *part_refs, tile_ref, cross_ref, left_ref, gram_ref = refs
    whole_gram(own_ref, part_refs, gram_ref)
    half = tile_ref.shape[0]
    low, high = pl.ds(0, half), pl.ds(half, half)
    tile_ref[...] = diagonal_inverse(gram_ref[low, low])
    panel = product(tile_ref[...], gram_ref[low, high], ((1,), (0,)))
    left_ref[...] = gram_ref[high, high] - product(panel, panel, ((0,), (0,)))
    cross_ref[...] = product(panel, tile_ref[...], ((0,), (0,)))


def factor_high_kernel(tile_ref, cross_ref, left_ref, out_ref):
    half = tile_ref.shape[0]
    low, high = pl.ds(0, half), pl.ds(half, half)
    out_ref[low, low] = tile_ref[...]
    out_ref[low, high] = jnp.zeros((half, half), jnp.float32)
    out_ref[high, high] = diagonal_inverse(left_ref[...])
    out_ref[high, low] = -product(out_ref[high, high], cross_ref[...], ((1,), (0,)))


FACTOR_FLOPS = 1_000_000_000


def inverse_factor(*parts):
    rank = parts[0].shape[1]
    half = rank // 2
    return call(
        factor_kernel,
        vmem(rank, rank),
        *parts,
        scratch=[(rank, rank), (half, half), (half, half)],
        flops=FACTOR_FLOPS,
    )


def inverse_factor_low(*parts):
    rank = parts[0].shape[1]
    half = rank // 2
    return call(
        factor_low_kernel, [vmem(half, half)] * 3, *parts, scratch=[(rank, rank)], flops=FACTOR_FLOPS
    )


def inverse_factor_high(*halves):
    rank = 2 * halves[0].shape[0]
    return call(factor_high_kernel, vmem(rank, rank), *halves, flops=FACTOR_FLOPS)


def distances(axis):
    size = lax.axis_size(axis)
    return [1 << i for i in range(size.bit_length() - 1)]


def side(axis, distance):
    return lax.axis_index(axis) // distance % 2


def swap(x, axis, distance):
    pairs = [(i, i ^ distance) for i in range(lax.axis_size(axis))]
    return lax.ppermute(x, axis, pairs)


def halve(x, axis, distance):
    half = x.shape[0] // 2
    mine = side(axis, distance)
    keep = lax.dynamic_slice_in_dim(x, mine * half, half, 0)
    send = lax.dynamic_slice_in_dim(x, (1 - mine) * half, half, 0)
    return keep + swap(send, axis, distance)


def double(x, axis, distance):
    other = swap(x, axis, distance)
    first = side(axis, distance) == 0
    return jnp.concatenate([jnp.where(first, x, other), jnp.where(first, other, x)])


def summed_rows(x, hops):
    for hop in hops:
        x = halve(x, *hop)
    for hop in reversed(hops):
        x = double(x, *hop)
    return x


def spread_body(keys, values, queries, start_block, lengths):
    _, tok_dev, kv_dev = keys.shape
    keys, values = keys[0], values[0]
    rank = start_block.shape[1]
    rows = queries.shape[1]
    local_heads = queries.shape[2] // HD
    group = QH // KVH
    kv_local = kv_dev // HD
    tok_hops = [("tok", d) for d in distances("tok")]
    wide_hops = [("head", d) for d in distances("head")] + [("lay", d) for d in distances("lay")]

    def whole_gram(block):
        share = rank
        at = 0
        for axis, distance in reversed(wide_hops):
            share //= 2
            at = at + side(axis, distance) * share
        part = lax.dynamic_slice_in_dim(block, at, share, 1)
        gram = product(part, block, ((0,), (0,)))
        for hop in tok_hops:
            gram = gram + swap(gram, *hop)
        for hop in wide_hops:
            gram = double(gram, *hop)
        return gram

    def project(block):
        return summed_rows(product(keys, block, ((0,), (0,))), tok_hops)

    def mix(coef):
        return summed_rows(product(keys, coef, ((1,), (0,))), wide_hops)

    block = start_block
    for step in range(ITERS):
        lower = inverse_factor(whole_gram(block))
        block = product(mix(project(block)), lower, ((1,), (1,)))
    lower = inverse_factor(whole_gram(block))
    coef = product(project(block), lower, ((1,), (1,)))
    basis = product(block, lower, ((1,), (1,)))

    quer = queries.reshape(rows, kv_local, group, HD)
    factor = coef.reshape(kv_local, HD, rank)
    reduced = jnp.einsum("bgid,gdr->gibr", quer, factor, precision=HIGHEST) / math.sqrt(HD)
    reduced = reduced.reshape(kv_local, group * rows, rank)
    scores = jnp.einsum("tr,gxr->tgx", basis, reduced, precision=HIGHEST)
    position = lax.axis_index("tok") * tok_dev + jnp.arange(tok_dev, dtype=jnp.int32)
    valid = position[:, None] < lengths[None, :]
    valid = jnp.tile(valid, (1, group))[:, None, :]
    peak = jnp.max(jnp.where(valid, scores, NEG), axis=0)
    weight = jnp.where(valid, jnp.exp(scores - peak[None]), 0.0)
    total = jnp.sum(weight, axis=0)
    vals = values.reshape(tok_dev, kv_local, HD)
    summed = jnp.einsum("tgx,tgd->gxd", weight, vals, precision=HIGHEST)
    peak = peak.reshape(local_heads, rows)
    total = total.reshape(local_heads, rows)
    summed = summed.reshape(local_heads, rows, HD)

    share = local_heads // lax.axis_size("tok")
    peak, total, summed = jax.tree.map(
        lambda a: a.reshape((-1, share) + a.shape[1:]), (peak, total, summed)
    )

    def pack(part):
        top, tot, acc = part
        blank = jnp.zeros(top.shape[:-1] + (HD - 2 * rows,), jnp.float32)
        extra = jnp.concatenate([top, tot, blank], axis=-1).reshape(-1, HD)
        return jnp.concatenate([acc.reshape(-1, HD), extra])

    def unpack(buffer, like):
        count = like[0].shape[0] * share
        extra = buffer[count * rows :]
        return (
            extra[:, :rows].reshape(like[0].shape),
            extra[:, rows : 2 * rows].reshape(like[0].shape),
            buffer[: count * rows].reshape(like[2].shape),
        )

    state = (peak, total, summed)
    for hop in tok_hops:
        mine = side(*hop)
        pairs = jax.tree.map(lambda a: a.reshape((-1, 2) + a.shape[1:]), state)
        keep = jax.tree.map(lambda a: lax.dynamic_index_in_dim(a, mine, 1, False), pairs)
        send = jax.tree.map(lambda a: lax.dynamic_index_in_dim(a, 1 - mine, 1, False), pairs)
        got = unpack(swap(pack(send), *hop), keep)
        top = jnp.maximum(keep[0], got[0])
        one, two = jnp.exp(keep[0] - top), jnp.exp(got[0] - top)
        state = (
            top,
            keep[1] * one + got[1] * two,
            keep[2] * one[..., None] + got[2] * two[..., None],
        )
    result = state[2][0] / state[1][0][..., None]
    return result.transpose(1, 0, 2).reshape(1, rows, 1, share * HD)


def pair_sides():
    return side("tok", 1), side("tok", 2), lax.axis_index("lay"), lax.axis_index("head")


def lanes(index, size=HD):
    return pl.ds(pl.multiple_of(index * size, size), size)


def gram_share(block_ref, scratch_ref, out_ref):
    _, _, lay, head = pair_sides()
    rows, half = out_ref.shape[0], scratch_ref.shape[0]
    scratch_ref[...] = product(block_ref[:, lanes(head, half)], block_ref[...], ((0,), (0,)))
    out_ref[...] = scratch_ref[lanes(lay, rows), :]


def gram_kernel(block_ref, out_ref, scratch_ref):
    gram_share(block_ref, scratch_ref, out_ref)


def start_kernel(keys_ref, block_ref, gram_ref, keep_ref, send_ref, kept_ref, sent_ref):
    del gram_ref
    mine, _, _, _ = pair_sides()
    for i in range(2):
        at = pl.ds(i * HD, HD)
        kept_ref[:, at] = keys_ref[:, lanes(2 * i + mine)]
        sent_ref[:, at] = keys_ref[:, lanes(2 * i + 1 - mine)]
    send_ref[...] = product(sent_ref[...], block_ref[...], ((0,), (0,)))
    keep_ref[...] = product(kept_ref[...], block_ref[...], ((0,), (0,)))


def mix_kernel(sent, own_ref, other_ref, first_ref, second_ref, out_ref):
    mine, _, _, head = pair_sides()
    coef = first_ref[...] + second_ref[...]
    half = own_ref.shape[0] // 2
    rows = lanes(head ^ int(sent), half)
    for keys_ref, piece in ((own_ref, mine), (other_ref, 1 - mine)):
        out_ref[lanes(piece, half), :] = product(keys_ref[rows, :], coef, ((1,), (0,)))


def streams_kernel(first_ref, second_ref, a_keep, a_send, b_keep, b_send):
    mine, _, lay, _ = pair_sides()
    half = first_ref.shape[0] // 2
    quarter, eighth = half // 2, half // 4

    def rows(piece, at, count):
        here = pl.ds(pl.multiple_of(piece * half + at, count), count)
        return first_ref[here, :] + second_ref[here, :]

    for piece in range(2):
        to = pl.ds(piece * eighth, eighth)
        a_keep[to, :] = rows(piece, lay * eighth, eighth)
        a_send[to, :] = rows(piece, (1 - lay) * eighth, eighth)
    b_keep[...] = rows(mine, quarter, quarter)
    b_send[...] = rows(1 - mine, quarter, quarter)


def summed_streams(keep, send, lower):
    got = swap(send, "head", 1)
    quarter = vmem(keep.shape[0] // 4, keep.shape[1])
    a_keep, a_send, b_keep, b_send = call(streams_kernel, [quarter] * 4, keep, got)
    a = a_keep + swap(a_send, "lay", 1)
    b = b_keep + swap(b_send, "tok", 1)
    a, b = a + swap(a, "tok", 1), b + swap(b, "lay", 1)
    a = after(a, lower)
    here = jnp.concatenate([a, b])
    return here, (swap(a, "lay", 1), swap(b, "tok", 1))


def stack_rows(far, beside, size):
    _, _, lay, head = pair_sides()
    count = size // 2
    first = (head ^ far) * size
    return first + (lay ^ beside) * (count // 2), first + count


def project_stack(far, beside, own_ref, other_ref, block_ref, rows_ref):
    mine, _, _, _ = pair_sides()
    size = block_ref.shape[0]
    half, quarter = size // 2, size // 4
    low, high = stack_rows(far, beside, size)
    low = pl.ds(pl.multiple_of(low, quarter), quarter)
    rows_ref[lanes(mine, quarter), :] = own_ref[low, :]
    rows_ref[lanes(1 - mine, quarter), :] = other_ref[low, :]
    high = pl.ds(pl.multiple_of(high, half), half)
    rows_ref[pl.ds(half, half), :] = (other_ref if beside else own_ref)[high, :]
    return product(rows_ref[...], block_ref[...], ((0,), (0,)))


def stack_kernel(far, beside, stack_ref, lower_ref, own_ref, other_ref, *refs):
    *part_refs, block_ref, gram_ref, proj_ref, rows_ref, scratch_ref = refs
    block_ref[...] = product(stack_ref[...], lower_ref[...], ((1,), (1,)))
    gram_share(block_ref, scratch_ref, gram_ref)
    proj_ref[...] = project_stack(far, beside, own_ref, other_ref, block_ref, rows_ref)
    for part_ref, ref in zip(part_refs, (gram_ref, proj_ref)):
        ref[...] += part_ref[...]


def last_stack_kernel(stack_ref, lower_ref, part_ref, block_ref, gram_ref, scratch_ref):
    block_ref[...] = product(stack_ref[...], lower_ref[...], ((1,), (1,)))
    gram_share(block_ref, scratch_ref, gram_ref)
    gram_ref[...] += part_ref[...]


def project_kernel(own_ref, other_ref, block_ref, part_ref, proj_ref, rows_ref):
    proj_ref[...] = part_ref[...] + project_stack(1, 1, own_ref, other_ref, block_ref, rows_ref)


def attend_kernel(sent, query_ref, *refs):
    *block_refs, first_ref, second_ref, lower_ref, own_ref, other_ref, length_ref = refs[:-2]
    out_ref, score_ref = refs[-2:]
    mine, upper, _, _ = pair_sides()
    which = upper ^ int(sent)
    tokens = own_ref.shape[1]
    half, width = tokens // 2, length_ref.shape[1]
    local = lanes(which)
    coef = product(first_ref[local, :] + second_ref[local, :], lower_ref[...], ((1,), (1,)))
    reduced = product(query_ref[lanes(which, width), :], coef, ((1,), (0,))) / math.sqrt(HD)
    reduced = product(reduced, lower_ref[...], ((1,), (0,)))
    for i, block_ref in enumerate(block_refs):
        far, beside = i % 2, i // 2
        part = product(block_ref[...], reduced, ((1,), (1,)))
        low, high = stack_rows(far, beside, half)
        quarter = half // 4
        for piece in range(2):
            to = pl.multiple_of((piece ^ mine) * tokens + low, quarter)
            score_ref[pl.ds(to, quarter), :] = part[piece * quarter : (piece + 1) * quarter]
        to = pl.multiple_of(beside * tokens + high, half // 2)
        score_ref[pl.ds(to, half // 2), :] = part[half // 2 :]
    scores = score_ref[...]
    at = lax.broadcasted_iota(jnp.int32, (tokens, width), 0)
    tok = lax.axis_index("tok")
    valid = jnp.concatenate(
        [(tok ^ piece) * tokens + at < length_ref[...] for piece in range(2)]
    )
    peak = jnp.max(jnp.where(valid, scores, NEG), axis=0, keepdims=True)
    weight = jnp.where(valid, jnp.exp(scores - peak), 0.0)
    total = jnp.sum(weight, axis=0, keepdims=True)
    acc = product(own_ref[local, :], weight[:tokens], ((1,), (0,)))
    out_ref[pl.ds(0, HD), :] = acc + product(other_ref[...], weight[tokens:], ((1,), (0,)))
    out_ref[pl.ds(HD, 8), :] = jnp.broadcast_to(peak, (8, width))
    out_ref[pl.ds(HD + 8, 8), :] = jnp.broadcast_to(total, (8, width))


def merge_kernel(first_ref, second_ref, out_ref):
    top = jnp.maximum(first_ref[pl.ds(HD, 1), :], second_ref[pl.ds(HD, 1), :])
    one = jnp.exp(first_ref[pl.ds(HD, 1), :] - top)
    two = jnp.exp(second_ref[pl.ds(HD, 1), :] - top)
    total = first_ref[pl.ds(HD + 8, 1), :] * one + second_ref[pl.ds(HD + 8, 1), :] * two
    acc = first_ref[pl.ds(0, HD), :] * one + second_ref[pl.ds(0, HD), :] * two
    out_ref[...] = (acc / total).T


def gathered(share):
    beside = swap(share, "lay", 1)
    return share, beside, swap(share, "head", 1), swap(beside, "head", 1)


def after(x, *others):
    return lax.optimization_barrier((x, *others))[0]


def split_kernel(values_ref, query_ref, kept_ref, first_ref, second_ref, order_ref):
    mine, upper, _, _ = pair_sides()
    rows, group = query_ref.shape[0], QH // KVH
    for i, ref in enumerate((first_ref, second_ref)):
        which = upper ^ 1 ^ i
        for k in range(group):
            order_ref[pl.ds(i * rows * group + k, rows, stride=group), :] = query_ref[
                :, lanes((2 * i + mine) * group + k)
            ]
        kept_ref[pl.ds(i * HD, HD), :] = values_ref[:, lanes(2 * i + mine)].T
        ref[...] = values_ref[:, lanes(2 * which + 1 - mine)].T


def paired_body(keys, values, queries, start_block, lengths):
    _, tokens, width = keys.shape
    keys, values, queries = keys[0], values[0], queries[0]
    rank = start_block.shape[1]
    rows = queries.shape[0]
    half, share = width // 2, rank // 4

    gram = call(
        gram_kernel,
        vmem(share, rank),
        start_block,
        scratch=[(rank // 2, rank)],
        flops=400_000_000,
    )
    keep, send, keys_own, keys_send = call(
        start_kernel,
        [vmem(half, rank)] * 2 + [vmem(tokens, half)] * 2,
        keys,
        start_block,
        gram,
        flops=900_000_000,
    )
    gram = gram + swap(gram, "tok", 1)
    proj = keep + swap(after(send, gram), "tok", 1)
    group = QH // KVH
    values_own, *values_send, ordered = call(
        split_kernel,
        [vmem(half, tokens)] + [vmem(HD, tokens)] * 2 + [vmem(2 * rows * group, HD)],
        after(values, proj),
        queries,
    )
    values_other = []
    lower = None
    for step in range(ITERS + 1):
        gram = gram + swap(gram, "tok", 2)
        last = step == ITERS
        if last:
            proj, gram = lax.optimization_barrier((proj, gram))
        elif step == 0:
            proj = after(proj, gram)
            if step == 0:
                keys_other = swap(after(keys_send, proj), "tok", 1)
        first, second = proj, swap(proj, "tok", 2)
        parts = gathered(gram)
        if step > 0:
            ready = parts[1] if last else gram
            values_other.append(swap(after(values_send[step - 1], proj, ready), "tok", 1))
        if step == 0 or last:
            lower = inverse_factor(after(parts[0], values_own), *parts[1:])
            first = after(first, lower)
        else:
            halves = inverse_factor_low(*parts)
            first = after(first, halves[0], *values_other)
            lower = inverse_factor_high(*halves)
        if last:
            break
        mix = (keys_own, keys_other, first, second)
        z_send, z_keep = (
            call(functools.partial(mix_kernel, sent), vmem(tokens, rank), *mix, flops=400_000_000)
            for sent in (True, False)
        )
        here, there = summed_streams(z_keep, z_send, lower)
        block, parts = vmem(tokens // 2, rank), ()
        blocks = []
        stacks = [here, swap(here, "head", 1)]
        for i in range(3):
            if i == 2:
                there = jnp.concatenate([after(x, *parts) for x in there])
                stacks += [there, swap(there, "head", 1)]
            done, *parts = call(
                functools.partial(stack_kernel, i % 2, i // 2),
                [block, vmem(share, rank), vmem(half, rank)],
                stacks[i],
                lower,
                keys_own,
                keys_other,
                *parts,
                scratch=[(tokens // 2, half), (rank // 2, rank)],
                flops=900_000_000,
            )
            blocks.append(done)
        done, gram = call(
            last_stack_kernel,
            [block, vmem(share, rank)],
            stacks[3],
            lower,
            parts[0],
            scratch=[(rank // 2, rank)],
            flops=600_000_000,
        )
        blocks.append(done)
        proj = call(
            project_kernel,
            vmem(half, rank),
            keys_own,
            keys_other,
            done,
            parts[1],
            scratch=[(tokens // 2, half)],
            flops=400_000_000,
        )
    operands = (
        ordered,
        *blocks,
        first,
        second,
        lower,
        values_own,
    )
    row_lengths = jnp.repeat(lengths, group)[None, :]
    send, keep = (
        call(
            functools.partial(attend_kernel, sent),
            vmem(HD + 16, HD),
            *operands,
            other,
            row_lengths,
            scratch=[(2 * tokens, group * rows)],
            flops=1_500_000_000,
        )
        for sent, other in zip((True, False), values_other)
    )
    result = call(merge_kernel, vmem(group * rows, HD), keep, swap(send, "tok", 2))
    return result.reshape(1, rows, 1, group * HD)


def solution(mesh):
    paired = (mesh.shape["tok"], mesh.shape["lay"], mesh.shape["head"]) == (4, 2, 2)
    body = paired_body if paired else spread_body
    return jax.shard_map(
        body,
        mesh=mesh,
        in_specs=(
            P("lay", ("groups", "tok"), "head"),
            P("lay", ("groups", "tok"), "head"),
            P("lay", "groups", "head"),
            P(("groups", "tok"), None),
            P("groups"),
        ),
        out_specs=P("lay", "groups", "head", "tok"),
        check_vma=False,
    )
```

```python
import functools
import math

import jax
import jax.numpy as jnp
from jax import lax
from jax.experimental import pallas as pl
from jax.experimental.pallas import tpu as pltpu
from jax.sharding import PartitionSpec as P

KVH = 8
HD = 128
QH = 64
ITERS = 2

NEG = -1e30
HIGHEST = lax.Precision.HIGHEST


def product(left, right, dims):
    return lax.dot_general(
        left, right, (dims, ((), ())), precision=HIGHEST, preferred_element_type=jnp.float32
    )


def diagonal_inverse(tile, step=8):
    size = tile.shape[0]
    rows = lax.broadcasted_iota(jnp.int32, (size, 2 * size), 0)
    cols = lax.broadcasted_iota(jnp.int32, (size, 2 * size), 1)
    state = jnp.concatenate([tile, jnp.zeros_like(tile)], axis=1)
    state = state + jnp.where(cols == rows + size, 1.0, 0.0)
    done = []
    for start in range(0, size, step):
        col = [
            jnp.broadcast_to(state[:, start + i : start + i + 1], state.shape) for i in range(step)
        ]
        row = [state[i : i + 1, :] for i in range(step)]
        state = state[step:]
        for i in range(step):
            pivot = col[i][i : i + 1, :]
            inverse = 1.0 / pivot
            for k in range(i + 1, step):
                ratio = col[i][k : k + 1, :] * inverse
                row[k] = row[k] - ratio * row[i]
                col[k] = col[k] - ratio * col[i]
            if start + step < size:
                state = state - col[i][step:] * (row[i] * inverse)
            done.append(row[i] * lax.rsqrt(pivot))
    return jnp.concatenate(done)[:, size:]


def vmem(*shape):
    return jax.ShapeDtypeStruct(shape, jnp.float32)


def call(kernel, out_shape, *args, scratch=(), flops=0):
    spec = pl.BlockSpec(memory_space=pltpu.VMEM)
    single = not isinstance(out_shape, (tuple, list))
    moved = sum(4 * math.prod(a.shape) for a in (*args, *((out_shape,) if single else out_shape)))
    return pl.pallas_call(
        kernel,
        out_shape=out_shape,
        in_specs=[spec] * len(args),
        out_specs=spec if single else [spec] * len(out_shape),
        scratch_shapes=[pltpu.VMEM(s, jnp.float32) for s in scratch],
        compiler_params=pltpu.CompilerParams(vmem_limit_bytes=40 << 20),
        cost_estimate=pl.CostEstimate(flops=flops, bytes_accessed=moved, transcendentals=0),
    )(*args)


def whole_gram(own_ref, part_refs, gram_ref):
    if not part_refs:
        gram_ref[...] = own_ref[...]
        return
    lay, head = lax.axis_index("lay"), lax.axis_index("head")
    rows = own_ref.shape[0]
    for i, ref in enumerate((own_ref, *part_refs)):
        at = (2 * (head ^ (i // 2)) + (lay ^ (i % 2))) * rows
        gram_ref[pl.ds(pl.multiple_of(at, rows), rows), :] = ref[...]


def factor_kernel(own_ref, *refs):
    *part_refs, out_ref, gram_ref, tile_ref, cross_ref = refs
    whole_gram(own_ref, part_refs, gram_ref)
    half = tile_ref.shape[0]
    low, high = pl.ds(0, half), pl.ds(half, half)

    @pl.loop(0, 2)
    def _(i):
        here = pl.ds(pl.multiple_of(i * half, half), half)
        tile_ref[...] = diagonal_inverse(gram_ref[here, here])
        out_ref[here, here] = tile_ref[...]

        @pl.when(i == 0)
        def _():
            panel = product(tile_ref[...], gram_ref[low, high], ((1,), (0,)))
            gram_ref[high, high] = gram_ref[high, high] - product(panel, panel, ((0,), (0,)))
            cross_ref[...] = product(panel, tile_ref[...], ((0,), (0,)))
            out_ref[low, high] = jnp.zeros((half, half), jnp.float32)

        @pl.when(i == 1)
        def _():
            out_ref[high, low] = -product(tile_ref[...], cross_ref[...], ((1,), (0,)))


def factor_low_kernel(own_ref, *refs):
    *part_refs, tile_ref, cross_ref, left_ref, gram_ref = refs
    whole_gram(own_ref, part_refs, gram_ref)
    half = tile_ref.shape[0]
    low, high = pl.ds(0, half), pl.ds(half, half)
    tile_ref[...] = diagonal_inverse(gram_ref[low, low])
    panel = product(tile_ref[...], gram_ref[low, high], ((1,), (0,)))
    left_ref[...] = gram_ref[high, high] - product(panel, panel, ((0,), (0,)))
    cross_ref[...] = product(panel, tile_ref[...], ((0,), (0,)))


def factor_high_kernel(tile_ref, cross_ref, left_ref, out_ref):
    half = tile_ref.shape[0]
    low, high = pl.ds(0, half), pl.ds(half, half)
    out_ref[low, low] = tile_ref[...]
    out_ref[low, high] = jnp.zeros((half, half), jnp.float32)
    out_ref[high, high] = diagonal_inverse(left_ref[...])
    out_ref[high, low] = -product(out_ref[high, high], cross_ref[...], ((1,), (0,)))


FACTOR_FLOPS = 1_000_000_000


def inverse_factor(*parts, flops=FACTOR_FLOPS):
    rank = parts[0].shape[1]
    half = rank // 2
    return call(
        factor_kernel,
        vmem(rank, rank),
        *parts,
        scratch=[(rank, rank), (half, half), (half, half)],
        flops=flops,
    )


def inverse_factor_low(*parts):
    rank = parts[0].shape[1]
    half = rank // 2
    return call(
        factor_low_kernel, [vmem(half, half)] * 3, *parts, scratch=[(rank, rank)], flops=FACTOR_FLOPS
    )


def inverse_factor_high(*halves):
    rank = 2 * halves[0].shape[0]
    return call(factor_high_kernel, vmem(rank, rank), *halves, flops=FACTOR_FLOPS)


def distances(axis):
    size = lax.axis_size(axis)
    return [1 << i for i in range(size.bit_length() - 1)]


def side(axis, distance):
    return lax.axis_index(axis) // distance % 2


def swap(x, axis, distance):
    pairs = [(i, i ^ distance) for i in range(lax.axis_size(axis))]
    return lax.ppermute(x, axis, pairs)


def halve(x, axis, distance):
    half = x.shape[0] // 2
    mine = side(axis, distance)
    keep = lax.dynamic_slice_in_dim(x, mine * half, half, 0)
    send = lax.dynamic_slice_in_dim(x, (1 - mine) * half, half, 0)
    return keep + swap(send, axis, distance)


def double(x, axis, distance):
    other = swap(x, axis, distance)
    first = side(axis, distance) == 0
    return jnp.concatenate([jnp.where(first, x, other), jnp.where(first, other, x)])


def summed_rows(x, hops):
    for hop in hops:
        x = halve(x, *hop)
    for hop in reversed(hops):
        x = double(x, *hop)
    return x


def spread_body(keys, values, queries, start_block, lengths):
    _, tok_dev, kv_dev = keys.shape
    keys, values = keys[0], values[0]
    rank = start_block.shape[1]
    rows = queries.shape[1]
    local_heads = queries.shape[2] // HD
    group = QH // KVH
    kv_local = kv_dev // HD
    tok_hops = [("tok", d) for d in distances("tok")]
    wide_hops = [("head", d) for d in distances("head")] + [("lay", d) for d in distances("lay")]

    def whole_gram(block):
        share = rank
        at = 0
        for axis, distance in reversed(wide_hops):
            share //= 2
            at = at + side(axis, distance) * share
        part = lax.dynamic_slice_in_dim(block, at, share, 1)
        gram = product(part, block, ((0,), (0,)))
        for hop in tok_hops:
            gram = gram + swap(gram, *hop)
        for hop in wide_hops:
            gram = double(gram, *hop)
        return gram

    def project(block):
        return summed_rows(product(keys, block, ((0,), (0,))), tok_hops)

    def mix(coef):
        return summed_rows(product(keys, coef, ((1,), (0,))), wide_hops)

    block = start_block
    for step in range(ITERS):
        lower = inverse_factor(whole_gram(block))
        block = product(mix(project(block)), lower, ((1,), (1,)))
    lower = inverse_factor(whole_gram(block))
    coef = product(project(block), lower, ((1,), (1,)))
    basis = product(block, lower, ((1,), (1,)))

    quer = queries.reshape(rows, kv_local, group, HD)
    factor = coef.reshape(kv_local, HD, rank)
    reduced = jnp.einsum("bgid,gdr->gibr", quer, factor, precision=HIGHEST) / math.sqrt(HD)
    reduced = reduced.reshape(kv_local, group * rows, rank)
    scores = jnp.einsum("tr,gxr->tgx", basis, reduced, precision=HIGHEST)
    position = lax.axis_index("tok") * tok_dev + jnp.arange(tok_dev, dtype=jnp.int32)
    valid = position[:, None] < lengths[None, :]
    valid = jnp.tile(valid, (1, group))[:, None, :]
    peak = jnp.max(jnp.where(valid, scores, NEG), axis=0)
    weight = jnp.where(valid, jnp.exp(scores - peak[None]), 0.0)
    total = jnp.sum(weight, axis=0)
    vals = values.reshape(tok_dev, kv_local, HD)
    summed = jnp.einsum("tgx,tgd->gxd", weight, vals, precision=HIGHEST)
    peak = peak.reshape(local_heads, rows)
    total = total.reshape(local_heads, rows)
    summed = summed.reshape(local_heads, rows, HD)

    share = local_heads // lax.axis_size("tok")
    peak, total, summed = jax.tree.map(
        lambda a: a.reshape((-1, share) + a.shape[1:]), (peak, total, summed)
    )

    def pack(part):
        top, tot, acc = part
        blank = jnp.zeros(top.shape[:-1] + (HD - 2 * rows,), jnp.float32)
        extra = jnp.concatenate([top, tot, blank], axis=-1).reshape(-1, HD)
        return jnp.concatenate([acc.reshape(-1, HD), extra])

    def unpack(buffer, like):
        count = like[0].shape[0] * share
        extra = buffer[count * rows :]
        return (
            extra[:, :rows].reshape(like[0].shape),
            extra[:, rows : 2 * rows].reshape(like[0].shape),
            buffer[: count * rows].reshape(like[2].shape),
        )

    state = (peak, total, summed)
    for hop in tok_hops:
        mine = side(*hop)
        pairs = jax.tree.map(lambda a: a.reshape((-1, 2) + a.shape[1:]), state)
        keep = jax.tree.map(lambda a: lax.dynamic_index_in_dim(a, mine, 1, False), pairs)
        send = jax.tree.map(lambda a: lax.dynamic_index_in_dim(a, 1 - mine, 1, False), pairs)
        got = unpack(swap(pack(send), *hop), keep)
        top = jnp.maximum(keep[0], got[0])
        one, two = jnp.exp(keep[0] - top), jnp.exp(got[0] - top)
        state = (
            top,
            keep[1] * one + got[1] * two,
            keep[2] * one[..., None] + got[2] * two[..., None],
        )
    result = state[2][0] / state[1][0][..., None]
    return result.transpose(1, 0, 2).reshape(1, rows, 1, share * HD)


def pair_sides():
    return side("tok", 1), side("tok", 2), lax.axis_index("lay"), lax.axis_index("head")


def lanes(index, size=HD):
    return pl.ds(pl.multiple_of(index * size, size), size)


def gram_share(block_ref, scratch_ref, out_ref):
    _, _, lay, head = pair_sides()
    rows, half = out_ref.shape[0], scratch_ref.shape[0]
    scratch_ref[...] = product(block_ref[:, lanes(head, half)], block_ref[...], ((0,), (0,)))
    out_ref[...] = scratch_ref[lanes(lay, rows), :]


def gram_kernel(block_ref, out_ref, scratch_ref):
    gram_share(block_ref, scratch_ref, out_ref)


def start_kernel(keys_ref, block_ref, gram_ref, keep_ref, send_ref, kept_ref, sent_ref):
    del gram_ref
    mine, _, _, _ = pair_sides()
    for i in range(2):
        at = pl.ds(i * HD, HD)
        kept_ref[:, at] = keys_ref[:, lanes(2 * i + mine)]
        sent_ref[:, at] = keys_ref[:, lanes(2 * i + 1 - mine)]
    send_ref[...] = product(sent_ref[...], block_ref[...], ((0,), (0,)))
    keep_ref[...] = product(kept_ref[...], block_ref[...], ((0,), (0,)))


def mix_kernel(sent, own_ref, other_ref, first_ref, second_ref, out_ref):
    mine, _, _, head = pair_sides()
    coef = first_ref[...] + second_ref[...]
    half = own_ref.shape[0] // 2
    rows = lanes(head ^ int(sent), half)
    for keys_ref, piece in ((own_ref, mine), (other_ref, 1 - mine)):
        out_ref[lanes(piece, half), :] = product(keys_ref[rows, :], coef, ((1,), (0,)))


def streams_kernel(first_ref, second_ref, a_keep, a_send, b_keep, b_send):
    mine, _, lay, _ = pair_sides()
    half = first_ref.shape[0] // 2
    quarter, eighth = half // 2, half // 4

    def rows(piece, at, count):
        here = pl.ds(pl.multiple_of(piece * half + at, count), count)
        return first_ref[here, :] + second_ref[here, :]

    for piece in range(2):
        to = pl.ds(piece * eighth, eighth)
        a_keep[to, :] = rows(piece, lay * eighth, eighth)
        a_send[to, :] = rows(piece, (1 - lay) * eighth, eighth)
    b_keep[...] = rows(mine, quarter, quarter)
    b_send[...] = rows(1 - mine, quarter, quarter)


def summed_streams(keep, send, lower):
    got = swap(send, "head", 1)
    quarter = vmem(keep.shape[0] // 4, keep.shape[1])
    a_keep, a_send, b_keep, b_send = call(streams_kernel, [quarter] * 4, keep, got)
    a = a_keep + swap(a_send, "lay", 1)
    b = b_keep + swap(b_send, "tok", 1)
    a, b = a + swap(a, "tok", 1), b + swap(b, "lay", 1)
    a = after(a, lower)
    here = jnp.concatenate([a, b])
    return here, (swap(a, "lay", 1), swap(b, "tok", 1))


def stack_rows(far, beside, size):
    _, _, lay, head = pair_sides()
    count = size // 2
    first = (head ^ far) * size
    return first + (lay ^ beside) * (count // 2), first + count


def project_stack(far, beside, own_ref, other_ref, block_ref, rows_ref):
    mine, _, _, _ = pair_sides()
    size = block_ref.shape[0]
    half, quarter = size // 2, size // 4
    low, high = stack_rows(far, beside, size)
    low = pl.ds(pl.multiple_of(low, quarter), quarter)
    rows_ref[lanes(mine, quarter), :] = own_ref[low, :]
    rows_ref[lanes(1 - mine, quarter), :] = other_ref[low, :]
    high = pl.ds(pl.multiple_of(high, half), half)
    rows_ref[pl.ds(half, half), :] = (other_ref if beside else own_ref)[high, :]
    return product(rows_ref[...], block_ref[...], ((0,), (0,)))


def stack_kernel(far, beside, stack_ref, lower_ref, own_ref, other_ref, *refs):
    *part_refs, block_ref, gram_ref, proj_ref, rows_ref, scratch_ref = refs
    block_ref[...] = product(stack_ref[...], lower_ref[...], ((1,), (1,)))
    gram_share(block_ref, scratch_ref, gram_ref)
    proj_ref[...] = project_stack(far, beside, own_ref, other_ref, block_ref, rows_ref)
    for part_ref, ref in zip(part_refs, (gram_ref, proj_ref)):
        ref[...] += part_ref[...]


def last_stack_kernel(stack_ref, lower_ref, part_ref, block_ref, gram_ref, scratch_ref):
    block_ref[...] = product(stack_ref[...], lower_ref[...], ((1,), (1,)))
    gram_share(block_ref, scratch_ref, gram_ref)
    gram_ref[...] += part_ref[...]


def project_kernel(own_ref, other_ref, block_ref, part_ref, proj_ref, rows_ref):
    proj_ref[...] = part_ref[...] + project_stack(1, 1, own_ref, other_ref, block_ref, rows_ref)


def attend_kernel(sent, query_ref, *refs):
    *block_refs, first_ref, second_ref, lower_ref, own_ref, other_ref, length_ref = refs[:-2]
    out_ref, score_ref = refs[-2:]
    mine, upper, _, _ = pair_sides()
    which = upper ^ int(sent)
    tokens = own_ref.shape[1]
    half, width = tokens // 2, length_ref.shape[1]
    local = lanes(which)
    coef = product(first_ref[local, :] + second_ref[local, :], lower_ref[...], ((1,), (1,)))
    reduced = product(query_ref[lanes(which, width), :], coef, ((1,), (0,))) / math.sqrt(HD)
    reduced = product(reduced, lower_ref[...], ((1,), (0,)))
    for i, block_ref in enumerate(block_refs):
        far, beside = i % 2, i // 2
        part = product(block_ref[...], reduced, ((1,), (1,)))
        low, high = stack_rows(far, beside, half)
        quarter = half // 4
        for piece in range(2):
            to = pl.multiple_of((piece ^ mine) * tokens + low, quarter)
            score_ref[pl.ds(to, quarter), :] = part[piece * quarter : (piece + 1) * quarter]
        to = pl.multiple_of(beside * tokens + high, half // 2)
        score_ref[pl.ds(to, half // 2), :] = part[half // 2 :]
    scores = score_ref[...]
    at = lax.broadcasted_iota(jnp.int32, (tokens, width), 0)
    tok = lax.axis_index("tok")
    valid = jnp.concatenate(
        [(tok ^ piece) * tokens + at < length_ref[...] for piece in range(2)]
    )
    peak = jnp.max(jnp.where(valid, scores, NEG), axis=0, keepdims=True)
    weight = jnp.where(valid, jnp.exp(scores - peak), 0.0)
    total = jnp.sum(weight, axis=0, keepdims=True)
    acc = product(own_ref[local, :], weight[:tokens], ((1,), (0,)))
    out_ref[pl.ds(0, HD), :] = acc + product(other_ref[...], weight[tokens:], ((1,), (0,)))
    out_ref[pl.ds(HD, 8), :] = jnp.broadcast_to(peak, (8, width))
    out_ref[pl.ds(HD + 8, 8), :] = jnp.broadcast_to(total, (8, width))


def merge_kernel(first_ref, second_ref, out_ref):
    top = jnp.maximum(first_ref[pl.ds(HD, 1), :], second_ref[pl.ds(HD, 1), :])
    one = jnp.exp(first_ref[pl.ds(HD, 1), :] - top)
    two = jnp.exp(second_ref[pl.ds(HD, 1), :] - top)
    total = first_ref[pl.ds(HD + 8, 1), :] * one + second_ref[pl.ds(HD + 8, 1), :] * two
    acc = first_ref[pl.ds(0, HD), :] * one + second_ref[pl.ds(0, HD), :] * two
    out_ref[...] = (acc / total).T


def gathered(share):
    beside = swap(share, "lay", 1)
    return share, beside, swap(share, "head", 1), swap(beside, "head", 1)


def after(x, *others):
    return lax.optimization_barrier((x, *others))[0]


def split_kernel(values_ref, query_ref, kept_ref, first_ref, second_ref, order_ref):
    mine, upper, _, _ = pair_sides()
    rows, group = query_ref.shape[0], QH // KVH
    for i, ref in enumerate((first_ref, second_ref)):
        which = upper ^ 1 ^ i
        for k in range(group):
            order_ref[pl.ds(i * rows * group + k, rows, stride=group), :] = query_ref[
                :, lanes((2 * i + mine) * group + k)
            ]
        kept_ref[pl.ds(i * HD, HD), :] = values_ref[:, lanes(2 * i + mine)].T
        ref[...] = values_ref[:, lanes(2 * which + 1 - mine)].T


def paired_body(keys, values, queries, start_block, lengths):
    _, tokens, width = keys.shape
    keys, values, queries = keys[0], values[0], queries[0]
    rank = start_block.shape[1]
    rows = queries.shape[0]
    half, share = width // 2, rank // 4

    gram = call(
        gram_kernel,
        vmem(share, rank),
        start_block,
        scratch=[(rank // 2, rank)],
        flops=400_000_000,
    )
    keep, send, keys_own, keys_send = call(
        start_kernel,
        [vmem(half, rank)] * 2 + [vmem(tokens, half)] * 2,
        keys,
        start_block,
        gram,
        flops=900_000_000,
    )
    gram = gram + swap(gram, "tok", 1)
    proj = keep + swap(after(send, gram), "tok", 1)
    group = QH // KVH
    values_own, *values_send, ordered = call(
        split_kernel,
        [vmem(half, tokens)] + [vmem(HD, tokens)] * 2 + [vmem(2 * rows * group, HD)],
        after(values, proj),
        queries,
    )
    values_other = []
    lower = None
    for step in range(ITERS + 1):
        gram = gram + swap(gram, "tok", 2)
        last = step == ITERS
        if last:
            proj, gram = lax.optimization_barrier((proj, gram))
        elif step == 0:
            proj = after(proj, gram)
            if step == 0:
                keys_other = swap(after(keys_send, proj), "tok", 1)
        first, second = proj, swap(proj, "tok", 2)
        parts = gathered(gram)
        if step > 0:
            ready = parts[1] if last else gram
            values_other.append(swap(after(values_send[step - 1], proj, ready), "tok", 1))
        if step == 0 or last:
            flops = 1_500_000_000 if last else FACTOR_FLOPS
            lower = inverse_factor(after(parts[0], values_own), *parts[1:], flops=flops)
            first = after(first, lower)
        else:
            halves = inverse_factor_low(*parts)
            first = after(first, halves[0], *values_other)
            lower = inverse_factor_high(*halves)
        if last:
            break
        mix = (keys_own, keys_other, first, second)
        z_send, z_keep = (
            call(functools.partial(mix_kernel, sent), vmem(tokens, rank), *mix, flops=400_000_000)
            for sent in (True, False)
        )
        here, there = summed_streams(z_keep, z_send, lower)
        block, parts = vmem(tokens // 2, rank), ()
        blocks = []
        stacks = [here, swap(here, "head", 1)]
        for i in range(3):
            if i == 2:
                there = jnp.concatenate([after(x, *parts) for x in there])
                stacks += [there, swap(there, "head", 1)]
            done, *parts = call(
                functools.partial(stack_kernel, i % 2, i // 2),
                [block, vmem(share, rank), vmem(half, rank)],
                stacks[i],
                lower,
                keys_own,
                keys_other,
                *parts,
                scratch=[(tokens // 2, half), (rank // 2, rank)],
                flops=900_000_000,
            )
            blocks.append(done)
        done, gram = call(
            last_stack_kernel,
            [block, vmem(share, rank)],
            stacks[3],
            lower,
            parts[0],
            scratch=[(rank // 2, rank)],
            flops=600_000_000,
        )
        blocks.append(done)
        proj = call(
            project_kernel,
            vmem(half, rank),
            keys_own,
            keys_other,
            done,
            parts[1],
            scratch=[(tokens // 2, half)],
            flops=400_000_000,
        )
    operands = (
        ordered,
        *blocks,
        first,
        second,
        lower,
        values_own,
    )
    row_lengths = jnp.repeat(lengths, group)[None, :]
    send, keep = (
        call(
            functools.partial(attend_kernel, sent),
            vmem(HD + 16, HD),
            *operands,
            other,
            row_lengths,
            scratch=[(2 * tokens, group * rows)],
            flops=1_500_000_000,
        )
        for sent, other in zip((True, False), values_other)
    )
    result = call(merge_kernel, vmem(group * rows, HD), keep, swap(send, "tok", 2))
    return result.reshape(1, rows, 1, group * HD)


def solution(mesh):
    paired = (mesh.shape["tok"], mesh.shape["lay"], mesh.shape["head"]) == (4, 2, 2)
    body = paired_body if paired else spread_body
    return jax.shard_map(
        body,
        mesh=mesh,
        in_specs=(
            P("lay", ("groups", "tok"), "head"),
            P("lay", ("groups", "tok"), "head"),
            P("lay", "groups", "head"),
            P(("groups", "tok"), None),
            P("groups"),
        ),
        out_specs=P("lay", "groups", "head", "tok"),
        check_vma=False,
    )
```
